512 devices in a mesh: band: 16 (over x, y), lon: 32 (over z, core).
Axes of the slice: x: 4, y: 4, z: 16, core: 2. Of those that a mesh axis runs over, the one named last changes fastest.
Arguments:
- back_height: float32 [1024, 8640], P('band', 'lon'), may hold values from -6 to 6
- back_east: float32 [1024, 8640], P('band', 'lon'), may hold values from -6 to 6
- back_north: float32 [1024, 8640], P('band', 'lon'), may hold values from -6 to 6
- obs_values: float32 [65536, 256], P(('band', 'lon')), may hold values from -6 to 6
- obs_owner: int32 [65536, 1], P(('band', 'lon')), may hold values from 0 to 31; in each aligned block of 128 rows (0 to 127, 128 to 255, ...) at most 12 rows name the same one
- obs_row: int32 [65536], P(('band', 'lon')), may hold values from 0 to 63
- obs_count: int32 [65536], P(('band', 'lon')), may hold values from 1 to 256
- polar_mask: int32 [1024], P('band'), may hold values from 0 to 1, as said below
- keep_share: float32 [1024], P('band'), may hold values from 0.05 to 0.9
- depth_level: int32 [1024, 8640], P('band', 'lon'), may hold values from 0 to 50
Outputs:
- grad_height: float32 [1024, 8640], P('band', 'lon')
- grad_east: float32 [1024, 8640], P('band', 'lon')
- grad_north: float32 [1024, 8640], P('band', 'lon')
The draws below stay inside these ranges and needn't reach their ends.
Inputs may be any that keep to these rules, and one draw needn't show every extreme that they name: `obs_owner`: among the rows of one device at most 12 name the same tile, a bound that some block reaches. `polar_mask`: among the 64 rows of one band at most 32 are 1, and some band has exactly 32.
All inputs are finite; a program needn't handle non-finite values.
Results may differ from the reference program's by a relative error of at most 0.00005.
Values sent between devices are 32-bit elements; how exact they have to be, the bound alone decides.
No kernel may reach another device: no remote copies, remote signals or barrier semaphores. Data moves between devices by JAX's collectives and lax.ppermute only.
A program may use at most 64 MiB of HBM per device.

```python
import math
import jax
import jax.numpy as jnp
import numpy as np

LON = 8640
MODES = 128
OBS_W = 256
LEVELS = 50
LAT_DEV = 64
OBS_DEV = 128
POLAR = 32
LAT = 1024
LON_DEV = 270
CAP = 12
OBS = 65536
N_BAND = 16
N_LON = 32


def draw_polar_mask(key, part):
    base_key = jax.random.fold_in(key, 17)
    count_key, pick_key, order_key = jax.random.split(base_key, 3)
    band_total = LAT // LAT_DEV
    band_counts = jax.random.randint(count_key, (band_total,), POLAR // 2, POLAR + 1)
    full_band = jax.random.randint(pick_key, (), 0, band_total)
    band_ids = jnp.arange(band_total, dtype=jnp.int32)
    band_counts = jnp.where(band_ids == full_band, POLAR, band_counts)
    order_keys = jax.random.split(order_key, band_total)
    ranks = jax.vmap(lambda one_key: jax.random.permutation(one_key, LAT_DEV))(order_keys)
    chosen = (ranks < band_counts[:, None]).astype(jnp.int32)
    return chosen.reshape(LAT)


def with_ends(drawn, rng, least, largest):
    longest = drawn.shape.index(max(drawn.shape))
    spots = []
    for shift in (0, 1):
        where = [jax.random.randint(jax.random.fold_in(rng, axis), (), 0, length) for axis, length in enumerate(drawn.shape)]
        where[longest] = (where[longest] + shift) % drawn.shape[longest]
        spots.append(tuple(where))
    return drawn.at[spots[0]].set(least).at[spots[1]].set(largest)


def shard_levels(own_key, dims, cuts, low, largest):
    loudness, own = 1.0, jax.random.fold_in(own_key, 6)
    for axis_at, blocks in cuts:
        heights = jnp.exp(jax.random.uniform(jax.random.fold_in(own, axis_at), (blocks,), jnp.float32, low / len(cuts), largest / len(cuts)))
        loudness = loudness * jnp.repeat(heights, dims[axis_at] // blocks).reshape([-1 if axis == axis_at else 1 for axis in range(len(dims))])
    return loudness


def deal_out(own_key, own, number, rows, number_of, top, reach, lean):
    sequence = jax.random.permutation(own_key, number_of)
    heavy_load, common = shares(number_of, rows * top, reach, lean, True), shares(number_of, rows * top, reach, lean, False)
    places = jnp.arange(number_of)

    def named(tallies, turn):
        used = int((tallies > 0).sum())
        fixed = max(1, used // 4)
        passed = fixed + (places - fixed + turn * (used - fixed)) % max(1, number_of - fixed)
        return jnp.zeros((number_of,), jnp.int32).at[sequence[jnp.where(places < fixed, places, passed)]].set(jnp.asarray(tallies, jnp.int32))

    tallies = jnp.where(number % 4 == 0, named(heavy_load, number // 4), named(common, number - number // 4 - 1))
    mixed = jax.random.permutation(jax.random.fold_in(own, 3), number_of)
    source_of, receiver = mixed[0:number_of // 2 * 2:2], mixed[1:number_of // 2 * 2:2]
    room = jnp.minimum(tallies[source_of] - 1, reach - tallies[receiver]) // 2
    room = jnp.where((source_of == sequence[0]) | (receiver == sequence[0]) | (tallies[receiver] == 0), 0, jnp.maximum(room, 0))
    passed = jax.random.randint(jax.random.fold_in(own, 4), (number_of // 2,), 0, 1 << 20) % (room + 1)
    tallies = tallies.at[source_of].add(-passed).at[receiver].add(passed)
    items = jnp.searchsorted(jnp.cumsum(tallies), jnp.arange(rows * top), side="right").astype(jnp.int32)
    table = items.reshape(top, rows).T
    table = table[jax.random.permutation(jax.random.fold_in(own, 1), rows)]
    turn = jax.random.randint(jax.random.fold_in(own, 2), (rows, 1), 0, top)
    return jnp.take_along_axis(table, (jnp.arange(top)[None, :] + turn) % top, axis=1)


def shares(amount, total, limit, lean, full):
    loads = [(1 << 20) // math.isqrt(rank ** lean) + 1 for rank in range(1, amount + 1)]
    largest = limit if full else min(limit, max(-(-total // amount), total * loads[0] // sum(loads)))
    least = 1 if total - largest >= amount - 1 else 0
    holding, spare = [largest] + [least] * (amount - 1), total - largest - least * (amount - 1)
    while spare > 0:
        candidates = [i for i in range(1, amount) if holding[i] < largest] or [i for i in range(1, amount) if holding[i] < limit]
        whole, budget = sum([loads[i] for i in candidates]), spare
        for i in candidates:
            more = min(limit - holding[i], max(1, budget * loads[i] // whole), spare)
            holding[i] = holding[i] + more
            spare = spare - more
    return np.array(holding)


def gaussian(stream_key, shape, deviation, reach, cuts=(), kind=jnp.bfloat16):
    entries = jax.random.normal(stream_key, shape, jnp.float32) * deviation
    if len(cuts) > 0:
        entries = shard_levels(stream_key, shape, cuts, -0.22, 0.18) * entries
    return jnp.clip(entries, min=-reach, max=reach).astype(kind)


def setup_inputs(seed: int = 0) -> dict:
    seeds = jax.random.split(jax.random.key(seed), 11)
    back_height = gaussian(seeds[0], (LAT, LON), 1.0, 6.0, ((0, 16), (1, 32)), jnp.float32)
    back_east = gaussian(seeds[1], (LAT, LON), 1.0, 6.0, ((0, 16), (1, 32)), jnp.float32)
    back_north = gaussian(seeds[2], (LAT, LON), 1.0, 6.0, ((0, 16), (1, 32)), jnp.float32)
    obs_values = gaussian(seeds[3], (OBS, OBS_W), 1.0, 6.0, ((0, 512),), jnp.float32)
    obs_owner_keys = jax.random.split(jax.random.fold_in(seeds[4], 1), OBS // OBS_DEV)
    obs_owner_turns = jax.random.permutation(jax.random.fold_in(seeds[4], 3), OBS // OBS_DEV)
    obs_owner = jax.vmap(lambda own, number: deal_out(jax.random.fold_in(seeds[4], 2), own, number, OBS_DEV, N_LON, 1, CAP, 2))(obs_owner_keys, obs_owner_turns).reshape((OBS, 1))
    obs_row = with_ends(jax.random.randint(seeds[5], (OBS,), 0, LAT_DEV), jax.random.fold_in(seeds[5], 1), 0, LAT_DEV - 1).astype(jnp.int32)
    obs_count = with_ends(jax.random.randint(seeds[6], (OBS,), 1, OBS_W + 1), jax.random.fold_in(seeds[6], 1), 1, OBS_W).astype(jnp.int32)
    polar_mask = draw_polar_mask(jax.random.fold_in(seeds[10], 71), 0)
    keep_share = jnp.clip(jnp.exp(math.log(0.9) - 2.8903717 * jax.random.uniform(seeds[8], (LAT,), jnp.float32) ** shard_levels(seeds[8], (LAT,), ((0, 16),), -0.2, 0.2)), 0.05, 0.9)
    depth_level = with_ends(jax.random.randint(seeds[9], (LAT, LON), 0, LEVELS + 1), jax.random.fold_in(seeds[9], 1), 0, LEVELS).astype(jnp.int32)
    return dict(back_height=back_height, back_east=back_east, back_north=back_north, obs_values=obs_values, obs_owner=obs_owner, obs_row=obs_row, obs_count=obs_count, polar_mask=polar_mask, keep_share=keep_share, depth_level=depth_level)


COURANT = 0.25
ROTATION = 0.4
LIMIT = 1.3089969389957472


def latitude_terms(total_rows):
    centre = (jnp.arange(total_rows, dtype=jnp.int32).astype(jnp.float32) + 0.5) / total_rows
    angle = (2.0 * centre - 1.0) * LIMIT
    return 1.0 / jnp.cos(angle), ROTATION * jnp.sin(angle)


def along_lon(field, metric):
    return metric[:, None] * (jnp.roll(field, -1, axis=1) - jnp.roll(field, 1, axis=1)) * 0.5


def along_lat(field):
    padded = jnp.pad(field, ((1, 1), (0, 0)))
    return (padded[2:] - padded[:-2]) * 0.5


def project(field):
    spectrum = jnp.fft.rfft(field, axis=1)
    kept = jnp.arange(spectrum.shape[1], dtype=jnp.int32) < MODES
    return jnp.fft.irfft(jnp.where(kept[None, :], spectrum, 0.0), n=field.shape[1], axis=1)


def smooth(field, weight):
    return field + weight[:, None] * (project(field) - field)


def adjoint_step(height, east, north, weight, wet_cells, depth_share, metric, rotation):
    height_kept = smooth(height, weight)
    east_kept = smooth(wet_cells * east, weight)
    north_kept = smooth(wet_cells * north, weight)
    middle = height_kept + COURANT * (along_lon(east_kept, metric) + along_lat(north_kept))
    new_east = east_kept - rotation[:, None] * north_kept + COURANT * depth_share * along_lon(middle, metric)
    new_north = north_kept + rotation[:, None] * east_kept + COURANT * depth_share * along_lat(middle)
    return middle, new_east, new_north


def deposit(obs_values, obs_owner, obs_row, obs_count, total_rows, total_cols):
    count_all = obs_values.shape[0]
    band_of = jnp.arange(count_all, dtype=jnp.int32) // (count_all // N_BAND)
    lat_index = band_of * LAT_DEV + obs_row
    offsets = jnp.arange(OBS_W, dtype=jnp.int32)
    lon_index = obs_owner[:, 0][:, None] * LON_DEV + offsets[None, :]
    alive_cells = offsets[None, :] < obs_count[:, None]
    values = jnp.where(alive_cells, obs_values, 0.0)
    grid = jnp.zeros((total_rows, total_cols), obs_values.dtype)
    return grid.at[lat_index[:, None], lon_index].add(values)


def reference(back_height, back_east, back_north, obs_values, obs_owner, obs_row, obs_count, polar_mask, keep_share, depth_level):
    total_rows, total_cols = back_height.shape
    metric, rotation = latitude_terms(total_rows)
    wet_cells = (depth_level > 0).astype(back_height.dtype)
    depth_share = depth_level.astype(back_height.dtype) / LEVELS
    weight = polar_mask.astype(back_height.dtype) * (1.0 - keep_share)
    middle, east, north = adjoint_step(back_height, back_east, back_north, weight, wet_cells, depth_share, metric, rotation)
    middle = middle + deposit(obs_values, obs_owner, obs_row, obs_count, total_rows, total_cols)
    return adjoint_step(middle, east, north, weight, wet_cells, depth_share, metric, rotation)
```

```python
import math

import jax
import jax.numpy as jnp
import numpy as np
from jax import lax
from jax.experimental import pallas as pl
from jax.experimental.pallas import tpu as pltpu
from jax.sharding import PartitionSpec as P

MODES = 128
LEVELS = 50
COURANT = 0.25
ROTATION = 0.4
LIMIT = 1.3089969389957472
CAP = 12
LANES = 384
GRID = 512
HALO = 4
F32 = jnp.float32


def hdot(left, right):
    return jnp.dot(left, right, precision=lax.Precision.HIGHEST, preferred_element_type=F32)


def iota(shape, dim):
    return lax.broadcasted_iota(jnp.int32, shape, dim)


def to_col(row):
    size = row.shape[1]
    same = iota((size, size), 0) == iota((size, size), 1)
    return jnp.sum(jnp.where(same, row, jnp.zeros_like(row)), axis=1, keepdims=True)


def to_row(col):
    size = col.shape[0]
    same = iota((size, size), 0) == iota((size, size), 1)
    return jnp.sum(jnp.where(same, col, jnp.zeros_like(col)), axis=0, keepdims=True)


def lon_diff(field):
    width = field.shape[1]
    return 0.5 * (pltpu.roll(field, width - 1, 1) - pltpu.roll(field, 1, 1))


def lat_diff(field):
    rows = field.shape[0]
    return 0.5 * (pltpu.roll(field, rows - 1, 0) - pltpu.roll(field, 1, 0))


def rank_in_row(mask_row):
    size = mask_row.shape[1]
    before = iota((size, size), 0) < iota((size, size), 1)
    return jnp.sum(jnp.where(before, to_col(mask_row), 0), axis=0, keepdims=True)


def slot_rows(mask_row, core, devices):
    rows = mask_row.shape[1]
    half = devices // 2
    line = iota((devices, rows), 0)
    near = (line < half).astype(jnp.int32)
    place = jnp.where(line < half, line, line - half)
    slot = 2 * place + near * core + (1 - near) * (1 - core)
    hit = (slot == rank_in_row(mask_row)) & (mask_row == 1)
    return hit.astype(F32)


def pack_lon(h_ref, e_ref, n_ref, d_ref, fields_ref, west_ref, east_ref):
    cols = h_ref.shape[1]
    level = d_ref[...].astype(F32)
    wet = (level > 0).astype(F32)
    values = (h_ref[...], wet * e_ref[...], wet * n_ref[...], level)
    lane = iota((h_ref.shape[0], 128), 1)
    west = jnp.zeros(lane.shape, F32)
    east = jnp.zeros(lane.shape, F32)
    last = cols - HALO - 256
    fields_ref[...] = jnp.zeros(fields_ref.shape, F32)
    for f, value in enumerate(values):
        fields_ref[f, :, 0:cols] = value
        inside = (lane >= HALO * f) & (lane < HALO * f + HALO)
        head = fields_ref[f, :, 0:128]
        tail = fields_ref[f, :, 256:384]
        if f:
            head = pltpu.roll(head, HALO * f, 1)
        west = jnp.where(inside, head, west)
        east = jnp.where(inside, pltpu.roll(tail, (HALO * f - last) % 128, 1), east)
    west_ref[...] = west
    east_ref[...] = east


def third_tile(tail, left, right, f, cols):
    lane = iota(tail.shape, 1)
    first = cols - 256
    shifted = pltpu.roll(right, (first - HALO * f) % 128, 1)
    tail = jnp.where((lane >= first) & (lane < first + HALO), shifted, tail)
    shifted = pltpu.roll(left, (128 - HALO - HALO * f) % 128, 1)
    return jnp.where(lane >= 128 - HALO, shifted, tail)


WEIGHT_LANE = 300 - 256


def pack_lat(cols, fields_ref, left_ref, right_ref, mask_ref, keep_ref, north_ref, south_ref):
    rows = fields_ref.shape[1]
    weight = to_col(mask_ref[...].astype(F32) * (1.0 - keep_ref[...]))
    for f in range(4):
        for out_ref, at in ((north_ref, 0), (south_ref, rows - HALO)):
            span = slice(at, at + HALO)
            tail = third_tile(
                fields_ref[f, span, 256:384], left_ref[span, :], right_ref[span, :], f, cols
            )
            if f == 3:
                tail = jnp.where(iota(tail.shape, 1) == WEIGHT_LANE, weight[span, :], tail)
            out_ref[HALO * f : HALO * f + HALO, 0:256] = fields_ref[f, span, 0:256]
            out_ref[HALO * f : HALO * f + HALO, 256:384] = tail


def row_terms(terms, band):
    lane = iota(terms.shape, 1)
    return [
        jnp.sum(jnp.where(lane == band + 16 * i, terms, 0.0), axis=1, keepdims=True)
        for i in range(3)
    ]


def partial_sums(
    cols,
    place_ref,
    fields_ref,
    left_ref,
    right_ref,
    above_ref,
    below_ref,
    mask_ref,
    keep_ref,
    terms_ref,
    cos_ref,
    sin_ref,
    table_ref,
    kernel_ref,
    placed_ref,
    ext_ref,
    weight_ref,
    mine_ref,
    other_ref,
    stack_ref,
    cells_ref,
):
    rows = fields_ref.shape[1]
    ext = rows + 2 * HALO
    devices = cos_ref.shape[0]
    half = devices // 2
    band, lon = place_ref[0], place_ref[1]
    core = lon % 2
    for f in range(4):
        ext_ref[f, 0:rows, 0:256] = fields_ref[f, :, 0:256]
        ext_ref[f, 0:rows, 256:384] = third_tile(
            fields_ref[f, :, 256:384], left_ref[...], right_ref[...], f, cols
        )
        ext_ref[f, rows : rows + HALO, :] = below_ref[HALO * f : HALO * f + HALO, :]
        ext_ref[f, rows + HALO : ext, :] = above_ref[HALO * f : HALO * f + HALO, :]
    edge = ext_ref[3, rows:ext, 256:384]
    marked = iota(edge.shape, 1) == WEIGHT_LANE
    mask = mask_ref[...]
    weight_ref[0:rows, :] = jnp.broadcast_to(
        to_col(mask.astype(F32) * (1.0 - keep_ref[...])), (rows, 128)
    )
    weight_ref[rows:ext, :] = jnp.broadcast_to(
        jnp.sum(jnp.where(marked, edge, 0.0), axis=1, keepdims=True), (2 * HALO, 128)
    )
    ext_ref[3, rows:ext, 256:384] = jnp.where(marked, 0.0, edge)
    weight = weight_ref[:, 0:1]
    rest = 1.0 - weight
    metric, rotation, valid = row_terms(terms_ref[...], band)
    metric = metric * valid
    height, east, north = ext_ref[0], ext_ref[1], ext_ref[2]
    share = ext_ref[3] / LEVELS
    low_height = weight * height + COURANT * (
        metric * lon_diff(weight * east) + lat_diff(weight * north)
    )
    low_height = valid * low_height
    east_rest, north_rest = rest * east, rest * north
    middle = valid * (
        rest * height + COURANT * (metric * lon_diff(east_rest) + lat_diff(north_rest))
    )
    new_east = east_rest - rotation * north_rest + COURANT * share * metric * lon_diff(middle)
    new_north = north_rest + rotation * east_rest + COURANT * share * lat_diff(middle)
    chosen = slot_rows(mask, core, devices)
    sources = (height, east, north, low_height, lat_diff(low_height), middle, new_east, new_north)
    for v, field in enumerate(sources):
        stack_ref[devices * v : devices * v + devices, :] = hdot(chosen, field[0:rows, :])
    level = ext_ref[3, 0:rows, :]
    cells_ref[0:devices, :] = hdot(chosen, (level > 0).astype(F32))
    cells_ref[devices : 2 * devices, :] = hdot(chosen, share[0:rows, :])
    sums = hdot(stack_ref[...], table_ref[...])
    turn_cos, turn_sin = cos_ref[pl.ds(lon, 1), :], sin_ref[pl.ds(lon, 1), :]
    for v in range(len(sources)):
        lines = slice(devices * v, devices * v + devices)
        on_cos, on_sin = sums[lines, 0:128], sums[lines, 128:256]
        all_cos = on_cos * turn_cos - on_sin * turn_sin
        all_sin = on_sin * turn_cos + on_cos * turn_sin
        if v == 5:
            all_cos = all_cos + placed_ref[:, 0:128]
            all_sin = all_sin + placed_ref[:, 128:256]
        for i, value in enumerate((all_cos, all_sin)):
            mine_ref[:, 2 * v + i, :] = value[0:half]
            other_ref[:, 2 * v + i, :] = value[half:devices]
    spread = pltpu.roll(hdot(cells_ref[...], kernel_ref[...]), lon * (GRID // devices), 1)
    for c in range(2):
        for i in range(4):
            part = spread[devices * c : devices * c + devices, 128 * i : 128 * i + 128]
            at = 16 + 4 * c + i
            mine_ref[:, at, :] = part[0:half]
            other_ref[:, at, :] = part[half:devices]


def pack_observations(
    place_ref,
    values_ref,
    owner_ref,
    row_ref,
    count_ref,
    mask_ref,
    cos_ref,
    sin_ref,
    table_ref,
    out_ref,
    placed_ref,
):
    number, width = values_ref.shape
    devices = cos_ref.shape[0]
    core = place_ref[1] % 2
    values = jnp.where(
        iota((number, width), 1) < to_col(count_ref[...]), values_ref[...], 0.0
    )
    owner_col = owner_ref[...]
    owner_row = to_row(owner_col)
    same = owner_col == owner_row
    before = same & (iota((number, number), 0) < iota((number, number), 1))
    arrival_row = jnp.sum(before.astype(jnp.int32), axis=0, keepdims=True)
    after = same & (iota((number, number), 0) > iota((number, number), 1))
    arrival_col = jnp.sum(after.astype(jnp.int32), axis=1, keepdims=True)
    target = owner_row * 16 + arrival_row
    sent = (iota((16 * devices, number), 0) == target).astype(F32)
    out_ref[...] = hdot(sent, values).reshape(devices, 16, width)
    named = (iota((devices, number), 0) == owner_row).astype(F32) * row_ref[...].astype(F32)
    lines = hdot(named, (iota((number, width), 1) == arrival_col).astype(F32))
    out_ref[:, CAP, :] = lines
    sums = hdot(values, table_ref[0:width, :])
    whose = (iota((number, devices), 1) == owner_col).astype(F32)
    turn_cos, turn_sin = hdot(whose, cos_ref[...]), hdot(whose, sin_ref[...])
    on_cos, on_sin = sums[:, 0:128], sums[:, 128:256]
    all_cos = on_cos * turn_cos - on_sin * turn_sin
    all_sin = on_sin * turn_cos + on_cos * turn_sin
    mask = mask_ref[...]
    rows = mask.shape[1]
    in_row = (iota((rows, number), 0) == row_ref[...]).astype(F32)
    chosen = hdot(slot_rows(mask, core, devices), in_row)
    placed_ref[:, 0:128] = hdot(chosen, all_cos)
    placed_ref[:, 128:256] = hdot(chosen, all_sin)


def unpack_observations(in_ref, dep_ref, edge_ref):
    devices, lines, width = in_ref.shape
    rows = dep_ref.shape[0]
    total = devices * lines
    labels = in_ref[:, CAP, 0:128]
    across = hdot(labels, (iota((128, total), 1) % lines == iota((128, total), 0)).astype(F32))
    own = iota((devices, total), 1) // lines == iota((devices, total), 0)
    label_row = jnp.sum(jnp.where(own, across, 0.0), axis=0, keepdims=True)
    line = iota((rows, total), 1) % lines
    hit = (iota((rows, total), 0).astype(F32) == label_row) & (line < CAP)
    summed = hdot(hit.astype(F32), in_ref[...].reshape(total, width))
    dep_ref[:, 0:256] = summed
    dep_ref[:, 256:384] = jnp.zeros((rows, 128), F32)
    edge_ref[...] = pltpu.roll(summed[:, 0:128], 14, 1)


def own_row(
    place_ref,
    in_ref,
    mask_ref,
    keep_ref,
    lines_ref,
    slope_ref,
    to_grid_ref,
    from_grid_ref,
    out_ref,
    left_ref,
    grid_ref,
    res_ref,
):
    band, lon = place_ref[0], place_ref[1]
    sums = in_ref[0]
    for i in range(1, in_ref.shape[0]):
        sums = sums + in_ref[i]
    mask = mask_ref[...]
    chosen = ((rank_in_row(mask) == lon) & (mask == 1)).astype(F32)

    def pick(row):
        return jnp.sum(chosen * row, axis=1, keepdims=True)

    rows = mask.shape[1]
    weight = pick(1.0 - keep_ref[...])
    both = lines_ref[pl.ds(band, 1), :]
    metric = pick(both[:, 0:rows])
    rotation = pick(both[:, 128 : 128 + rows])

    def line(i):
        return sums[i : i + 1, :]

    slope = slope_ref[0:1, :]
    left_ref[...] = jnp.zeros(left_ref.shape, F32)
    pairs = (
        (weight * (line(2) - rotation * line(4)), weight * (line(3) - rotation * line(5))),
        (metric * slope * line(7), -metric * slope * line(6)),
        (weight * (line(4) + rotation * line(2)), weight * (line(5) + rotation * line(3))),
        (line(8), line(9)),
    )
    for i, (on_cos, on_sin) in enumerate(pairs):
        left_ref[i : i + 1, 0:128] = on_cos
        left_ref[i : i + 1, 128:256] = on_sin
    at = hdot(left_ref[...], to_grid_ref[...])
    wet = jnp.concatenate([line(16), line(17), line(18), line(19)], axis=1)
    share = COURANT * jnp.concatenate([line(20), line(21), line(22), line(23)], axis=1)
    grid_ref[...] = jnp.zeros(grid_ref.shape, F32)
    grid_ref[0:1, :] = wet * at[0:1] + share * at[1:2]
    grid_ref[1:2, :] = wet * at[2:3] + share * at[3:4]
    back = hdot(grid_ref[...], from_grid_ref[...])
    res_ref[...] = jnp.zeros(res_ref.shape, F32)
    res_ref[0:6, :] = sums[0:6]
    res_ref[6:8, :] = sums[10:12] + sums[6:8]
    for i in range(2):
        res_ref[8 + 2 * i : 9 + 2 * i, :] = line(12 + 2 * i) + back[i : i + 1, 0:128]
        res_ref[9 + 2 * i : 10 + 2 * i, :] = line(13 + 2 * i) + back[i : i + 1, 128:256]
    out_ref[...] = jnp.broadcast_to(res_ref[...][None], out_ref.shape)


def band_edges(cols, all_ref, dep_ref, edge_ref, mask_ref, coef_ref, depx_ref, north_ref, south_ref):
    devices = all_ref.shape[0]
    rows = dep_ref.shape[0]
    mask = mask_ref[...]
    rank = to_col(rank_in_row(mask))
    chosen = ((iota((rows, devices), 1) == rank) & (to_col(mask) == 1)).astype(F32)
    first = cols - 256
    lane = iota((rows, 128), 1)
    depx_ref[:, 0:256] = dep_ref[:, 0:256]
    depx_ref[:, 256:384] = jnp.where((lane == first) | (lane == first + 1), edge_ref[...], 0.0)
    for v in range(12):
        own = hdot(chosen, all_ref[:, v, :])
        coef_ref[v] = own
        north_ref[4 * v : 4 * v + 4, :] = own[0:4]
        south_ref[4 * v : 4 * v + 4, :] = own[rows - 4 : rows]
    for out_ref, at in ((north_ref, 0), (south_ref, rows - 2)):
        for r in range(2):
            for t in range(3):
                out_ref[48 + 3 * r + t : 49 + 3 * r + t, :] = depx_ref[
                    at + r : at + r + 1, 128 * t : 128 * t + 128
                ]
        out_ref[54:56, :] = jnp.zeros((2, 128), F32)


def last_stage(
    place_ref,
    ext_ref,
    weight_ref,
    coef_ref,
    depx_ref,
    above_ref,
    below_ref,
    terms_ref,
    cos_ref,
    sin_ref,
    table_ref,
    h_ref,
    e_ref,
    n_ref,
    stack_ref,
    dep_ref,
):
    ext = ext_ref.shape[1]
    rows, cols = h_ref.shape
    band, lon = place_ref[0], place_ref[1]
    turn_cos, turn_sin = cos_ref[pl.ds(lon, 1), :], sin_ref[pl.ds(lon, 1), :]
    for f in range(6):
        for lines, on_cos, on_sin in (
            (slice(ext * f, ext * f + rows), coef_ref[2 * f], coef_ref[2 * f + 1]),
            (
                slice(ext * f + rows, ext * f + rows + 4),
                below_ref[8 * f : 8 * f + 4, :],
                below_ref[8 * f + 4 : 8 * f + 8, :],
            ),
            (
                slice(ext * f + rows + 4, ext * f + ext),
                above_ref[8 * f : 8 * f + 4, :],
                above_ref[8 * f + 4 : 8 * f + 8, :],
            ),
        ):
            stack_ref[lines, 0:128] = on_cos * turn_cos + on_sin * turn_sin
            stack_ref[lines, 128:256] = on_sin * turn_cos - on_cos * turn_sin
    low = hdot(stack_ref[...], table_ref[...])
    dep_ref[0:rows, :] = depx_ref[...]
    dep_ref[rows:ext, :] = jnp.zeros((ext - rows, LANES), F32)
    for in_ref, at in ((below_ref, rows), (above_ref, ext - 2)):
        for r in range(2):
            for t in range(3):
                dep_ref[at + r : at + r + 1, 128 * t : 128 * t + 128] = in_ref[
                    48 + 3 * r + t : 49 + 3 * r + t, :
                ]
    weight = weight_ref[:, 0:1]
    metric, rotation, valid = row_terms(terms_ref[...], band)
    level = ext_ref[3]
    wet = (level > 0).astype(F32)
    share = COURANT * (level / LEVELS)

    def step(height, east, north, f):
        height = height + weight * (low[ext * f : ext * f + ext] - height)
        east = east + weight * (low[ext * f + ext : ext * f + 2 * ext] - east)
        north = north + weight * (low[ext * f + 2 * ext : ext * f + 3 * ext] - north)
        middle = valid * (height + COURANT * (metric * lon_diff(east) + lat_diff(north)))
        new_east = east - rotation * north + share * (metric * lon_diff(middle))
        new_north = north + rotation * east + share * lat_diff(middle)
        return middle, new_east, new_north

    middle, east, north = step(ext_ref[0], ext_ref[1], ext_ref[2], 0)
    middle, east, north = step(middle + dep_ref[...], wet * east, wet * north, 3)
    h_ref[...] = middle[0:rows, 0:cols]
    e_ref[...] = east[0:rows, 0:cols]
    n_ref[...] = north[0:rows, 0:cols]


def tables(length, cols, devices, rows, bands):
    mode = np.arange(MODES)
    norm = np.where(mode == 0, 1.0 / length, 2.0 / length)
    lane = np.arange(LANES)

    def angle(at, number):
        phase = (at[:, None].astype(np.int64) * number[None, :]) % length
        return phase * (2.0 * math.pi / length)

    ahead = angle(lane, mode)
    inside = (lane < cols)[:, None]
    analyse = np.concatenate([np.cos(ahead) * norm, np.sin(ahead) * norm], axis=1) * inside
    place = np.where(lane < LANES - HALO, lane, lane - LANES)
    shown = ((lane < cols + HALO) | (lane >= LANES - HALO))[:, None]
    around = angle(place, mode)
    evaluate = (np.concatenate([np.cos(around), np.sin(around)], axis=1) * shown).T
    wide = np.arange(1, 2 * MODES - 1)
    spot = np.arange(GRID) * (length / GRID)
    gap = spot[None, :] - lane[:, None]
    kernel = np.full((LANES, GRID), 1.0 / length)
    for k in wide:
        kernel += (2.0 / length) * np.cos(2.0 * math.pi / length * k * gap)
    kernel *= inside
    coarse = (np.arange(GRID)[:, None] * mode[None, :]) % GRID * (2.0 * math.pi / GRID)
    to_grid = np.concatenate([np.cos(coarse), np.sin(coarse)], axis=1).T
    part = np.where(mode == 0, 1.0 / GRID, 2.0 / GRID)
    from_grid = np.concatenate([np.cos(coarse) * part, np.sin(coarse) * part], axis=1)
    turn = (np.arange(devices)[:, None] * mode[None, :]) % devices * (2.0 * math.pi / devices)
    slope = np.tile(np.sin(2.0 * math.pi / length * mode)[None, :], (8, 1))
    total = rows * bands
    index = np.arange(rows + 2 * HALO)
    local = np.where(index < rows + HALO, index, index - (rows + 2 * HALO))
    terms = np.zeros((rows + 2 * HALO, 128))
    lines = np.zeros((bands, 256))
    for b in range(bands):
        g = b * rows + local
        phi = (2.0 * ((g + 0.5) / total) - 1.0) * LIMIT
        terms[:, b] = 1.0 / np.cos(phi)
        terms[:, 16 + b] = ROTATION * np.sin(phi)
        terms[:, 32 + b] = (g >= 0) & (g < total)
        lines[b, 0:rows] = terms[0:rows, b]
        lines[b, 128 : 128 + rows] = terms[0:rows, 16 + b]
    made = dict(
        analyse=analyse,
        evaluate=evaluate,
        kernel=kernel,
        to_grid=to_grid,
        from_grid=from_grid,
        cos=np.cos(turn),
        sin=np.sin(turn),
        slope=slope,
        terms=terms,
        lines=lines,
    )
    return {name: value.astype(np.float32) for name, value in made.items()}


VMEM = pl.BlockSpec(memory_space=pltpu.VMEM)
SMEM = pl.BlockSpec(memory_space=pltpu.SMEM)


def call(kernel, name, outs, args, scratch=(), scalars=False):
    shapes = [jax.ShapeDtypeStruct(shape, F32) for shape in outs]
    specs = [SMEM if scalars and i == 0 else VMEM for i in range(len(args))]
    return pl.pallas_call(
        kernel,
        name=name,
        out_shape=shapes,
        in_specs=specs,
        out_specs=[VMEM] * len(shapes),
        scratch_shapes=[pltpu.VMEM(shape, F32) for shape in scratch],
        compiler_params=pltpu.CompilerParams(vmem_limit_bytes=40 * 2**20),
    )(*args)


def on_device(
    back_height,
    back_east,
    back_north,
    obs_values,
    obs_owner,
    obs_row,
    obs_count,
    polar_mask,
    keep_share,
    depth_level,
):
    rows, cols = back_height.shape
    bands, devices = lax.axis_size("band"), lax.axis_size("lon")
    half = devices // 2
    number, width = obs_values.shape
    ext = rows + 2 * HALO
    made = tables(cols * devices, cols, devices, rows, bands)
    place = jnp.stack([lax.axis_index("band"), lax.axis_index("lon")]).astype(jnp.int32)
    mask = polar_mask.reshape(1, rows)
    keep = keep_share.reshape(1, rows)

    def send(value, axis, shift, closed):
        count = lax.axis_size(axis)
        pairs = [(i, (i + shift) % count) for i in range(count) if closed or 0 <= i + shift < count]
        return lax.ppermute(value, axis, pairs)

    fields, west, east = call(
        pack_lon,
        "pack_lon",
        [(4, rows, LANES), (rows, 128), (rows, 128)],
        (back_height, back_east, back_north, depth_level),
    )
    right, left = send(west, "lon", -1, True), send(east, "lon", 1, True)
    outgoing, placed = call(
        pack_observations,
        "pack_observations",
        [(devices, 16, width), (devices, 256)],
        (
            place,
            obs_values,
            obs_owner,
            obs_row.reshape(1, number),
            obs_count.reshape(1, number),
            mask,
            made["cos"],
            made["sin"],
            made["analyse"],
        ),
        scalars=True,
    )
    north, south = call(
        lambda *refs: pack_lat(cols, *refs),
        "pack_lat",
        [(4 * HALO, LANES)] * 2,
        (fields, left, right, mask, keep),
    )
    below, above = send(north, "band", -1, False), send(south, "band", 1, False)
    ext_fields, weight, mine, other = call(
        lambda *refs: partial_sums(cols, *refs),
        "partial_sums",
        [(4, ext, LANES), (ext, 128), (half, 24, 128), (half, 24, 128)],
        (
            place,
            fields,
            left,
            right,
            above,
            below,
            mask,
            keep,
            made["terms"],
            made["cos"],
            made["sin"],
            made["analyse"],
            made["kernel"],
            placed,
        ),
        scratch=[(8 * devices, LANES), (2 * devices, LANES)],
        scalars=True,
    )
    swapped = lax.ppermute(other, "lon", [(i, i ^ 1) for i in range(devices)])
    groups = [[2 * i + c for i in range(half)] for c in range(2)]
    owned = lax.all_to_all(
        mine + swapped, "lon", split_axis=0, concat_axis=0, axis_index_groups=groups, tiled=True
    )
    (spread,) = call(
        own_row,
        "own_row",
        [(devices, 16, 128)],
        (
            place,
            owned,
            mask,
            keep,
            made["lines"],
            made["slope"],
            made["to_grid"],
            made["from_grid"],
        ),
        scratch=[(8, 256), (8, GRID), (16, 128)],
        scalars=True,
    )
    everyone = lax.all_to_all(spread, "lon", split_axis=0, concat_axis=0, tiled=True)
    incoming = lax.all_to_all(outgoing, "lon", split_axis=0, concat_axis=0, tiled=True)
    dep, edge = call(
        unpack_observations, "unpack_observations", [(rows, LANES), (rows, 128)], (incoming,)
    )
    dep_right = send(edge, "lon", -1, True)
    coef, depx, north, south = call(
        lambda *refs: band_edges(cols, *refs),
        "band_edges",
        [(12, rows, 128), (rows, LANES), (56, 128), (56, 128)],
        (everyone, dep, dep_right, mask),
    )
    below, above = send(north, "band", -1, False), send(south, "band", 1, False)
    return tuple(
        call(
            last_stage,
            "last_stage",
            [(rows, cols)] * 3,
            (
                place,
                ext_fields,
                weight,
                coef,
                depx,
                above,
                below,
                made["terms"],
                made["cos"],
                made["sin"],
                made["evaluate"],
            ),
            scratch=[(6 * ext, 256), (ext, LANES)],
            scalars=True,
        )
    )


def solution(mesh):
    placed = (
        P("band", "lon"),
        P("band", "lon"),
        P("band", "lon"),
        P(("band", "lon"), None),
        P(("band", "lon"), None),
        P(("band", "lon")),
        P(("band", "lon")),
        P("band"),
        P("band"),
        P("band", "lon"),
    )
    return jax.shard_map(
        on_device,
        mesh=mesh,
        in_specs=placed,
        out_specs=(P("band", "lon"), P("band", "lon"), P("band", "lon")),
        check_vma=False,
    )
```

```python
import math

import jax
import jax.numpy as jnp
import numpy as np
from jax import lax
from jax.experimental import pallas as pl
from jax.experimental.pallas import tpu as pltpu
from jax.sharding import PartitionSpec as P

MODES = 128
LEVELS = 50
COURANT = 0.25
ROTATION = 0.4
LIMIT = 1.3089969389957472
CAP = 12
LANES = 384
GRID = 512
HALO = 4
F32 = jnp.float32


def hdot(left, right):
    return jnp.dot(left, right, precision=lax.Precision.HIGHEST, preferred_element_type=F32)


def iota(shape, dim):
    return lax.broadcasted_iota(jnp.int32, shape, dim)


def to_col(row):
    size = row.shape[1]
    same = iota((size, size), 0) == iota((size, size), 1)
    return jnp.sum(jnp.where(same, row, jnp.zeros_like(row)), axis=1, keepdims=True)


def to_row(col):
    size = col.shape[0]
    same = iota((size, size), 0) == iota((size, size), 1)
    return jnp.sum(jnp.where(same, col, jnp.zeros_like(col)), axis=0, keepdims=True)


def lon_diff(field):
    width = field.shape[1]
    return 0.5 * (pltpu.roll(field, width - 1, 1) - pltpu.roll(field, 1, 1))


def lat_diff(field):
    rows = field.shape[0]
    return 0.5 * (pltpu.roll(field, rows - 1, 0) - pltpu.roll(field, 1, 0))


def rank_in_row(mask_row):
    size = mask_row.shape[1]
    before = iota((size, size), 0) < iota((size, size), 1)
    return jnp.sum(jnp.where(before, to_col(mask_row), 0), axis=0, keepdims=True)


def slot_rows(mask_row, core, devices):
    rows = mask_row.shape[1]
    half = devices // 2
    line = iota((devices, rows), 0)
    slot = jnp.where(line < half, 2 * line + core, 2 * (line - half) + 1 - core)
    hit = (slot == rank_in_row(mask_row)) & (mask_row == 1)
    return hit.astype(F32)


WEIGHT_LANE = 300 - 256


def pack_tile(
    h_hbm,
    e_hbm,
    n_hbm,
    d_hbm,
    mask_hbm,
    keep_hbm,
    fields_ref,
    west_ref,
    east_ref,
    north_ref,
    south_ref,
    filter_ref,
    h_ref,
    e_ref,
    n_ref,
    d_ref,
    mask_ref,
    keep_ref,
    sems,
):
    pairs = (
        (h_hbm, h_ref),
        (e_hbm, e_ref),
        (n_hbm, n_ref),
        (d_hbm, d_ref),
        (mask_hbm, mask_ref),
        (keep_hbm, keep_ref),
    )
    copies = [pltpu.make_async_copy(a, b, sems.at[i]) for i, (a, b) in enumerate(pairs)]
    for copy in copies:
        copy.start()
    fields_ref[...] = jnp.zeros(fields_ref.shape, F32)
    for copy in copies:
        copy.wait()
    rows, cols = h_ref.shape
    filter_ref[0:1, :] = mask_ref[...].astype(F32)
    filter_ref[1:2, :] = keep_ref[...]
    filter_ref[2:8, :] = jnp.zeros((6, rows), F32)
    weight = to_col(mask_ref[...].astype(F32) * (1.0 - keep_ref[...]))
    level = d_ref[...].astype(F32)
    wet = (level > 0).astype(F32)
    values = (h_ref[...], wet * e_ref[...], wet * n_ref[...], level)
    lane = iota((rows, 128), 1)
    west = jnp.zeros(lane.shape, F32)
    east = jnp.zeros(lane.shape, F32)
    last = cols - HALO - 256
    for f, value in enumerate(values):
        fields_ref[f, :, 0:cols] = value
        inside = (lane >= HALO * f) & (lane < HALO * f + HALO)
        head = fields_ref[f, :, 0:128]
        tail = fields_ref[f, :, 256:384]
        if f:
            head = pltpu.roll(head, HALO * f, 1)
        west = jnp.where(inside, head, west)
        east = jnp.where(inside, pltpu.roll(tail, (HALO * f - last) % 128, 1), east)
        for out_ref, at in ((north_ref, 0), (south_ref, rows - HALO)):
            span = slice(at, at + HALO)
            lines = slice(HALO * f, HALO * f + HALO)
            edge = fields_ref[f, span, 256:384]
            if f == 3:
                edge = jnp.where(iota(edge.shape, 1) == WEIGHT_LANE, weight[span, :], edge)
            out_ref[lines, 0:256] = fields_ref[f, span, 0:256]
            out_ref[lines, 256:384] = edge
    west_ref[...] = west
    east_ref[...] = east


def third_tile(tail, left, right, f, cols):
    lane = iota(tail.shape, 1)
    first = cols - 256
    shifted = pltpu.roll(right, (first - HALO * f) % 128, 1)
    tail = jnp.where((lane >= first) & (lane < first + HALO), shifted, tail)
    shifted = pltpu.roll(left, (128 - HALO - HALO * f) % 128, 1)
    return jnp.where(lane >= 128 - HALO, shifted, tail)


def row_terms(terms, band):
    lane = iota(terms.shape, 1)
    return [
        jnp.sum(jnp.where(lane == band + 16 * i, terms, 0.0), axis=1, keepdims=True)
        for i in range(3)
    ]


def partial_sums(
    cols,
    place_ref,
    fields_ref,
    left_ref,
    right_ref,
    above_ref,
    below_ref,
    filter_ref,
    terms_ref,
    cos_ref,
    sin_ref,
    table_ref,
    kernel_ref,
    placed_ref,
    ext_ref,
    weight_ref,
    west_ref,
    east_ref,
    mine_ref,
    other_ref,
    stack_ref,
    cells_ref,
):
    rows = fields_ref.shape[1]
    ext = rows + 2 * HALO
    devices = cos_ref.shape[0]
    half = devices // 2
    band, lon = place_ref[0], place_ref[1]
    for f in range(4):
        ext_ref[f, 0:rows, :] = fields_ref[f]
        ext_ref[f, rows : rows + HALO, :] = below_ref[HALO * f : HALO * f + HALO, :]
        ext_ref[f, rows + HALO : ext, :] = above_ref[HALO * f : HALO * f + HALO, :]
    edge = ext_ref[3, rows:ext, 256:384]
    marked = iota(edge.shape, 1) == WEIGHT_LANE
    mask, keep = filter_ref[0:1, :], filter_ref[1:2, :]
    weight_ref[0:rows, :] = jnp.broadcast_to(to_col(mask * (1.0 - keep)), (rows, 128))
    weight_ref[rows:ext, :] = jnp.broadcast_to(
        jnp.sum(jnp.where(marked, edge, 0.0), axis=1, keepdims=True), (2 * HALO, 128)
    )
    ext_ref[3, rows:ext, 256:384] = jnp.where(marked, 0.0, edge)
    corner = iota((2 * HALO, 128), 1)
    last = cols - HALO - 256
    for f in range(4):
        lines = slice(2 * HALO * f, 2 * HALO * f + 2 * HALO)
        inside = (corner >= HALO * f) & (corner < HALO * f + HALO)
        head = ext_ref[f, rows:ext, 0:128]
        tail = ext_ref[f, rows:ext, 256:384]
        if f:
            head = pltpu.roll(head, HALO * f, 1)
        west_ref[lines, :] = jnp.where(inside, head, 0.0)
        east_ref[lines, :] = jnp.where(inside, pltpu.roll(tail, (HALO * f - last) % 128, 1), 0.0)
    weight = weight_ref[:, 0:1]
    rest = 1.0 - weight
    metric, rotation, valid = row_terms(terms_ref[...], band)
    metric = metric * valid
    height, east, north = ext_ref[0], ext_ref[1], ext_ref[2]
    ext_ref[3, 0:rows, 256:384] = third_tile(
        ext_ref[3, 0:rows, 256:384], left_ref[...], right_ref[...], 3, cols
    )
    share = ext_ref[3] / LEVELS
    low_height = weight * height + COURANT * (
        metric * lon_diff(weight * east) + lat_diff(weight * north)
    )
    low_height = valid * low_height
    east_rest, north_rest = rest * east, rest * north
    middle = valid * (
        rest * height + COURANT * (metric * lon_diff(east_rest) + lat_diff(north_rest))
    )
    new_east = east_rest - rotation * north_rest + COURANT * share * metric * lon_diff(middle)
    new_north = north_rest + rotation * east_rest + COURANT * share * lat_diff(middle)
    chosen = slot_rows(mask, place_ref[1] % 2, devices)
    sources = (height, east, north, low_height, lat_diff(low_height), middle, new_east, new_north)
    for v, field in enumerate(sources):
        stack_ref[devices * v : devices * v + devices, :] = hdot(chosen, field[0:rows, :])
    level = ext_ref[3, 0:rows, :]
    cells_ref[0:devices, :] = hdot(chosen, (level > 0).astype(F32))
    cells_ref[devices : 2 * devices, :] = hdot(chosen, share[0:rows, :])
    sums = hdot(stack_ref[...], table_ref[...])
    turn_cos, turn_sin = cos_ref[pl.ds(lon, 1), :], sin_ref[pl.ds(lon, 1), :]
    for v in range(len(sources)):
        lines = slice(devices * v, devices * v + devices)
        on_cos, on_sin = sums[lines, 0:128], sums[lines, 128:256]
        all_cos = on_cos * turn_cos - on_sin * turn_sin
        all_sin = on_sin * turn_cos + on_cos * turn_sin
        if v == 5:
            all_cos = all_cos + placed_ref[:, 0:128]
            all_sin = all_sin + placed_ref[:, 128:256]
        for i, value in enumerate((all_cos, all_sin)):
            mine_ref[:, 2 * v + i, :] = value[0:half]
            other_ref[:, 2 * v + i, :] = value[half:devices]
    spread = pltpu.roll(hdot(cells_ref[...], kernel_ref[...]), lon * (GRID // devices), 1)
    for c in range(2):
        for i in range(4):
            part = spread[devices * c : devices * c + devices, 128 * i : 128 * i + 128]
            at = 16 + 4 * c + i
            mine_ref[:, at, :] = part[0:half]
            other_ref[:, at, :] = part[half:devices]


def pack_observations(
    place_ref,
    values_hbm,
    owner_hbm,
    row_hbm,
    count_hbm,
    near_ref,
    far_ref,
    kept_ref,
    marks_ref,
    values_ref,
    owner_ref,
    row_ref,
    count_ref,
    sems,
):
    pairs = (
        (values_hbm, values_ref),
        (owner_hbm, owner_ref),
        (row_hbm, row_ref),
        (count_hbm, count_ref),
    )
    copies = [pltpu.make_async_copy(a, b, sems.at[i]) for i, (a, b) in enumerate(pairs)]
    for copy in copies:
        copy.start()
    for copy in copies:
        copy.wait()
    number, width = values_ref.shape
    half = near_ref.shape[0]
    core = place_ref[1] % 2
    values = jnp.where(
        iota((number, width), 1) < to_col(count_ref[...]), values_ref[...], 0.0
    )
    kept_ref[...] = values
    owner_row = owner_ref[...]
    owner_col = to_col(owner_row)
    marks_ref[0:1, :] = owner_row.astype(F32)
    marks_ref[1:2, :] = row_ref[...].astype(F32)
    marks_ref[2:8, :] = jnp.zeros((6, number), F32)
    same = owner_col == owner_row
    before = same & (iota((number, number), 0) < iota((number, number), 1))
    arrival_row = jnp.sum(before.astype(jnp.int32), axis=0, keepdims=True)
    after = same & (iota((number, number), 0) > iota((number, number), 1))
    arrival_col = jnp.sum(after.astype(jnp.int32), axis=1, keepdims=True)
    chip_row, core_row = owner_row // 2, owner_row % 2
    target = chip_row * 16 + arrival_row
    label = row_ref[...].astype(F32)
    arrived = (iota((number, 128), 1) == arrival_col).astype(F32)
    for out_ref, side in ((near_ref, core), (far_ref, 1 - core)):
        goes = core_row == side
        sent = ((iota((16 * half, number), 0) == target) & goes).astype(F32)
        block = hdot(sent, values).reshape(half, 16, width)
        out_ref[:, 0:CAP, :] = block[:, 0:CAP, 0:128]
        out_ref[:, CAP : 2 * CAP, :] = block[:, 0:CAP, 128:256]
        named = ((iota((half, number), 0) == chip_row) & goes).astype(F32) * label
        out_ref[:, 2 * CAP : 32, :] = jnp.zeros((half, 32 - 2 * CAP, 128), F32)
        out_ref[:, 2 * CAP, :] = hdot(named, arrived)


def sum_observations(
    place_ref, values_ref, marks_ref, filter_ref, cos_ref, sin_ref, table_ref, placed_ref
):
    number, width = values_ref.shape
    devices = cos_ref.shape[0]
    owner_col = to_col(marks_ref[0:1, :])
    sums = hdot(values_ref[...], table_ref[0:width, :])
    whose = (iota((number, devices), 1).astype(F32) == owner_col).astype(F32)
    turn_cos, turn_sin = hdot(whose, cos_ref[...]), hdot(whose, sin_ref[...])
    on_cos, on_sin = sums[:, 0:128], sums[:, 128:256]
    all_cos = on_cos * turn_cos - on_sin * turn_sin
    all_sin = on_sin * turn_cos + on_cos * turn_sin
    mask = filter_ref[0:1, :]
    rows = mask.shape[1]
    in_row = (iota((rows, number), 0).astype(F32) == marks_ref[1:2, :]).astype(F32)
    chosen = hdot(slot_rows(mask, place_ref[1] % 2, devices), in_row)
    placed_ref[:, 0:128] = hdot(chosen, all_cos)
    placed_ref[:, 128:256] = hdot(chosen, all_sin)


def join(mine_ref, swapped_ref, near_ref, far_ref, out_ref):
    half = out_ref.shape[0]
    out_ref[:, 0:24, :] = mine_ref[...] + swapped_ref[...]
    out_ref[:, 24:48, :] = near_ref[:, 0:24, :]
    out_ref[:, 48:72, :] = far_ref[:, 0:24, :]
    out_ref[:, 72:80, :] = jnp.zeros((half, 8, 128), F32)
    out_ref[:, 72, :] = near_ref[:, 24, :]
    out_ref[:, 73, :] = far_ref[:, 24, :]


def unpack_observations(in_ref, corner_ref, dep_ref, west_ref):
    half = in_ref.shape[0]
    rows = dep_ref.shape[0]
    lines = 4 * CAP
    total = half * lines
    spot = iota((128, total), 1) % lines
    label_row = jnp.zeros((1, total), F32)
    own = iota((half, total), 1) // lines == iota((half, total), 0)
    for s in range(2):
        here = (spot // (2 * CAP) == s) & (spot % CAP == iota((128, total), 0))
        across = hdot(in_ref[:, 72 + s, :], here.astype(F32))
        label_row = label_row + jnp.sum(jnp.where(own, across, 0.0), axis=0, keepdims=True)
    line = iota((rows, total), 1) % lines
    hit = iota((rows, total), 0).astype(F32) == label_row
    data = in_ref[:, 24 : 24 + lines, :].reshape(total, 128)
    for i in range(2):
        side = (hit & ((line // CAP) % 2 == i)).astype(F32)
        dep_ref[:, 128 * i : 128 * i + 128] = hdot(side, data)
    dep_ref[:, 256:384] = jnp.zeros((rows, 128), F32)
    west_ref[0:rows, :] = pltpu.roll(dep_ref[:, 0:128], 14, 1)
    west_ref[rows : rows + corner_ref.shape[0], :] = corner_ref[...]


def own_row(
    place_ref,
    in_ref,
    filter_ref,
    lines_ref,
    slope_ref,
    to_grid_ref,
    from_grid_ref,
    res_ref,
    left_ref,
    grid_ref,
):
    band, lon = place_ref[0], place_ref[1]
    sums = in_ref[0, 0:24, :]
    for i in range(1, in_ref.shape[0]):
        sums = sums + in_ref[i, 0:24, :]
    mask, keep = filter_ref[0:1, :], filter_ref[1:2, :]
    chosen = ((rank_in_row(mask) == lon) & (mask == 1)).astype(F32)

    def pick(row):
        return jnp.sum(chosen * row, axis=1, keepdims=True)

    rows = mask.shape[1]
    weight = pick(1.0 - keep)
    both = lines_ref[pl.ds(band, 1), :]
    metric = pick(both[:, 0:rows])
    rotation = pick(both[:, 128 : 128 + rows])

    def line(i):
        return sums[i : i + 1, :]

    slope = slope_ref[0:1, :]
    left_ref[...] = jnp.zeros(left_ref.shape, F32)
    pairs = (
        (weight * (line(2) - rotation * line(4)), weight * (line(3) - rotation * line(5))),
        (metric * slope * line(7), -metric * slope * line(6)),
        (weight * (line(4) + rotation * line(2)), weight * (line(5) + rotation * line(3))),
        (line(8), line(9)),
    )
    for i, (on_cos, on_sin) in enumerate(pairs):
        left_ref[i : i + 1, 0:128] = on_cos
        left_ref[i : i + 1, 128:256] = on_sin
    at = hdot(left_ref[...], to_grid_ref[...])
    wet = jnp.concatenate([line(16), line(17), line(18), line(19)], axis=1)
    share = COURANT * jnp.concatenate([line(20), line(21), line(22), line(23)], axis=1)
    grid_ref[...] = jnp.zeros(grid_ref.shape, F32)
    grid_ref[0:1, :] = wet * at[0:1] + share * at[1:2]
    grid_ref[1:2, :] = wet * at[2:3] + share * at[3:4]
    back = hdot(grid_ref[...], from_grid_ref[...])
    res_ref[0:6, :] = sums[0:6]
    res_ref[6:8, :] = sums[10:12] + sums[6:8]
    for i in range(2):
        res_ref[8 + 2 * i : 9 + 2 * i, :] = line(12 + 2 * i) + back[i : i + 1, 0:128]
        res_ref[9 + 2 * i : 10 + 2 * i, :] = line(13 + 2 * i) + back[i : i + 1, 128:256]


def spread_pair(pair_ref, out_ref):
    both = jnp.concatenate([pair_ref[0], pair_ref[1]], axis=0)
    out_ref[...] = jnp.broadcast_to(both[None], out_ref.shape)


def band_edges(cols, all_ref, dep_ref, edge_ref, filter_ref, coef_ref, depx_ref, north_ref, south_ref):
    half = all_ref.shape[0]
    rows = dep_ref.shape[0]
    mask = filter_ref[0:1, :]
    rank = to_col(rank_in_row(mask))
    kept = to_col(mask) == 1
    first = cols - 256
    lane = iota((rows, 128), 1)
    depx_ref[:, 0:256] = dep_ref[:, 0:256]
    depx_ref[:, 256:384] = jnp.where(
        (lane == first) | (lane == first + 1), edge_ref[0:rows, :], 0.0
    )
    chosen = [
        ((2 * iota((rows, half), 1) + c == rank) & kept).astype(F32) for c in range(2)
    ]
    for v in range(12):
        own = hdot(chosen[0], all_ref[:, v, :]) + hdot(chosen[1], all_ref[:, 12 + v, :])
        coef_ref[v] = own
        north_ref[4 * v : 4 * v + 4, :] = own[0:4]
        south_ref[4 * v : 4 * v + 4, :] = own[rows - 4 : rows]
    for out_ref, at in ((north_ref, 0), (south_ref, rows - 2)):
        for r in range(2):
            for t in range(3):
                out_ref[48 + 3 * r + t : 49 + 3 * r + t, :] = depx_ref[
                    at + r : at + r + 1, 128 * t : 128 * t + 128
                ]
        out_ref[54:56, :] = jnp.zeros((2, 128), F32)


def last_stage(
    place_ref,
    wide_ref,
    left_ref,
    right_ref,
    corner_left_ref,
    corner_right_ref,
    weight_ref,
    coef_ref,
    depx_ref,
    above_ref,
    below_ref,
    terms_ref,
    cos_ref,
    sin_ref,
    table_ref,
    h_ref,
    e_ref,
    n_ref,
    stack_ref,
    dep_ref,
    ext_ref,
):
    ext = ext_ref.shape[1]
    rows, cols = h_ref.shape
    for f in range(4):
        ext_ref[f, :, 0:256] = wide_ref[f, :, 0:256]
        ext_ref[f, 0:rows, 256:384] = third_tile(
            wide_ref[f, 0:rows, 256:384], left_ref[...], right_ref[...], f, cols
        )
        lines = slice(2 * HALO * f, 2 * HALO * f + 2 * HALO)
        ext_ref[f, rows:ext, 256:384] = third_tile(
            wide_ref[f, rows:ext, 256:384],
            corner_left_ref[lines, :],
            corner_right_ref[rows + 2 * HALO * f : rows + 2 * HALO * f + 2 * HALO, :],
            f,
            cols,
        )
    band, lon = place_ref[0], place_ref[1]
    turn_cos, turn_sin = cos_ref[pl.ds(lon, 1), :], sin_ref[pl.ds(lon, 1), :]
    for f in range(6):
        for lines, on_cos, on_sin in (
            (slice(ext * f, ext * f + rows), coef_ref[2 * f], coef_ref[2 * f + 1]),
            (
                slice(ext * f + rows, ext * f + rows + 4),
                below_ref[8 * f : 8 * f + 4, :],
                below_ref[8 * f + 4 : 8 * f + 8, :],
            ),
            (
                slice(ext * f + rows + 4, ext * f + ext),
                above_ref[8 * f : 8 * f + 4, :],
                above_ref[8 * f + 4 : 8 * f + 8, :],
            ),
        ):
            stack_ref[lines, 0:128] = on_cos * turn_cos + on_sin * turn_sin
            stack_ref[lines, 128:256] = on_sin * turn_cos - on_cos * turn_sin
    low = hdot(stack_ref[...], table_ref[...])
    dep_ref[0:rows, :] = depx_ref[...]
    dep_ref[rows:ext, :] = jnp.zeros((ext - rows, LANES), F32)
    for in_ref, at in ((below_ref, rows), (above_ref, ext - 2)):
        for r in range(2):
            for t in range(3):
                dep_ref[at + r : at + r + 1, 128 * t : 128 * t + 128] = in_ref[
                    48 + 3 * r + t : 49 + 3 * r + t, :
                ]
    weight = weight_ref[:, 0:1]
    metric, rotation, valid = row_terms(terms_ref[...], band)
    level = ext_ref[3]
    wet = (level > 0).astype(F32)
    share = COURANT * (level / LEVELS)

    def step(height, east, north, f):
        height = height + weight * (low[ext * f : ext * f + ext] - height)
        east = east + weight * (low[ext * f + ext : ext * f + 2 * ext] - east)
        north = north + weight * (low[ext * f + 2 * ext : ext * f + 3 * ext] - north)
        middle = valid * (height + COURANT * (metric * lon_diff(east) + lat_diff(north)))
        new_east = east - rotation * north + share * (metric * lon_diff(middle))
        new_north = north + rotation * east + share * lat_diff(middle)
        return middle, new_east, new_north

    middle, east, north = step(ext_ref[0], ext_ref[1], ext_ref[2], 0)
    middle, east, north = step(middle + dep_ref[...], wet * east, wet * north, 3)
    h_ref[...] = middle[0:rows, 0:cols]
    e_ref[...] = east[0:rows, 0:cols]
    n_ref[...] = north[0:rows, 0:cols]


def tables(length, cols, devices, rows, bands):
    mode = np.arange(MODES)
    norm = np.where(mode == 0, 1.0 / length, 2.0 / length)
    lane = np.arange(LANES)

    def angle(at, number):
        phase = (at[:, None].astype(np.int64) * number[None, :]) % length
        return phase * (2.0 * math.pi / length)

    inside = (lane < cols)[:, None]
    place = np.where(lane < LANES - HALO, lane, lane - LANES)
    shown = ((lane < cols + HALO) | (lane >= LANES - HALO))[:, None]
    around = angle(place, mode)
    analyse = np.concatenate([np.cos(around) * norm, np.sin(around) * norm], axis=1) * shown
    evaluate = (np.concatenate([np.cos(around), np.sin(around)], axis=1) * shown).T
    wide = np.arange(1, 2 * MODES - 1)
    spot = np.arange(GRID) * (length / GRID)
    gap = spot[None, :] - lane[:, None]
    kernel = np.full((LANES, GRID), 1.0 / length)
    for k in wide:
        kernel += (2.0 / length) * np.cos(2.0 * math.pi / length * k * gap)
    kernel *= inside
    coarse = (np.arange(GRID)[:, None] * mode[None, :]) % GRID * (2.0 * math.pi / GRID)
    to_grid = np.concatenate([np.cos(coarse), np.sin(coarse)], axis=1).T
    part = np.where(mode == 0, 1.0 / GRID, 2.0 / GRID)
    from_grid = np.concatenate([np.cos(coarse) * part, np.sin(coarse) * part], axis=1)
    turn = (np.arange(devices)[:, None] * mode[None, :]) % devices * (2.0 * math.pi / devices)
    slope = np.tile(np.sin(2.0 * math.pi / length * mode)[None, :], (8, 1))
    total = rows * bands
    index = np.arange(rows + 2 * HALO)
    local = np.where(index < rows + HALO, index, index - (rows + 2 * HALO))
    terms = np.zeros((rows + 2 * HALO, 128))
    lines = np.zeros((bands, 256))
    for b in range(bands):
        g = b * rows + local
        phi = (2.0 * ((g + 0.5) / total) - 1.0) * LIMIT
        terms[:, b] = 1.0 / np.cos(phi)
        terms[:, 16 + b] = ROTATION * np.sin(phi)
        terms[:, 32 + b] = (g >= 0) & (g < total)
        lines[b, 0:rows] = terms[0:rows, b]
        lines[b, 128 : 128 + rows] = terms[0:rows, 16 + b]
    made = dict(
        analyse=analyse,
        evaluate=evaluate,
        kernel=kernel,
        to_grid=to_grid,
        from_grid=from_grid,
        cos=np.cos(turn),
        sin=np.sin(turn),
        slope=slope,
        terms=terms,
        lines=lines,
    )
    return {name: value.astype(np.float32) for name, value in made.items()}


VMEM = pl.BlockSpec(memory_space=pltpu.VMEM)
SMEM = pl.BlockSpec(memory_space=pltpu.SMEM)
HBM = pl.BlockSpec(memory_space=pltpu.HBM)


def call(kernel, name, outs, args, scratch=(), scalars=False, direct=(), cost=1.0):
    shapes = [jax.ShapeDtypeStruct(shape, F32) for shape in outs]
    specs = [
        SMEM if scalars and i == 0 else HBM if i in direct else VMEM for i in range(len(args))
    ]
    args = [
        pltpu.with_memory_space_constraint(arg, pltpu.HBM) if i in direct else arg
        for i, arg in enumerate(args)
    ]
    held = [pltpu.VMEM(args[i].shape, args[i].dtype) for i in direct]
    held += [pltpu.SemaphoreType.DMA((len(direct),))] if direct else []
    return pl.pallas_call(
        kernel,
        name=name,
        out_shape=shapes,
        in_specs=specs,
        out_specs=[VMEM] * len(shapes),
        scratch_shapes=held + [pltpu.VMEM(shape, F32) for shape in scratch],
        cost_estimate=pl.CostEstimate(
            flops=int(cost * 1e9), bytes_accessed=int(cost * 2e6), transcendentals=0
        ),
        compiler_params=pltpu.CompilerParams(
            vmem_limit_bytes=40 * 2**20
        ),
    )(*args)


LON = ("z", "core")


def on_device(
    back_height,
    back_east,
    back_north,
    obs_values,
    obs_owner,
    obs_row,
    obs_count,
    polar_mask,
    keep_share,
    depth_level,
):
    rows, cols = back_height.shape
    bands, devices = lax.axis_size("band"), lax.axis_size(LON)
    half = devices // 2
    number, width = obs_values.shape
    ext = rows + 2 * HALO
    made = tables(cols * devices, cols, devices, rows, bands)
    place = jnp.stack([lax.axis_index("band"), lax.axis_index(LON)]).astype(jnp.int32)

    def send(value, axis, shift, closed):
        count = lax.axis_size(axis)
        pairs = [(i, (i + shift) % count) for i in range(count) if closed or 0 <= i + shift < count]
        return lax.ppermute(value, axis, pairs)

    fields, west, east, north, south, kept = call(
        pack_tile,
        "pack_tile",
        [(4, rows, LANES), (rows, 128), (rows, 128)] + [(4 * HALO, LANES)] * 2 + [(8, rows)],
        (
            back_height,
            back_east,
            back_north,
            depth_level,
            polar_mask.reshape(1, rows),
            keep_share.reshape(1, rows),
        ),
        direct=range(6),
    )
    below, above = send(north, "band", -1, False), send(south, "band", 1, False)
    right, left = send(west, LON, -1, True), send(east, LON, 1, True)
    other_core = [(i, i ^ 1) for i in range(devices)]
    near, far, values, marks = call(
        pack_observations,
        "pack_observations",
        [(half, 32, 128), (half, 32, 128), (number, width), (8, number)],
        (
            place,
            obs_values,
            obs_owner.reshape(1, number),
            obs_row.reshape(1, number),
            obs_count.reshape(1, number),
        ),
        cost=3.0,
        scalars=True,
        direct=range(1, 5),
    )
    far = lax.ppermute(far, LON, other_core)
    (placed,) = call(
        sum_observations,
        "sum_observations",
        [(devices, 256)],
        (place, values, marks, kept, made["cos"], made["sin"], made["analyse"]),
        scalars=True,
    )
    wide, weight, corner_west, corner_east, mine, other = call(
        lambda *refs: partial_sums(cols, *refs),
        "partial_sums",
        [(4, ext, LANES), (ext, 128)] + [(8 * HALO, 128)] * 2 + [(half, 24, 128)] * 2,
        (
            place,
            fields,
            left,
            right,
            above,
            below,
            kept,
            made["terms"],
            made["cos"],
            made["sin"],
            made["analyse"],
            made["kernel"],
            placed,
        ),
        scratch=[(8 * devices, LANES), (2 * devices, LANES)],
        scalars=True,
    )
    swapped = lax.ppermute(other, LON, other_core)
    (joined,) = call(join, "join", [(half, 80, 128)], (mine, swapped, near, far))
    owned = lax.all_to_all(joined, "z", split_axis=0, concat_axis=0, tiled=True)
    (result,) = call(
        own_row,
        "own_row",
        [(12, 128)],
        (
            place,
            owned,
            kept,
            made["lines"],
            made["slope"],
            made["to_grid"],
            made["from_grid"],
        ),
        scratch=[(8, 256), (8, GRID)],
        scalars=True,
    )
    pair = lax.all_gather(result, "core", axis=0, tiled=False)
    (spread,) = call(spread_pair, "spread_pair", [(half, 24, 128)], (pair,))
    everyone = lax.all_to_all(spread, "z", split_axis=0, concat_axis=0, tiled=True)
    dep, west = call(
        unpack_observations,
        "unpack_observations",
        [(rows, LANES), (rows + 8 * HALO, 128)],
        (owned, corner_west),
    )
    corner_east = lax.optimization_barrier((corner_east, spread))[0]
    corner_right, corner_left = send(west, LON, -1, True), send(corner_east, LON, 1, True)
    dep, corner_left = lax.optimization_barrier((dep, corner_left))
    coef, depx, north, south = call(
        lambda *refs: band_edges(cols, *refs),
        "band_edges",
        [(12, rows, 128), (rows, LANES), (56, 128), (56, 128)],
        (everyone, dep, corner_right, kept),
    )
    below, above = send(north, "band", -1, False), send(south, "band", 1, False)
    return tuple(
        call(
            last_stage,
            "last_stage",
            [(rows, cols)] * 3,
            (
                place,
                wide,
                left,
                right,
                corner_left,
                corner_right,
                weight,
                coef,
                depx,
                above,
                below,
                made["terms"],
                made["cos"],
                made["sin"],
                made["evaluate"],
            ),
            scratch=[(6 * ext, 256), (ext, LANES), (4, ext, LANES)],
            scalars=True,
        )
    )


def solution(mesh):
    placed = (
        P("band", LON),
        P("band", LON),
        P("band", LON),
        P(("band", *LON), None),
        P(("band", *LON), None),
        P(("band", *LON)),
        P(("band", *LON)),
        P("band"),
        P("band"),
        P("band", LON),
    )
    fine = jax.sharding.Mesh(
        mesh.devices.reshape(mesh.devices.shape[0], -1, 2), ("band", *LON)
    )
    return jax.shard_map(
        on_device,
        mesh=fine,
        in_specs=placed,
        out_specs=(P("band", LON), P("band", LON), P("band", LON)),
        check_vma=False,
    )
```

```python
import math

import jax
import jax.numpy as jnp
import ml_dtypes
import numpy as np
from jax import lax
from jax.experimental import pallas as pl
from jax.experimental.pallas import tpu as pltpu
from jax.sharding import PartitionSpec as P

MODES = 128
LEVELS = 50
COURANT = 0.25
ROTATION = 0.4
LIMIT = 1.3089969389957472
CAP = 12
LANES = 384
GRID = 512
HALO = 4
F32 = jnp.float32


def hdot(left, right):
    return jnp.dot(left, right, precision=lax.Precision.HIGHEST, preferred_element_type=F32)


def halves_of(value):
    high = value.astype(jnp.bfloat16)
    return high, (value - high.astype(F32)).astype(jnp.bfloat16)


def bdot(left, right):
    return jnp.dot(left, right, preferred_element_type=F32)


def tdot(left, table_ref):
    high, low = halves_of(left)
    return bdot(high, table_ref[0]) + bdot(low, table_ref[0]) + bdot(high, table_ref[1])


def mdot(left, right):
    return jnp.dot(left, right, precision=lax.Precision.HIGH, preferred_element_type=F32)


def iota(shape, dim):
    return lax.broadcasted_iota(jnp.int32, shape, dim)


def to_col(row):
    size = row.shape[1]
    same = iota((size, size), 0) == iota((size, size), 1)
    return jnp.sum(jnp.where(same, row, jnp.zeros_like(row)), axis=1, keepdims=True)


def to_row(col):
    size = col.shape[0]
    same = iota((size, size), 0) == iota((size, size), 1)
    return jnp.sum(jnp.where(same, col, jnp.zeros_like(col)), axis=0, keepdims=True)


def lon_diff(field):
    width = field.shape[1]
    return 0.5 * (pltpu.roll(field, width - 1, 1) - pltpu.roll(field, 1, 1))


def lat_diff(field):
    rows = field.shape[0]
    return 0.5 * (pltpu.roll(field, rows - 1, 0) - pltpu.roll(field, 1, 0))


def rank_in_row(mask_row):
    size = mask_row.shape[1]
    before = iota((size, size), 0) < iota((size, size), 1)
    return jnp.sum(jnp.where(before, to_col(mask_row), 0), axis=0, keepdims=True)


def slot_rows(mask_row, core, devices):
    rows = mask_row.shape[1]
    half = devices // 2
    line = iota((devices, rows), 0)
    slot = jnp.where(line < half, 2 * line + core, 2 * (line - half) + 1 - core)
    hit = (slot == rank_in_row(mask_row)) & (mask_row == 1)
    return hit.astype(F32)


WEIGHT_LANE = 300 - 256


def pack_tile(
    h_hbm,
    e_hbm,
    n_hbm,
    d_hbm,
    mask_hbm,
    keep_hbm,
    owner_hbm,
    row_hbm,
    count_hbm,
    fields_ref,
    west_ref,
    east_ref,
    north_ref,
    south_ref,
    filter_ref,
    marks_ref,
    h_ref,
    e_ref,
    n_ref,
    d_ref,
    mask_ref,
    keep_ref,
    owner_ref,
    row_ref,
    count_ref,
    sems,
):
    pairs = (
        (h_hbm, h_ref),
        (e_hbm, e_ref),
        (n_hbm, n_ref),
        (d_hbm, d_ref),
        (mask_hbm, mask_ref),
        (keep_hbm, keep_ref),
        (owner_hbm, owner_ref),
        (row_hbm, row_ref),
        (count_hbm, count_ref),
    )
    copies = [pltpu.make_async_copy(a, b, sems.at[i]) for i, (a, b) in enumerate(pairs)]
    for copy in copies:
        copy.start()
    fields_ref[...] = jnp.zeros(fields_ref.shape, F32)
    for copy in copies:
        copy.wait()
    rows, cols = h_ref.shape
    filter_ref[0:1, :] = mask_ref[...].astype(F32)
    filter_ref[1:2, :] = keep_ref[...]
    filter_ref[2:8, :] = jnp.zeros((6, rows), F32)
    for i, in_ref in enumerate((owner_ref, row_ref, count_ref)):
        marks_ref[i : i + 1, :] = in_ref[...].astype(F32)
    marks_ref[3:8, :] = jnp.zeros((5, marks_ref.shape[1]), F32)
    weight = to_col(mask_ref[...].astype(F32) * (1.0 - keep_ref[...]))
    level = d_ref[...].astype(F32)
    wet = (level > 0).astype(F32)
    values = (h_ref[...], wet * e_ref[...], wet * n_ref[...], level)
    lane = iota((rows, 128), 1)
    west = jnp.zeros(lane.shape, F32)
    east = jnp.zeros(lane.shape, F32)
    last = cols - HALO - 256
    for f, value in enumerate(values):
        fields_ref[f, :, 0:cols] = value
        inside = (lane >= HALO * f) & (lane < HALO * f + HALO)
        head = fields_ref[f, :, 0:128]
        tail = fields_ref[f, :, 256:384]
        if f:
            head = pltpu.roll(head, HALO * f, 1)
        west = jnp.where(inside, head, west)
        east = jnp.where(inside, pltpu.roll(tail, (HALO * f - last) % 128, 1), east)
        for out_ref, at in ((north_ref, 0), (south_ref, rows - HALO)):
            span = slice(at, at + HALO)
            lines = slice(HALO * f, HALO * f + HALO)
            edge = fields_ref[f, span, 256:384]
            if f == 3:
                edge = jnp.where(iota(edge.shape, 1) == WEIGHT_LANE, weight[span, :], edge)
            out_ref[lines, 0:256] = fields_ref[f, span, 0:256]
            out_ref[lines, 256:384] = edge
    west_ref[...] = west
    east_ref[...] = east


def third_tile(tail, left, right, f, cols):
    lane = iota(tail.shape, 1)
    first = cols - 256
    shifted = pltpu.roll(right, (first - HALO * f) % 128, 1)
    tail = jnp.where((lane >= first) & (lane < first + HALO), shifted, tail)
    shifted = pltpu.roll(left, (128 - HALO - HALO * f) % 128, 1)
    return jnp.where(lane >= 128 - HALO, shifted, tail)


def row_terms(terms, band):
    lane = iota(terms.shape, 1)
    return [
        jnp.sum(jnp.where(lane == band + 16 * i, terms, 0.0), axis=1, keepdims=True)
        for i in range(3)
    ]


def partial_sums(
    cols,
    place_ref,
    fields_ref,
    left_ref,
    right_ref,
    above_ref,
    below_ref,
    filter_ref,
    terms_ref,
    cos_ref,
    sin_ref,
    table_ref,
    kernel_ref,
    placed_ref,
    near_ref,
    far_ref,
    ext_ref,
    weight_ref,
    west_ref,
    east_ref,
    mine_ref,
    other_ref,
    high_ref,
    low_ref,
    cells_ref,
):
    rows = fields_ref.shape[1]
    ext = rows + 2 * HALO
    devices = cos_ref.shape[0]
    half = devices // 2
    band, lon = place_ref[0], place_ref[1]
    for f in range(4):
        ext_ref[f, 0:rows, :] = fields_ref[f]
        ext_ref[f, rows : rows + HALO, :] = below_ref[HALO * f : HALO * f + HALO, :]
        ext_ref[f, rows + HALO : ext, :] = above_ref[HALO * f : HALO * f + HALO, :]
    edge = ext_ref[3, rows:ext, 256:384]
    marked = iota(edge.shape, 1) == WEIGHT_LANE
    mask, keep = filter_ref[0:1, :], filter_ref[1:2, :]
    weight_ref[0:rows, :] = jnp.broadcast_to(to_col(mask * (1.0 - keep)), (rows, 128))
    weight_ref[rows:ext, :] = jnp.broadcast_to(
        jnp.sum(jnp.where(marked, edge, 0.0), axis=1, keepdims=True), (2 * HALO, 128)
    )
    ext_ref[3, rows:ext, 256:384] = jnp.where(marked, 0.0, edge)
    corner = iota((2 * HALO, 128), 1)
    last = cols - HALO - 256
    for f in range(4):
        lines = slice(2 * HALO * f, 2 * HALO * f + 2 * HALO)
        inside = (corner >= HALO * f) & (corner < HALO * f + HALO)
        head = ext_ref[f, rows:ext, 0:128]
        tail = ext_ref[f, rows:ext, 256:384]
        if f:
            head = pltpu.roll(head, HALO * f, 1)
        west_ref[lines, :] = jnp.where(inside, head, 0.0)
        east_ref[lines, :] = jnp.where(inside, pltpu.roll(tail, (HALO * f - last) % 128, 1), 0.0)
    weight = weight_ref[:, 0:1]
    rest = 1.0 - weight
    metric, rotation, valid = row_terms(terms_ref[...], band)
    metric = metric * valid
    height, east, north = ext_ref[0], ext_ref[1], ext_ref[2]
    ext_ref[3, 0:rows, 256:384] = third_tile(
        ext_ref[3, 0:rows, 256:384], left_ref[...], right_ref[...], 3, cols
    )
    share = ext_ref[3] / LEVELS
    low_height = weight * height + COURANT * (
        metric * lon_diff(weight * east) + lat_diff(weight * north)
    )
    low_height = valid * low_height
    east_rest, north_rest = rest * east, rest * north
    middle = valid * (
        rest * height + COURANT * (metric * lon_diff(east_rest) + lat_diff(north_rest))
    )
    new_east = east_rest - rotation * north_rest + COURANT * share * metric * lon_diff(middle)
    new_north = north_rest + rotation * east_rest + COURANT * share * lat_diff(middle)
    chosen = slot_rows(mask, place_ref[1] % 2, devices).astype(jnp.bfloat16)
    sources = (height, east, north, low_height, lat_diff(low_height), middle, new_east, new_north)
    for v, field in enumerate(sources):
        lines = slice(devices * v, devices * v + devices)
        high, low = halves_of(field[0:rows, :])
        high_ref[lines, :] = bdot(chosen, high).astype(jnp.bfloat16)
        low_ref[lines, :] = bdot(chosen, low).astype(jnp.bfloat16)
    mine_ref[:, 24:56, :] = near_ref[...]
    other_ref[:, 24:56, :] = far_ref[...]
    level = ext_ref[3, 0:rows, :]
    for c, cells in enumerate(((level > 0).astype(F32), level)):
        cells_ref[devices * c : devices * c + devices, :] = bdot(
            chosen, cells.astype(jnp.bfloat16)
        ).astype(jnp.bfloat16)
    sums = bdot(high_ref[...], table_ref[0]) + bdot(low_ref[...], table_ref[0])
    sums = sums + bdot(high_ref[...], table_ref[1])
    turn_cos, turn_sin = cos_ref[pl.ds(lon, 1), :], sin_ref[pl.ds(lon, 1), :]
    for v in range(len(sources)):
        lines = slice(devices * v, devices * v + devices)
        on_cos, on_sin = sums[lines, 0:128], sums[lines, 128:256]
        all_cos = on_cos * turn_cos - on_sin * turn_sin
        all_sin = on_sin * turn_cos + on_cos * turn_sin
        if v == 5:
            all_cos = all_cos + placed_ref[:, 0:128]
            all_sin = all_sin + placed_ref[:, 128:256]
        for i, value in enumerate((all_cos, all_sin)):
            mine_ref[:, 2 * v + i, :] = value[0:half]
            other_ref[:, 2 * v + i, :] = value[half:devices]
    spread = bdot(cells_ref[...], kernel_ref[0]) + bdot(cells_ref[...], kernel_ref[1])
    spread = pltpu.roll(spread, lon * (GRID // devices), 1)
    for c in range(2):
        for i in range(4):
            part = spread[devices * c : devices * c + devices, 128 * i : 128 * i + 128]
            at = 16 + 4 * c + i
            mine_ref[:, at, :] = part[0:half]
            other_ref[:, at, :] = part[half:devices]


def pack_observations(place_ref, values_ref, marks_ref, near_ref, far_ref, kept_ref):
    number, width = values_ref.shape
    half = near_ref.shape[0]
    core = place_ref[1] % 2
    lengths = to_col(marks_ref[2:3, :])
    values = jnp.where(iota((number, width), 1).astype(F32) < lengths, values_ref[...], 0.0)
    kept_ref[...] = values
    owner_row = marks_ref[0:1, :].astype(jnp.int32)
    owner_col = to_col(owner_row)
    same = owner_col == owner_row
    before = same & (iota((number, number), 0) < iota((number, number), 1))
    arrival_row = jnp.sum(before.astype(jnp.int32), axis=0, keepdims=True)
    after = same & (iota((number, number), 0) > iota((number, number), 1))
    arrival_col = jnp.sum(after.astype(jnp.int32), axis=1, keepdims=True)
    chip_row, core_row = owner_row // 2, owner_row % 2
    target = chip_row * 16 + arrival_row
    label = marks_ref[1:2, :]
    arrived = (iota((number, 128), 1) == arrival_col).astype(F32)
    for out_ref, side in ((near_ref, core), (far_ref, 1 - core)):
        goes = core_row == side
        sent = ((iota((16 * half, number), 0) == target) & goes).astype(F32)
        block = hdot(sent, values).reshape(half, 16, width)
        out_ref[:, 0:CAP, :] = block[:, 0:CAP, 0:128]
        out_ref[:, CAP : 2 * CAP, :] = block[:, 0:CAP, 128:256]
        named = ((iota((half, number), 0) == chip_row) & goes).astype(F32) * label
        out_ref[:, 2 * CAP : 32, :] = jnp.zeros((half, 32 - 2 * CAP, 128), F32)
        out_ref[:, 2 * CAP, :] = hdot(named, arrived)


def sum_observations(
    place_ref, values_ref, marks_ref, filter_ref, cos_ref, sin_ref, table_ref, placed_ref
):
    number, width = values_ref.shape
    devices = cos_ref.shape[0]
    owner_col = to_col(marks_ref[0:1, :])
    sums = tdot(values_ref[...], table_ref.at[:, 0:width, :])
    whose = (iota((number, devices), 1).astype(F32) == owner_col).astype(F32)
    turn_cos, turn_sin = mdot(whose, cos_ref[...]), mdot(whose, sin_ref[...])
    on_cos, on_sin = sums[:, 0:128], sums[:, 128:256]
    all_cos = on_cos * turn_cos - on_sin * turn_sin
    all_sin = on_sin * turn_cos + on_cos * turn_sin
    mask = filter_ref[0:1, :]
    rows = mask.shape[1]
    in_row = (iota((rows, number), 0).astype(F32) == marks_ref[1:2, :]).astype(F32)
    chosen = mdot(slot_rows(mask, place_ref[1] % 2, devices), in_row)
    placed_ref[:, 0:128] = mdot(chosen, all_cos)
    placed_ref[:, 128:256] = mdot(chosen, all_sin)


def join(mine_ref, swapped_ref, out_ref):
    for i in range(12):
        pair = slice(2 * i, 2 * i + 2)
        out_ref[:, i, :, :] = mine_ref[:, pair, :] + swapped_ref[:, pair, :]
    for i in range(12, 24):
        out_ref[:, i, :, :] = mine_ref[:, 2 * i : 2 * i + 2, :]
        out_ref[:, i + 12, :, :] = swapped_ref[:, 2 * i : 2 * i + 2, :]
    out_ref[:, 36, 0, :] = mine_ref[:, 48, :]
    out_ref[:, 36, 1, :] = swapped_ref[:, 48, :]


def unpack_observations(in_ref, corner_ref, dep_ref, west_ref, data_ref):
    half = in_ref.shape[0]
    rows = dep_ref.shape[0]
    lines = 4 * CAP
    total = half * lines
    spot = iota((128, total), 1) % lines
    label_row = jnp.zeros((1, total), F32)
    own = iota((half, total), 1) // lines == iota((half, total), 0)
    for s in range(2):
        here = (spot // (2 * CAP) == s) & (spot % CAP == iota((128, total), 0))
        across = hdot(in_ref[:, 36, s, :], here.astype(F32))
        label_row = label_row + jnp.sum(jnp.where(own, across, 0.0), axis=0, keepdims=True)
    line = iota((rows, total), 1) % lines
    hit = iota((rows, total), 0).astype(F32) == label_row
    for i in range(2 * CAP):
        data_ref[:, 2 * i : 2 * i + 2, :] = in_ref[:, 12 + i, :, :]
    data = data_ref[...].reshape(total, 128)
    for i in range(2):
        side = (hit & ((line // CAP) % 2 == i)).astype(F32)
        dep_ref[:, 128 * i : 128 * i + 128] = hdot(side, data)
    dep_ref[:, 256:384] = jnp.zeros((rows, 128), F32)
    west_ref[0:rows, :] = pltpu.roll(dep_ref[:, 0:128], 14, 1)
    west_ref[rows : rows + corner_ref.shape[0], :] = corner_ref[...]


def own_row(
    place_ref,
    in_ref,
    filter_ref,
    lines_ref,
    slope_ref,
    to_grid_ref,
    from_grid_ref,
    out_ref,
    left_ref,
    grid_ref,
    res_ref,
    sum_ref,
):
    band, lon = place_ref[0], place_ref[1]
    pairs = in_ref[0, 0:12, :, :]
    for i in range(1, in_ref.shape[0]):
        pairs = pairs + in_ref[i, 0:12, :, :]
    for i in range(12):
        sum_ref[2 * i : 2 * i + 2, :] = pairs[i]
    sums = sum_ref[...]
    mask, keep = filter_ref[0:1, :], filter_ref[1:2, :]
    chosen = ((rank_in_row(mask) == lon) & (mask == 1)).astype(F32)

    def pick(row):
        return jnp.sum(chosen * row, axis=1, keepdims=True)

    rows = mask.shape[1]
    weight = pick(1.0 - keep)
    both = lines_ref[pl.ds(band, 1), :]
    metric = pick(both[:, 0:rows])
    rotation = pick(both[:, 128 : 128 + rows])

    def line(i):
        return sums[i : i + 1, :]

    slope = slope_ref[0:1, :]
    left_ref[...] = jnp.zeros(left_ref.shape, F32)
    pairs = (
        (weight * (line(2) - rotation * line(4)), weight * (line(3) - rotation * line(5))),
        (metric * slope * line(7), -metric * slope * line(6)),
        (weight * (line(4) + rotation * line(2)), weight * (line(5) + rotation * line(3))),
        (line(8), line(9)),
    )
    for i, (on_cos, on_sin) in enumerate(pairs):
        left_ref[i : i + 1, 0:128] = on_cos
        left_ref[i : i + 1, 128:256] = on_sin
    at = tdot(left_ref[...], to_grid_ref)
    wet = jnp.concatenate([line(16), line(17), line(18), line(19)], axis=1)
    share = (COURANT / LEVELS) * jnp.concatenate([line(20), line(21), line(22), line(23)], axis=1)
    grid_ref[...] = jnp.zeros(grid_ref.shape, F32)
    grid_ref[0:1, :] = wet * at[0:1] + share * at[1:2]
    grid_ref[1:2, :] = wet * at[2:3] + share * at[3:4]
    back = tdot(grid_ref[...], from_grid_ref)
    res_ref[0:6, :] = sums[0:6]
    res_ref[6:8, :] = sums[10:12] + sums[6:8]
    for i in range(2):
        res_ref[8 + 2 * i : 9 + 2 * i, :] = line(12 + 2 * i) + back[i : i + 1, 0:128]
        res_ref[9 + 2 * i : 10 + 2 * i, :] = line(13 + 2 * i) + back[i : i + 1, 128:256]
    for i in range(3):
        out_ref[:, i, :, :] = jnp.broadcast_to(
            res_ref[4 * i : 4 * i + 4, :][None], (out_ref.shape[0], 4, 128)
        )


def band_edges(cols, all_ref, dep_ref, edge_ref, filter_ref, coef_ref, depx_ref, north_ref, south_ref):
    half = all_ref.shape[1]
    rows = dep_ref.shape[0]
    mask = filter_ref[0:1, :]
    rank = to_col(rank_in_row(mask))
    kept = to_col(mask) == 1
    first = cols - 256
    lane = iota((rows, 128), 1)
    depx_ref[:, 0:256] = dep_ref[:, 0:256]
    depx_ref[:, 256:384] = jnp.where(
        (lane == first) | (lane == first + 1), edge_ref[0:rows, :], 0.0
    )
    chosen = [
        ((2 * iota((rows, half), 1) + c == rank) & kept).astype(F32) for c in range(2)
    ]
    for v in range(12):
        own = hdot(chosen[0], all_ref[0, :, v // 4, v % 4, :]) + hdot(
            chosen[1], all_ref[1, :, v // 4, v % 4, :]
        )
        coef_ref[v] = own
        north_ref[4 * v : 4 * v + 4, :] = own[0:4]
        south_ref[4 * v : 4 * v + 4, :] = own[rows - 4 : rows]
    for out_ref, at in ((north_ref, 0), (south_ref, rows - 2)):
        for r in range(2):
            for t in range(3):
                out_ref[48 + 3 * r + t : 49 + 3 * r + t, :] = depx_ref[
                    at + r : at + r + 1, 128 * t : 128 * t + 128
                ]
        out_ref[54:56, :] = jnp.zeros((2, 128), F32)


def own_modes(place_ref, coef_ref, cos_ref, sin_ref, table_ref, low_ref, stack_ref):
    rows = coef_ref.shape[1]
    lon = place_ref[1]
    turn_cos, turn_sin = cos_ref[pl.ds(lon, 1), :], sin_ref[pl.ds(lon, 1), :]
    for f in range(6):
        lines = slice(rows * f, rows * f + rows)
        on_cos, on_sin = coef_ref[2 * f], coef_ref[2 * f + 1]
        stack_ref[lines, 0:128] = on_cos * turn_cos + on_sin * turn_sin
        stack_ref[lines, 128:256] = on_sin * turn_cos - on_cos * turn_sin
    low_ref[...] = tdot(stack_ref[...], table_ref)


def last_stage(
    place_ref,
    wide_ref,
    left_ref,
    right_ref,
    corner_left_ref,
    corner_right_ref,
    weight_ref,
    own_ref,
    depx_ref,
    above_ref,
    below_ref,
    terms_ref,
    cos_ref,
    sin_ref,
    table_ref,
    h_ref,
    e_ref,
    n_ref,
    stack_ref,
    dep_ref,
    ext_ref,
    low_ref,
):
    ext = ext_ref.shape[1]
    rows, cols = h_ref.shape
    for f in range(4):
        ext_ref[f, :, 0:256] = wide_ref[f, :, 0:256]
        ext_ref[f, 0:rows, 256:384] = third_tile(
            wide_ref[f, 0:rows, 256:384], left_ref[...], right_ref[...], f, cols
        )
        lines = slice(2 * HALO * f, 2 * HALO * f + 2 * HALO)
        ext_ref[f, rows:ext, 256:384] = third_tile(
            wide_ref[f, rows:ext, 256:384],
            corner_left_ref[lines, :],
            corner_right_ref[rows + 2 * HALO * f : rows + 2 * HALO * f + 2 * HALO, :],
            f,
            cols,
        )
    band, lon = place_ref[0], place_ref[1]
    turn_cos, turn_sin = cos_ref[pl.ds(lon, 1), :], sin_ref[pl.ds(lon, 1), :]
    for f in range(6):
        for at, in_ref in ((8 * f, below_ref), (8 * f + 4, above_ref)):
            on_cos = in_ref[8 * f : 8 * f + 4, :]
            on_sin = in_ref[8 * f + 4 : 8 * f + 8, :]
            stack_ref[at : at + 4, 0:128] = on_cos * turn_cos + on_sin * turn_sin
            stack_ref[at : at + 4, 128:256] = on_sin * turn_cos - on_cos * turn_sin
    edges = tdot(stack_ref[...], table_ref)
    for f in range(6):
        low_ref[ext * f : ext * f + rows, :] = own_ref[rows * f : rows * f + rows, :]
        low_ref[ext * f + rows : ext * f + ext, :] = edges[8 * f : 8 * f + 8, :]
    low = low_ref
    dep_ref[0:rows, :] = depx_ref[...]
    dep_ref[rows:ext, :] = jnp.zeros((ext - rows, LANES), F32)
    for in_ref, at in ((below_ref, rows), (above_ref, ext - 2)):
        for r in range(2):
            for t in range(3):
                dep_ref[at + r : at + r + 1, 128 * t : 128 * t + 128] = in_ref[
                    48 + 3 * r + t : 49 + 3 * r + t, :
                ]
    weight = weight_ref[:, 0:1]
    metric, rotation, valid = row_terms(terms_ref[...], band)
    level = ext_ref[3]
    wet = (level > 0).astype(F32)
    share = COURANT * (level / LEVELS)

    def step(height, east, north, f):
        height = height + weight * (low[ext * f : ext * f + ext] - height)
        east = east + weight * (low[ext * f + ext : ext * f + 2 * ext] - east)
        north = north + weight * (low[ext * f + 2 * ext : ext * f + 3 * ext] - north)
        middle = valid * (height + COURANT * (metric * lon_diff(east) + lat_diff(north)))
        new_east = east - rotation * north + share * (metric * lon_diff(middle))
        new_north = north + rotation * east + share * lat_diff(middle)
        return middle, new_east, new_north

    middle, east, north = step(ext_ref[0], ext_ref[1], ext_ref[2], 0)
    middle, east, north = step(middle + dep_ref[...], wet * east, wet * north, 3)
    h_ref[...] = middle[0:rows, 0:cols]
    e_ref[...] = east[0:rows, 0:cols]
    n_ref[...] = north[0:rows, 0:cols]


def tables(length, cols, devices, rows, bands):
    mode = np.arange(MODES)
    norm = np.where(mode == 0, 1.0 / length, 2.0 / length)
    lane = np.arange(LANES)

    def angle(at, number):
        phase = (at[:, None].astype(np.int64) * number[None, :]) % length
        return phase * (2.0 * math.pi / length)

    inside = (lane < cols)[:, None]
    place = np.where(lane < LANES - HALO, lane, lane - LANES)
    shown = ((lane < cols + HALO) | (lane >= LANES - HALO))[:, None]
    around = angle(place, mode)
    analyse = np.concatenate([np.cos(around) * norm, np.sin(around) * norm], axis=1) * shown
    evaluate = (np.concatenate([np.cos(around), np.sin(around)], axis=1) * shown).T
    wide = np.arange(1, 2 * MODES - 1)
    spot = np.arange(GRID) * (length / GRID)
    gap = spot[None, :] - lane[:, None]
    kernel = np.full((LANES, GRID), 1.0 / length)
    for k in wide:
        kernel += (2.0 / length) * np.cos(2.0 * math.pi / length * k * gap)
    kernel *= inside
    coarse = (np.arange(GRID)[:, None] * mode[None, :]) % GRID * (2.0 * math.pi / GRID)
    to_grid = np.concatenate([np.cos(coarse), np.sin(coarse)], axis=1).T
    part = np.where(mode == 0, 1.0 / GRID, 2.0 / GRID)
    from_grid = np.concatenate([np.cos(coarse) * part, np.sin(coarse) * part], axis=1)
    turn = (np.arange(devices)[:, None] * mode[None, :]) % devices * (2.0 * math.pi / devices)
    slope = np.tile(np.sin(2.0 * math.pi / length * mode)[None, :], (8, 1))
    total = rows * bands
    index = np.arange(rows + 2 * HALO)
    local = np.where(index < rows + HALO, index, index - (rows + 2 * HALO))
    terms = np.zeros((rows + 2 * HALO, 128))
    lines = np.zeros((bands, 256))
    for b in range(bands):
        g = b * rows + local
        phi = (2.0 * ((g + 0.5) / total) - 1.0) * LIMIT
        terms[:, b] = 1.0 / np.cos(phi)
        terms[:, 16 + b] = ROTATION * np.sin(phi)
        terms[:, 32 + b] = (g >= 0) & (g < total)
        lines[b, 0:rows] = terms[0:rows, b]
        lines[b, 128 : 128 + rows] = terms[0:rows, 16 + b]
    made = dict(
        analyse=analyse,
        evaluate=evaluate,
        kernel=kernel,
        to_grid=to_grid,
        from_grid=from_grid,
        cos=np.cos(turn),
        sin=np.sin(turn),
        slope=slope,
        terms=terms,
        lines=lines,
    )
    for name, value in made.items():
        made[name] = value.astype(np.float32)
        if name in ("analyse", "evaluate", "kernel", "to_grid", "from_grid"):
            high = value.astype(ml_dtypes.bfloat16)
            low = (value - high.astype(np.float64)).astype(ml_dtypes.bfloat16)
            made[name] = np.stack([high, low])
    return made


VMEM = pl.BlockSpec(memory_space=pltpu.VMEM)
SMEM = pl.BlockSpec(memory_space=pltpu.SMEM)
HBM = pl.BlockSpec(memory_space=pltpu.HBM)


def call(kernel, name, outs, args, scratch=(), scalars=False, direct=(), cost=1.0):
    shapes = [jax.ShapeDtypeStruct(shape, F32) for shape in outs]
    specs = [
        SMEM if scalars and i == 0 else HBM if i in direct else VMEM for i in range(len(args))
    ]
    args = [
        pltpu.with_memory_space_constraint(arg, pltpu.HBM) if i in direct else arg
        for i, arg in enumerate(args)
    ]
    held = [pltpu.VMEM(args[i].shape, args[i].dtype) for i in direct]
    held += [pltpu.SemaphoreType.DMA((len(direct),))] if direct else []
    return pl.pallas_call(
        kernel,
        name=name,
        out_shape=shapes,
        in_specs=specs,
        out_specs=[VMEM] * len(shapes),
        scratch_shapes=held + [
            pltpu.VMEM(shape, F32) if isinstance(shape, tuple) else shape for shape in scratch
        ],
        cost_estimate=pl.CostEstimate(
            flops=int(cost * 1e9), bytes_accessed=int(cost * 2e6), transcendentals=0
        ),
        compiler_params=pltpu.CompilerParams(
            vmem_limit_bytes=40 * 2**20
        ),
    )(*args)


LON = ("z", "core")


def on_device(
    back_height,
    back_east,
    back_north,
    obs_values,
    obs_owner,
    obs_row,
    obs_count,
    polar_mask,
    keep_share,
    depth_level,
):
    rows, cols = back_height.shape
    bands, devices = lax.axis_size("band"), lax.axis_size(LON)
    half = devices // 2
    number, width = obs_values.shape
    ext = rows + 2 * HALO
    made = tables(cols * devices, cols, devices, rows, bands)
    place = jnp.stack([lax.axis_index("band"), lax.axis_index(LON)]).astype(jnp.int32)

    def send(value, axis, shift, closed):
        count = lax.axis_size(axis)
        pairs = [(i, (i + shift) % count) for i in range(count) if closed or 0 <= i + shift < count]
        return lax.ppermute(value, axis, pairs)

    fields, west, east, north, south, kept, marks = call(
        pack_tile,
        "pack_tile",
        [(4, rows, LANES), (rows, 128), (rows, 128)] + [(4 * HALO, LANES)] * 2 + [(8, rows), (8, number)],
        (
            back_height,
            back_east,
            back_north,
            depth_level,
            polar_mask.reshape(1, rows),
            keep_share.reshape(1, rows),
            obs_owner.reshape(1, number),
            obs_row.reshape(1, number),
            obs_count.reshape(1, number),
        ),
        direct=range(9),
    )
    below, above = send(north, "band", -1, False), send(south, "band", 1, False)
    right, left = send(west, LON, -1, True), send(east, LON, 1, True)
    other_core = [(i, i ^ 1) for i in range(devices)]
    near, far, values = call(
        pack_observations,
        "pack_observations",
        [(half, 32, 128), (half, 32, 128), (number, width)],
        (place, obs_values, marks),
        cost=3.0,
        scalars=True,
    )
    (placed,) = call(
        sum_observations,
        "sum_observations",
        [(devices, 256)],
        (place, values, marks, kept, made["cos"], made["sin"], made["analyse"]),
        scalars=True,
    )
    wide, weight, corner_west, corner_east, mine, other = call(
        lambda *refs: partial_sums(cols, *refs),
        "partial_sums",
        [(4, ext, LANES), (ext, 128)] + [(8 * HALO, 128)] * 2 + [(half, 56, 128)] * 2,
        (
            place,
            fields,
            left,
            right,
            above,
            below,
            kept,
            made["terms"],
            made["cos"],
            made["sin"],
            made["analyse"],
            made["kernel"],
            placed,
            near,
            far,
        ),
        scratch=[pltpu.VMEM((n * devices, LANES), jnp.bfloat16) for n in (8, 8, 2)],
        scalars=True,
    )
    swapped = lax.ppermute(other, LON, other_core)
    (joined,) = call(join, "join", [(half, 37, 2, 128)], (mine, swapped))
    owned = lax.all_to_all(joined, "z", split_axis=0, concat_axis=0, tiled=True)
    (spread,) = call(
        own_row,
        "own_row",
        [(half, 3, 4, 128)],
        (
            place,
            owned,
            kept,
            made["lines"],
            made["slope"],
            made["to_grid"],
            made["from_grid"],
        ),
        scratch=[(8, 256), (8, GRID), (12, 128), (24, 128)],
        scalars=True,
    )
    shared = lax.all_to_all(spread, "z", split_axis=0, concat_axis=0, tiled=True)
    everyone = lax.all_gather(shared, "core", axis=0, tiled=False)
    dep, west = call(
        unpack_observations,
        "unpack_observations",
        [(rows, LANES), (rows + 8 * HALO, 128)],
        (owned, corner_west),
        scratch=[(half, 48, 128)],
    )
    corner_east = lax.optimization_barrier((corner_east, spread))[0]
    corner_right, corner_left = send(west, LON, -1, True), send(corner_east, LON, 1, True)
    dep, corner_left = lax.optimization_barrier((dep, corner_left))
    coef, depx, north, south = call(
        lambda *refs: band_edges(cols, *refs),
        "band_edges",
        [(12, rows, 128), (rows, LANES), (56, 128), (56, 128)],
        (everyone, dep, corner_right, kept),
    )
    below, above = send(north, "band", -1, False), send(south, "band", 1, False)
    (own,) = call(
        own_modes,
        "own_modes",
        [(6 * rows, LANES)],
        (place, coef, made["cos"], made["sin"], made["evaluate"]),
        scratch=[(6 * rows, 256)],
        scalars=True,
    )
    return tuple(
        call(
            last_stage,
            "last_stage",
            [(rows, cols)] * 3,
            (
                place,
                wide,
                left,
                right,
                corner_left,
                corner_right,
                weight,
                own,
                depx,
                above,
                below,
                made["terms"],
                made["cos"],
                made["sin"],
                made["evaluate"],
            ),
            scratch=[(48, 256), (ext, LANES), (4, ext, LANES), (6 * ext, LANES)],
            scalars=True,
        )
    )


def solution(mesh):
    placed = (
        P("band", LON),
        P("band", LON),
        P("band", LON),
        P(("band", *LON), None),
        P(("band", *LON), None),
        P(("band", *LON)),
        P(("band", *LON)),
        P("band"),
        P("band"),
        P("band", LON),
    )
    fine = jax.sharding.Mesh(
        mesh.devices.reshape(mesh.devices.shape[0], -1, 2), ("band", *LON)
    )
    return jax.shard_map(
        on_device,
        mesh=fine,
        in_specs=placed,
        out_specs=(P("band", LON), P("band", LON), P("band", LON)),
        check_vma=False,
    )
```

```python
import math

import jax
import jax.numpy as jnp
import ml_dtypes
import numpy as np
from jax import lax
from jax.experimental import pallas as pl
from jax.experimental.pallas import tpu as pltpu
from jax.sharding import PartitionSpec as P

MODES = 128
LEVELS = 50
COURANT = 0.25
ROTATION = 0.4
LIMIT = 1.3089969389957472
CAP = 12
LANES = 384
GRID = 512
HALO = 4
F32 = jnp.float32


def hdot(left, right):
    return jnp.dot(left, right, precision=lax.Precision.HIGHEST, preferred_element_type=F32)


def halves_of(value):
    high = value.astype(jnp.bfloat16)
    return high, (value - high.astype(F32)).astype(jnp.bfloat16)


def bdot(left, right):
    return jnp.dot(left, right, preferred_element_type=F32)


def pick_dot(chosen, value):
    high, low = halves_of(value)
    rest = (value - high.astype(F32) - low.astype(F32)).astype(jnp.bfloat16)
    chosen = chosen.astype(jnp.bfloat16)
    return bdot(chosen, high) + bdot(chosen, low) + bdot(chosen, rest)


def tdot(left, table_ref):
    high, low = halves_of(left)
    return bdot(high, table_ref[0]) + bdot(low, table_ref[0]) + bdot(high, table_ref[1])


def tdot_few(left, table_ref):
    lines = left.shape[0]
    high = left.astype(jnp.bfloat16).astype(F32)
    both = jnp.concatenate([high, left - high], axis=0).astype(jnp.bfloat16)
    first = bdot(both, table_ref[0])
    return first[0:lines] + first[lines:] + bdot(left.astype(jnp.bfloat16), table_ref[1])


def mdot(left, right):
    return jnp.dot(left, right, precision=lax.Precision.HIGH, preferred_element_type=F32)


def iota(shape, dim):
    return lax.broadcasted_iota(jnp.int32, shape, dim)


def to_col(row):
    size = row.shape[1]
    same = iota((size, size), 0) == iota((size, size), 1)
    return jnp.sum(jnp.where(same, row, jnp.zeros_like(row)), axis=1, keepdims=True)


def to_row(col):
    size = col.shape[0]
    same = iota((size, size), 0) == iota((size, size), 1)
    return jnp.sum(jnp.where(same, col, jnp.zeros_like(col)), axis=0, keepdims=True)


def lon_diff(field):
    width = field.shape[1]
    return 0.5 * (pltpu.roll(field, width - 1, 1) - pltpu.roll(field, 1, 1))


def lat_diff(field):
    rows = field.shape[0]
    return 0.5 * (pltpu.roll(field, rows - 1, 0) - pltpu.roll(field, 1, 0))


def rank_in_row(mask_row):
    size = mask_row.shape[1]
    before = iota((size, size), 0) < iota((size, size), 1)
    return jnp.sum(jnp.where(before, to_col(mask_row), 0), axis=0, keepdims=True)


def slot_rows(mask_row, core, devices):
    rows = mask_row.shape[1]
    half = devices // 2
    line = iota((devices, rows), 0)
    slot = jnp.where(line < half, 2 * line + core, 2 * (line - half) + 1 - core)
    hit = (slot == rank_in_row(mask_row)) & (mask_row == 1)
    return hit.astype(F32)


WEIGHT_LANE = 300 - 256


def pack_tile(
    h_hbm,
    e_hbm,
    n_hbm,
    d_hbm,
    mask_hbm,
    keep_hbm,
    owner_hbm,
    row_hbm,
    count_hbm,
    fields_ref,
    west_ref,
    east_ref,
    north_ref,
    south_ref,
    filter_ref,
    marks_ref,
    h_ref,
    e_ref,
    n_ref,
    d_ref,
    mask_ref,
    keep_ref,
    owner_ref,
    row_ref,
    count_ref,
    sems,
):
    pairs = (
        (h_hbm, h_ref),
        (e_hbm, e_ref),
        (n_hbm, n_ref),
        (d_hbm, d_ref),
        (mask_hbm, mask_ref),
        (keep_hbm, keep_ref),
        (owner_hbm, owner_ref),
        (row_hbm, row_ref),
        (count_hbm, count_ref),
    )
    copies = [pltpu.make_async_copy(a, b, sems.at[i]) for i, (a, b) in enumerate(pairs)]
    for copy in copies:
        copy.start()
    fields_ref[...] = jnp.zeros(fields_ref.shape, F32)
    for copy in copies:
        copy.wait()
    rows, cols = h_ref.shape
    filter_ref[0:1, :] = mask_ref[...].astype(F32)
    filter_ref[1:2, :] = keep_ref[...]
    filter_ref[2:8, :] = jnp.zeros((6, rows), F32)
    for i, in_ref in enumerate((owner_ref, row_ref, count_ref)):
        marks_ref[i : i + 1, :] = in_ref[...].astype(F32)
    marks_ref[3:8, :] = jnp.zeros((5, marks_ref.shape[1]), F32)
    weight = to_col(mask_ref[...].astype(F32) * (1.0 - keep_ref[...]))
    level = d_ref[...].astype(F32)
    wet = (level > 0).astype(F32)
    values = (h_ref[...], wet * e_ref[...], wet * n_ref[...], level)
    lane = iota((rows, 128), 1)
    west = jnp.zeros(lane.shape, F32)
    east = jnp.zeros(lane.shape, F32)
    last = cols - HALO - 256
    for f, value in enumerate(values):
        fields_ref[f, :, 0:cols] = value
        inside = (lane >= HALO * f) & (lane < HALO * f + HALO)
        head = fields_ref[f, :, 0:128]
        tail = fields_ref[f, :, 256:384]
        if f:
            head = pltpu.roll(head, HALO * f, 1)
        west = jnp.where(inside, head, west)
        east = jnp.where(inside, pltpu.roll(tail, (HALO * f - last) % 128, 1), east)
        for out_ref, at in ((north_ref, 0), (south_ref, rows - HALO)):
            span = slice(at, at + HALO)
            lines = slice(HALO * f, HALO * f + HALO)
            edge = fields_ref[f, span, 256:384]
            if f == 3:
                edge = jnp.where(iota(edge.shape, 1) == WEIGHT_LANE, weight[span, :], edge)
            out_ref[lines, 0:256] = fields_ref[f, span, 0:256]
            out_ref[lines, 256:384] = edge
    west_ref[...] = west
    east_ref[...] = east


def third_tile(tail, left, right, f, cols):
    lane = iota(tail.shape, 1)
    first = cols - 256
    shifted = pltpu.roll(right, (first - HALO * f) % 128, 1)
    tail = jnp.where((lane >= first) & (lane < first + HALO), shifted, tail)
    shifted = pltpu.roll(left, (128 - HALO - HALO * f) % 128, 1)
    return jnp.where(lane >= 128 - HALO, shifted, tail)


def row_terms(terms, band):
    lane = iota(terms.shape, 1)
    return [
        jnp.sum(jnp.where(lane == band + 16 * i, terms, 0.0), axis=1, keepdims=True)
        for i in range(3)
    ]


def partial_sums(
    cols,
    place_ref,
    fields_ref,
    left_ref,
    right_ref,
    above_ref,
    below_ref,
    filter_ref,
    terms_ref,
    cos_ref,
    sin_ref,
    table_ref,
    kernel_ref,
    placed_ref,
    near_ref,
    far_ref,
    ext_ref,
    weight_ref,
    west_ref,
    east_ref,
    mine_ref,
    other_ref,
    high_ref,
    low_ref,
    cells_ref,
):
    rows = fields_ref.shape[1]
    ext = rows + 2 * HALO
    devices = cos_ref.shape[0]
    half = devices // 2
    band, lon = place_ref[0], place_ref[1]
    for f in range(4):
        ext_ref[f, 0:rows, :] = fields_ref[f]
        ext_ref[f, rows : rows + HALO, :] = below_ref[HALO * f : HALO * f + HALO, :]
        ext_ref[f, rows + HALO : ext, :] = above_ref[HALO * f : HALO * f + HALO, :]
    edge = ext_ref[3, rows:ext, 256:384]
    marked = iota(edge.shape, 1) == WEIGHT_LANE
    mask, keep = filter_ref[0:1, :], filter_ref[1:2, :]
    weight_ref[0:rows, :] = jnp.broadcast_to(to_col(mask * (1.0 - keep)), (rows, 128))
    weight_ref[rows:ext, :] = jnp.broadcast_to(
        jnp.sum(jnp.where(marked, edge, 0.0), axis=1, keepdims=True), (2 * HALO, 128)
    )
    ext_ref[3, rows:ext, 256:384] = jnp.where(marked, 0.0, edge)
    corner = iota((2 * HALO, 128), 1)
    last = cols - HALO - 256
    for f in range(4):
        lines = slice(2 * HALO * f, 2 * HALO * f + 2 * HALO)
        inside = (corner >= HALO * f) & (corner < HALO * f + HALO)
        head = ext_ref[f, rows:ext, 0:128]
        tail = ext_ref[f, rows:ext, 256:384]
        if f:
            head = pltpu.roll(head, HALO * f, 1)
        west_ref[lines, :] = jnp.where(inside, head, 0.0)
        east_ref[lines, :] = jnp.where(inside, pltpu.roll(tail, (HALO * f - last) % 128, 1), 0.0)
    weight = weight_ref[:, 0:1]
    rest = 1.0 - weight
    metric, rotation, valid = row_terms(terms_ref[...], band)
    metric = metric * valid
    height, east, north = ext_ref[0], ext_ref[1], ext_ref[2]
    ext_ref[3, 0:rows, 256:384] = third_tile(
        ext_ref[3, 0:rows, 256:384], left_ref[...], right_ref[...], 3, cols
    )
    share = ext_ref[3] / LEVELS
    low_height = weight * height + COURANT * (
        metric * lon_diff(weight * east) + lat_diff(weight * north)
    )
    low_height = valid * low_height
    east_rest, north_rest = rest * east, rest * north
    middle = valid * (
        rest * height + COURANT * (metric * lon_diff(east_rest) + lat_diff(north_rest))
    )
    new_east = east_rest - rotation * north_rest + COURANT * share * metric * lon_diff(middle)
    new_north = north_rest + rotation * east_rest + COURANT * share * lat_diff(middle)
    chosen = slot_rows(mask, place_ref[1] % 2, devices).astype(jnp.bfloat16)
    sources = (height, east, north, low_height, lat_diff(low_height), middle, new_east, new_north)
    for v, field in enumerate(sources):
        lines = slice(devices * v, devices * v + devices)
        high, low = halves_of(field[0:rows, :])
        high_ref[lines, :] = bdot(chosen, high).astype(jnp.bfloat16)
        low_ref[lines, :] = bdot(chosen, low).astype(jnp.bfloat16)
    mine_ref[:, 24:56, :] = near_ref[...]
    other_ref[:, 24:56, :] = far_ref[...]
    level = ext_ref[3, 0:rows, :]
    for c, cells in enumerate(((level > 0).astype(F32), level)):
        cells_ref[devices * c : devices * c + devices, :] = bdot(
            chosen, cells.astype(jnp.bfloat16)
        ).astype(jnp.bfloat16)
    sums = bdot(high_ref[...], table_ref[0]) + bdot(low_ref[...], table_ref[0])
    sums = sums + bdot(high_ref[...], table_ref[1])
    turn_cos, turn_sin = cos_ref[pl.ds(lon, 1), :], sin_ref[pl.ds(lon, 1), :]
    for v in range(len(sources)):
        lines = slice(devices * v, devices * v + devices)
        on_cos, on_sin = sums[lines, 0:128], sums[lines, 128:256]
        all_cos = on_cos * turn_cos - on_sin * turn_sin
        all_sin = on_sin * turn_cos + on_cos * turn_sin
        if v == 5:
            all_cos = all_cos + placed_ref[:, 0:128]
            all_sin = all_sin + placed_ref[:, 128:256]
        for i, value in enumerate((all_cos, all_sin)):
            mine_ref[:, 2 * v + i, :] = value[0:half]
            other_ref[:, 2 * v + i, :] = value[half:devices]
    spread = bdot(cells_ref[...], kernel_ref[0]) + bdot(cells_ref[...], kernel_ref[1])
    spread = pltpu.roll(spread, lon * (GRID // devices), 1)
    for c in range(2):
        for i in range(4):
            part = spread[devices * c : devices * c + devices, 128 * i : 128 * i + 128]
            at = 16 + 4 * c + i
            mine_ref[:, at, :] = part[0:half]
            other_ref[:, at, :] = part[half:devices]


def pack_observations(
    place_ref,
    values_ref,
    marks_ref,
    filter_ref,
    cos_ref,
    sin_ref,
    table_ref,
    near_ref,
    far_ref,
    placed_ref,
):
    number, width = values_ref.shape
    half = near_ref.shape[0]
    devices = 2 * half
    core = place_ref[1] % 2
    lengths = to_col(marks_ref[2:3, :])
    values = jnp.where(iota((number, width), 1).astype(F32) < lengths, values_ref[...], 0.0)
    high, low = halves_of(values)
    rest = (values - high.astype(F32) - low.astype(F32)).astype(jnp.bfloat16)
    owner_row = marks_ref[0:1, :].astype(jnp.int32)
    owner_col = to_col(owner_row)
    same = owner_col == owner_row
    before = same & (iota((number, number), 0) < iota((number, number), 1))
    arrival_row = jnp.sum(before.astype(jnp.int32), axis=0, keepdims=True)
    after = same & (iota((number, number), 0) > iota((number, number), 1))
    arrival_col = jnp.sum(after.astype(jnp.int32), axis=1, keepdims=True)
    chip_row, core_row = owner_row // 2, owner_row % 2
    target = chip_row * 16 + arrival_row
    label = marks_ref[1:2, :]
    arrived = (iota((number, 128), 1) == arrival_col).astype(F32).astype(jnp.bfloat16)
    for out_ref, side in ((near_ref, core), (far_ref, 1 - core)):
        goes = core_row == side
        sent = ((iota((16 * half, number), 0) == target) & goes).astype(F32)
        sent = sent.astype(jnp.bfloat16)
        block = bdot(sent, high) + bdot(sent, low) + bdot(sent, rest)
        block = block.reshape(half, 16, width)
        out_ref[:, 0:CAP, :] = block[:, 0:CAP, 0:128]
        out_ref[:, CAP : 2 * CAP, :] = block[:, 0:CAP, 128:256]
        named = ((iota((half, number), 0) == chip_row) & goes).astype(F32) * label
        out_ref[:, 2 * CAP : 32, :] = jnp.zeros((half, 32 - 2 * CAP, 128), F32)
        out_ref[:, 2 * CAP, :] = bdot(named.astype(jnp.bfloat16), arrived)
    head = table_ref[0, 0:width, :]
    sums = bdot(high, head) + bdot(low, head) + bdot(high, table_ref[1, 0:width, :])
    whose = (iota((number, devices), 1) == owner_col).astype(F32)
    turn_cos, turn_sin = pick_dot(whose, cos_ref[...]), pick_dot(whose, sin_ref[...])
    on_cos, on_sin = sums[:, 0:128], sums[:, 128:256]
    all_cos = on_cos * turn_cos - on_sin * turn_sin
    all_sin = on_sin * turn_cos + on_cos * turn_sin
    mask = filter_ref[0:1, :]
    rows = mask.shape[1]
    in_row = (iota((rows, number), 0).astype(F32) == label).astype(F32)
    slots = slot_rows(mask, core, devices).astype(jnp.bfloat16)
    chosen = bdot(slots, in_row.astype(jnp.bfloat16))
    placed_ref[:, 0:128] = pick_dot(chosen, all_cos)
    placed_ref[:, 128:256] = pick_dot(chosen, all_sin)


def join(mine_ref, swapped_ref, out_ref):
    for i in range(12):
        pair = slice(2 * i, 2 * i + 2)
        out_ref[:, i, :, :] = mine_ref[:, pair, :] + swapped_ref[:, pair, :]
    for i in range(12, 24):
        out_ref[:, i, :, :] = mine_ref[:, 2 * i : 2 * i + 2, :]
        out_ref[:, i + 12, :, :] = swapped_ref[:, 2 * i : 2 * i + 2, :]
    out_ref[:, 36, 0, :] = mine_ref[:, 48, :]
    out_ref[:, 36, 1, :] = swapped_ref[:, 48, :]


def unpack_observations(in_ref, corner_ref, dep_ref, west_ref, data_ref):
    half = in_ref.shape[0]
    rows = dep_ref.shape[0]
    lines = 4 * CAP
    total = half * lines
    spot = iota((128, total), 1) % lines
    label_row = jnp.zeros((1, total), F32)
    own = iota((half, total), 1) // lines == iota((half, total), 0)
    for s in range(2):
        here = (spot // (2 * CAP) == s) & (spot % CAP == iota((128, total), 0))
        across = bdot(
            in_ref[:, 36, s, :].astype(jnp.bfloat16), here.astype(F32).astype(jnp.bfloat16)
        )
        label_row = label_row + jnp.sum(jnp.where(own, across, 0.0), axis=0, keepdims=True)
    line = iota((rows, total), 1) % lines
    hit = iota((rows, total), 0).astype(F32) == label_row
    for i in range(2 * CAP):
        data_ref[:, 2 * i : 2 * i + 2, :] = in_ref[:, 12 + i, :, :]
    data = data_ref[...].reshape(total, 128)
    for i in range(2):
        side = (hit & ((line // CAP) % 2 == i)).astype(F32)
        dep_ref[:, 128 * i : 128 * i + 128] = pick_dot(side, data)
    dep_ref[:, 256:384] = jnp.zeros((rows, 128), F32)
    west_ref[0:rows, :] = pltpu.roll(dep_ref[:, 0:128], 14, 1)
    west_ref[rows : rows + corner_ref.shape[0], :] = corner_ref[...]


def own_row(
    place_ref,
    in_ref,
    filter_ref,
    lines_ref,
    slope_ref,
    to_grid_ref,
    from_grid_ref,
    out_ref,
    left_ref,
    grid_ref,
    res_ref,
    sum_ref,
):
    band, lon = place_ref[0], place_ref[1]
    pairs = in_ref[0, 0:12, :, :]
    for i in range(1, in_ref.shape[0]):
        pairs = pairs + in_ref[i, 0:12, :, :]
    for i in range(12):
        sum_ref[2 * i : 2 * i + 2, :] = pairs[i]
    sums = sum_ref[...]
    mask, keep = filter_ref[0:1, :], filter_ref[1:2, :]
    chosen = ((rank_in_row(mask) == lon) & (mask == 1)).astype(F32)

    def pick(row):
        return jnp.sum(chosen * row, axis=1, keepdims=True)

    rows = mask.shape[1]
    weight = pick(1.0 - keep)
    both = lines_ref[pl.ds(band, 1), :]
    metric = pick(both[:, 0:rows])
    rotation = pick(both[:, 128 : 128 + rows])

    def line(i):
        return sums[i : i + 1, :]

    slope = slope_ref[0:1, :]
    left_ref[...] = jnp.zeros(left_ref.shape, F32)
    pairs = (
        (weight * (line(2) - rotation * line(4)), weight * (line(3) - rotation * line(5))),
        (metric * slope * line(7), -metric * slope * line(6)),
        (weight * (line(4) + rotation * line(2)), weight * (line(5) + rotation * line(3))),
        (line(8), line(9)),
    )
    for i, (on_cos, on_sin) in enumerate(pairs):
        left_ref[i : i + 1, 0:128] = on_cos
        left_ref[i : i + 1, 128:256] = on_sin
    at = tdot_few(left_ref[...], to_grid_ref)
    wet = jnp.concatenate([line(16), line(17), line(18), line(19)], axis=1)
    share = (COURANT / LEVELS) * jnp.concatenate([line(20), line(21), line(22), line(23)], axis=1)
    grid_ref[...] = jnp.zeros(grid_ref.shape, F32)
    grid_ref[0:1, :] = wet * at[0:1] + share * at[1:2]
    grid_ref[1:2, :] = wet * at[2:3] + share * at[3:4]
    back = tdot_few(grid_ref[...], from_grid_ref)
    res_ref[0:6, :] = sums[0:6]
    res_ref[6:8, :] = sums[10:12] + sums[6:8]
    for i in range(2):
        res_ref[8 + 2 * i : 9 + 2 * i, :] = line(12 + 2 * i) + back[i : i + 1, 0:128]
        res_ref[9 + 2 * i : 10 + 2 * i, :] = line(13 + 2 * i) + back[i : i + 1, 128:256]
    for i in range(3):
        out_ref[:, i, :, :] = jnp.broadcast_to(
            res_ref[4 * i : 4 * i + 4, :][None], (out_ref.shape[0], 4, 128)
        )


def slots_to_rows(all_ref, mask, at):
    half = all_ref.shape[1]
    lines = at.shape[0]
    here = iota((lines, mask.shape[1]), 1) == at
    rank = jnp.sum(
        jnp.where(here & (mask == 1), rank_in_row(mask) + 1.0, 0.0), axis=1, keepdims=True
    )
    total = jnp.zeros((lines, 12 * 128), F32)
    for c in range(2):
        chosen = (2 * iota((lines, half), 1) + c + 1).astype(F32) == rank
        every = [all_ref[c, :, v // 4, v % 4, :] for v in range(12)]
        total = total + pick_dot(chosen.astype(F32), jnp.concatenate(every, axis=1))
    return total


def band_edges(cols, all_ref, dep_ref, edge_ref, filter_ref, depx_ref, north_ref, south_ref):
    rows = dep_ref.shape[0]
    mask = filter_ref[0:1, :]
    first = cols - 256
    lane = iota((rows, 128), 1)
    depx_ref[:, 0:256] = dep_ref[:, 0:256]
    depx_ref[:, 256:384] = jnp.where(
        (lane == first) | (lane == first + 1), edge_ref[0:rows, :], 0.0
    )
    line = iota((8, 1), 0)
    ends = slots_to_rows(all_ref, mask, jnp.where(line < 4, line, line + (rows - 8)))
    for v in range(12):
        own = ends[:, 128 * v : 128 * v + 128]
        north_ref[4 * v : 4 * v + 4, :] = own[0:4]
        south_ref[4 * v : 4 * v + 4, :] = own[4:8]
    for out_ref, at in ((north_ref, 0), (south_ref, rows - 2)):
        for r in range(2):
            for t in range(3):
                out_ref[48 + 3 * r + t : 49 + 3 * r + t, :] = depx_ref[
                    at + r : at + r + 1, 128 * t : 128 * t + 128
                ]
        out_ref[54:56, :] = jnp.zeros((2, 128), F32)


EDGE = 16
SURE = 8


def two_steps(fields, low, weight, terms, dep):
    metric, rotation, valid = terms
    level = fields[3]
    wet = (level > 0).astype(F32)
    share = COURANT * (level / LEVELS)

    def half_step(height, east, north, f):
        height = height + weight * (low[f] - height)
        east = east + weight * (low[f + 1] - east)
        north = north + weight * (low[f + 2] - north)
        middle = valid * (height + COURANT * (metric * lon_diff(east) + lat_diff(north)))
        new_east = east - rotation * north + share * (metric * lon_diff(middle))
        new_north = north + rotation * east + share * lat_diff(middle)
        return middle, new_east, new_north

    middle, east, north = half_step(fields[0], fields[1], fields[2], 0)
    return half_step(middle + dep, wet * east, wet * north, 3)


def own_rows(
    cols,
    place_ref,
    all_ref,
    filter_ref,
    cos_ref,
    sin_ref,
    table_ref,
    wide_ref,
    left_ref,
    right_ref,
    weight_ref,
    depx_ref,
    terms_ref,
    low_ref,
    inner_ref,
    stack_ref,
    ext_ref,
):
    mask = filter_ref[0:1, :]
    rows = mask.shape[1]
    band, lon = place_ref[0], place_ref[1]
    turn_cos, turn_sin = cos_ref[pl.ds(lon, 1), :], sin_ref[pl.ds(lon, 1), :]
    coef = slots_to_rows(all_ref, mask, iota((rows, 1), 0))
    for f in range(6):
        lines = slice(rows * f, rows * f + rows)
        on_cos = coef[:, 256 * f : 256 * f + 128]
        on_sin = coef[:, 256 * f + 128 : 256 * f + 256]
        stack_ref[lines, 0:128] = on_cos * turn_cos + on_sin * turn_sin
        stack_ref[lines, 128:256] = on_sin * turn_cos - on_cos * turn_sin
    low_ref[...] = tdot(stack_ref[...], table_ref)
    for f in range(4):
        ext_ref[f, :, 0:256] = wide_ref[f, 0:rows, 0:256]
        ext_ref[f, :, 256:384] = third_tile(
            wide_ref[f, 0:rows, 256:384], left_ref[...], right_ref[...], f, cols
        )
    state = two_steps(
        [ext_ref[f] for f in range(4)],
        [low_ref[rows * f : rows * f + rows, :] for f in range(6)],
        weight_ref[0:rows, 0:1],
        row_terms(terms_ref[0:rows, :], band),
        depx_ref[...],
    )
    for i in range(3):
        inner_ref[i] = state[i][SURE : rows - SURE]


def last_stage(
    place_ref,
    wide_ref,
    left_ref,
    right_ref,
    corner_left_ref,
    corner_right_ref,
    weight_ref,
    own_ref,
    inner_ref,
    depx_ref,
    above_ref,
    below_ref,
    terms_ref,
    cos_ref,
    sin_ref,
    table_ref,
    h_hbm,
    e_hbm,
    n_hbm,
    stack_ref,
    dep_ref,
    ext_ref,
    h_ref,
    e_ref,
    n_ref,
    sems,
):
    rows, cols = h_ref.shape
    ext = rows + 2 * HALO
    band, lon = place_ref[0], place_ref[1]
    pairs = ((h_ref, h_hbm), (e_ref, e_hbm), (n_ref, n_hbm))
    spans = (pl.ds(SURE, rows - 2 * SURE), pl.ds(0, SURE), pl.ds(rows - SURE, SURE))
    copies = [
        [
            pltpu.make_async_copy(a.at[span, :], b.at[span, :], sems.at[i, j])
            for j, span in enumerate(spans)
        ]
        for i, (a, b) in enumerate(pairs)
    ]
    for i, (out_ref, _) in enumerate(pairs):
        out_ref[SURE : rows - SURE, :] = inner_ref[i, :, 0:cols]
        copies[i][0].start()
    for f in range(4):
        parts = (
            (slice(0, EDGE), slice(rows - EDGE, rows)),
            (slice(EDGE + 2 * HALO, 2 * EDGE + 2 * HALO), slice(0, EDGE)),
        )
        for to, at in parts:
            ext_ref[f, to, 0:256] = wide_ref[f, at, 0:256]
            ext_ref[f, to, 256:384] = third_tile(
                wide_ref[f, at, 256:384], left_ref[at, :], right_ref[at, :], f, cols
            )
        to = slice(EDGE, EDGE + 2 * HALO)
        lines = slice(2 * HALO * f, 2 * HALO * f + 2 * HALO)
        ext_ref[f, to, 0:256] = wide_ref[f, rows:ext, 0:256]
        ext_ref[f, to, 256:384] = third_tile(
            wide_ref[f, rows:ext, 256:384],
            corner_left_ref[lines, :],
            corner_right_ref[rows + 2 * HALO * f : rows + 2 * HALO * f + 2 * HALO, :],
            f,
            cols,
        )
    turn_cos, turn_sin = cos_ref[pl.ds(lon, 1), :], sin_ref[pl.ds(lon, 1), :]
    for f in range(6):
        for at, in_ref in ((8 * f, below_ref), (8 * f + 4, above_ref)):
            on_cos = in_ref[8 * f : 8 * f + 4, :]
            on_sin = in_ref[8 * f + 4 : 8 * f + 8, :]
            stack_ref[at : at + 4, 0:128] = on_cos * turn_cos + on_sin * turn_sin
            stack_ref[at : at + 4, 128:256] = on_sin * turn_cos - on_cos * turn_sin
    edges = tdot(stack_ref[...], table_ref)
    low = [
        jnp.concatenate(
            [
                own_ref[rows * f + rows - EDGE : rows * f + rows, :],
                edges[8 * f : 8 * f + 8, :],
                own_ref[rows * f : rows * f + EDGE, :],
            ],
            axis=0,
        )
        for f in range(6)
    ]
    dep_ref[0:EDGE, :] = depx_ref[rows - EDGE : rows, :]
    dep_ref[EDGE : EDGE + 2 * HALO, :] = jnp.zeros((2 * HALO, LANES), F32)
    dep_ref[EDGE + 2 * HALO : 2 * EDGE + 2 * HALO, :] = depx_ref[0:EDGE, :]
    for in_ref, at in ((below_ref, EDGE), (above_ref, EDGE + 2 * HALO - 2)):
        for r in range(2):
            for t in range(3):
                dep_ref[at + r : at + r + 1, 128 * t : 128 * t + 128] = in_ref[
                    48 + 3 * r + t : 49 + 3 * r + t, :
                ]

    def around(ref):
        return jnp.concatenate([ref[rows - EDGE : ext, :], ref[0:EDGE, :]], axis=0)

    state = two_steps(
        [ext_ref[f] for f in range(4)],
        low,
        around(weight_ref)[:, 0:1],
        row_terms(around(terms_ref), band),
        dep_ref[...],
    )
    south, north = slice(EDGE - SURE, EDGE), slice(EDGE + 2 * HALO, EDGE + 2 * HALO + SURE)
    for i, (out_ref, _) in enumerate(pairs):
        out_ref[0:SURE, :] = state[i][north, 0:cols]
        out_ref[rows - SURE : rows, :] = state[i][south, 0:cols]
        copies[i][1].start()
        copies[i][2].start()
    for group in copies:
        for copy in group:
            copy.wait()


def tables(length, cols, devices, rows, bands):
    mode = np.arange(MODES)
    norm = np.where(mode == 0, 1.0 / length, 2.0 / length)
    lane = np.arange(LANES)

    def angle(at, number):
        phase = (at[:, None].astype(np.int64) * number[None, :]) % length
        return phase * (2.0 * math.pi / length)

    inside = (lane < cols)[:, None]
    place = np.where(lane < LANES - HALO, lane, lane - LANES)
    shown = ((lane < cols + HALO) | (lane >= LANES - HALO))[:, None]
    around = angle(place, mode)
    analyse = np.concatenate([np.cos(around) * norm, np.sin(around) * norm], axis=1) * shown
    evaluate = (np.concatenate([np.cos(around), np.sin(around)], axis=1) * shown).T
    wide = np.arange(1, 2 * MODES - 1)
    spot = np.arange(GRID) * (length / GRID)
    gap = spot[None, :] - lane[:, None]
    kernel = np.full((LANES, GRID), 1.0 / length)
    for k in wide:
        kernel += (2.0 / length) * np.cos(2.0 * math.pi / length * k * gap)
    kernel *= inside
    coarse = (np.arange(GRID)[:, None] * mode[None, :]) % GRID * (2.0 * math.pi / GRID)
    to_grid = np.concatenate([np.cos(coarse), np.sin(coarse)], axis=1).T
    part = np.where(mode == 0, 1.0 / GRID, 2.0 / GRID)
    from_grid = np.concatenate([np.cos(coarse) * part, np.sin(coarse) * part], axis=1)
    turn = (np.arange(devices)[:, None] * mode[None, :]) % devices * (2.0 * math.pi / devices)
    slope = np.tile(np.sin(2.0 * math.pi / length * mode)[None, :], (8, 1))
    total = rows * bands
    index = np.arange(rows + 2 * HALO)
    local = np.where(index < rows + HALO, index, index - (rows + 2 * HALO))
    terms = np.zeros((rows + 2 * HALO, 128))
    lines = np.zeros((bands, 256))
    for b in range(bands):
        g = b * rows + local
        phi = (2.0 * ((g + 0.5) / total) - 1.0) * LIMIT
        terms[:, b] = 1.0 / np.cos(phi)
        terms[:, 16 + b] = ROTATION * np.sin(phi)
        terms[:, 32 + b] = (g >= 0) & (g < total)
        lines[b, 0:rows] = terms[0:rows, b]
        lines[b, 128 : 128 + rows] = terms[0:rows, 16 + b]
    made = dict(
        analyse=analyse,
        evaluate=evaluate,
        kernel=kernel,
        to_grid=to_grid,
        from_grid=from_grid,
        cos=np.cos(turn),
        sin=np.sin(turn),
        slope=slope,
        terms=terms,
        lines=lines,
    )
    for name, value in made.items():
        made[name] = value.astype(np.float32)
        if name in ("analyse", "evaluate", "kernel", "to_grid", "from_grid"):
            high = value.astype(ml_dtypes.bfloat16)
            low = (value - high.astype(np.float64)).astype(ml_dtypes.bfloat16)
            made[name] = np.stack([high, low])
    return made


VMEM = pl.BlockSpec(memory_space=pltpu.VMEM)
SMEM = pl.BlockSpec(memory_space=pltpu.SMEM)
HBM = pl.BlockSpec(memory_space=pltpu.HBM)


def call(kernel, name, outs, args, scratch=(), scalars=False, direct=(), cost=1.0, outside=False):
    shapes = [jax.ShapeDtypeStruct(shape, F32) for shape in outs]
    specs = [
        SMEM if scalars and i == 0 else HBM if i in direct else VMEM for i in range(len(args))
    ]
    args = [
        pltpu.with_memory_space_constraint(arg, pltpu.HBM) if i in direct else arg
        for i, arg in enumerate(args)
    ]
    held = [pltpu.VMEM(args[i].shape, args[i].dtype) for i in direct]
    held += [pltpu.SemaphoreType.DMA((len(direct),))] if direct else []
    return pl.pallas_call(
        kernel,
        name=name,
        out_shape=shapes,
        in_specs=specs,
        out_specs=[HBM if outside else VMEM] * len(shapes),
        scratch_shapes=held + [
            pltpu.VMEM(shape, F32) if isinstance(shape, tuple) else shape for shape in scratch
        ],
        cost_estimate=pl.CostEstimate(
            flops=int(cost * 1e9), bytes_accessed=int(cost * 2e6), transcendentals=0
        ),
        compiler_params=pltpu.CompilerParams(
            vmem_limit_bytes=40 * 2**20
        ),
    )(*args)


LON = ("z", "core")


def on_device(
    back_height,
    back_east,
    back_north,
    obs_values,
    obs_owner,
    obs_row,
    obs_count,
    polar_mask,
    keep_share,
    depth_level,
):
    rows, cols = back_height.shape
    bands, devices = lax.axis_size("band"), lax.axis_size(LON)
    half = devices // 2
    number, width = obs_values.shape
    ext = rows + 2 * HALO
    made = tables(cols * devices, cols, devices, rows, bands)
    place = jnp.stack([lax.axis_index("band"), lax.axis_index(LON)]).astype(jnp.int32)

    def send(value, axis, shift, closed):
        count = lax.axis_size(axis)
        pairs = [(i, (i + shift) % count) for i in range(count) if closed or 0 <= i + shift < count]
        return lax.ppermute(value, axis, pairs)

    fields, west, east, north, south, kept, marks = call(
        pack_tile,
        "pack_tile",
        [(4, rows, LANES), (rows, 128), (rows, 128)] + [(4 * HALO, LANES)] * 2 + [(8, rows), (8, number)],
        (
            back_height,
            back_east,
            back_north,
            depth_level,
            polar_mask.reshape(1, rows),
            keep_share.reshape(1, rows),
            obs_owner.reshape(1, number),
            obs_row.reshape(1, number),
            obs_count.reshape(1, number),
        ),
        direct=range(9),
    )
    below, above = send(north, "band", -1, False), send(south, "band", 1, False)
    right, left = send(west, LON, -1, True), send(east, LON, 1, True)
    other_core = [(i, i ^ 1) for i in range(devices)]
    near, far, placed = call(
        pack_observations,
        "pack_observations",
        [(half, 32, 128), (half, 32, 128), (devices, 256)],
        (place, obs_values, marks, kept, made["cos"], made["sin"], made["analyse"]),
        cost=3.0,
        scalars=True,
    )
    wide, weight, corner_west, corner_east, mine, other = call(
        lambda *refs: partial_sums(cols, *refs),
        "partial_sums",
        [(4, ext, LANES), (ext, 128)] + [(8 * HALO, 128)] * 2 + [(half, 56, 128)] * 2,
        (
            place,
            fields,
            left,
            right,
            above,
            below,
            kept,
            made["terms"],
            made["cos"],
            made["sin"],
            made["analyse"],
            made["kernel"],
            placed,
            near,
            far,
        ),
        scratch=[pltpu.VMEM((n * devices, LANES), jnp.bfloat16) for n in (8, 8, 2)],
        scalars=True,
    )
    swapped = lax.ppermute(other, LON, other_core)
    (joined,) = call(join, "join", [(half, 37, 2, 128)], (mine, swapped))
    owned = lax.all_to_all(joined, "z", split_axis=0, concat_axis=0, tiled=True)
    (spread,) = call(
        own_row,
        "own_row",
        [(half, 3, 4, 128)],
        (
            place,
            owned,
            kept,
            made["lines"],
            made["slope"],
            made["to_grid"],
            made["from_grid"],
        ),
        scratch=[(8, 256), (8, GRID), (12, 128), (24, 128)],
        scalars=True,
    )
    shared = lax.all_to_all(spread, "z", split_axis=0, concat_axis=0, tiled=True)
    everyone = lax.all_gather(shared, "core", axis=0, tiled=False)
    dep, west = call(
        unpack_observations,
        "unpack_observations",
        [(rows, LANES), (rows + 8 * HALO, 128)],
        (owned, corner_west),
        scratch=[(half, 48, 128)],
    )
    corner_east = lax.optimization_barrier((corner_east, spread))[0]
    corner_right, corner_left = send(west, LON, -1, True), send(corner_east, LON, 1, True)
    dep, corner_left = lax.optimization_barrier((dep, corner_left))
    depx, north, south = call(
        lambda *refs: band_edges(cols, *refs),
        "band_edges",
        [(rows, LANES), (56, 128), (56, 128)],
        (everyone, dep, corner_right, kept),
    )
    below, above = send(north, "band", -1, False), send(south, "band", 1, False)
    own, inner = call(
        lambda *refs: own_rows(cols, *refs),
        "own_rows",
        [(6 * rows, LANES), (3, rows - 2 * SURE, LANES)],
        (
            place,
            everyone,
            kept,
            made["cos"],
            made["sin"],
            made["evaluate"],
            wide,
            left,
            right,
            weight,
            depx,
            made["terms"],
        ),
        scratch=[(6 * rows, 256), (4, rows, LANES)],
        scalars=True,
    )
    edge = 2 * EDGE + 2 * HALO
    return tuple(
        call(
            last_stage,
            "last_stage",
            [(rows, cols)] * 3,
            (
                place,
                wide,
                left,
                right,
                corner_left,
                corner_right,
                weight,
                own,
                inner,
                depx,
                above,
                below,
                made["terms"],
                made["cos"],
                made["sin"],
                made["evaluate"],
            ),
            scratch=[(48, 256), (edge, LANES), (4, edge, LANES)]
            + [(rows, cols)] * 3
            + [pltpu.SemaphoreType.DMA((3, 3))],
            outside=True,
            scalars=True,
        )
    )


def solution(mesh):
    placed = (
        P("band", LON),
        P("band", LON),
        P("band", LON),
        P(("band", *LON), None),
        P(("band", *LON), None),
        P(("band", *LON)),
        P(("band", *LON)),
        P("band"),
        P("band"),
        P("band", LON),
    )
    fine = jax.sharding.Mesh(
        mesh.devices.reshape(mesh.devices.shape[0], -1, 2), ("band", *LON)
    )
    return jax.shard_map(
        on_device,
        mesh=fine,
        in_specs=placed,
        out_specs=(P("band", LON), P("band", LON), P("band", LON)),
        check_vma=False,
    )
```

```python
import math

import jax
import jax.numpy as jnp
import ml_dtypes
import numpy as np
from jax import lax
from jax.experimental import pallas as pl
from jax.experimental.pallas import tpu as pltpu
from jax.sharding import PartitionSpec as P

MODES = 128
LEVELS = 50
COURANT = 0.25
ROTATION = 0.4
LIMIT = 1.3089969389957472
CAP = 12
LANES = 384
GRID = 512
HALO = 4
F32 = jnp.float32


def hdot(left, right):
    return jnp.dot(left, right, precision=lax.Precision.HIGHEST, preferred_element_type=F32)


def halves_of(value):
    high = value.astype(jnp.bfloat16)
    return high, (value - high.astype(F32)).astype(jnp.bfloat16)


def bdot(left, right):
    return jnp.dot(left, right, preferred_element_type=F32)


def pick_dot(chosen, value):
    high, low = halves_of(value)
    rest = (value - high.astype(F32) - low.astype(F32)).astype(jnp.bfloat16)
    chosen = chosen.astype(jnp.bfloat16)
    return bdot(chosen, high) + bdot(chosen, low) + bdot(chosen, rest)


def tdot(left, table_ref):
    high, low = halves_of(left)
    return bdot(high, table_ref[0]) + bdot(low, table_ref[0]) + bdot(high, table_ref[1])


def tdot_few(left, table_ref):
    lines = left.shape[0]
    high = left.astype(jnp.bfloat16).astype(F32)
    both = jnp.concatenate([high, left - high], axis=0).astype(jnp.bfloat16)
    first = bdot(both, table_ref[0])
    return first[0:lines] + first[lines:] + bdot(left.astype(jnp.bfloat16), table_ref[1])


def mdot(left, right):
    return jnp.dot(left, right, precision=lax.Precision.HIGH, preferred_element_type=F32)


def iota(shape, dim):
    return lax.broadcasted_iota(jnp.int32, shape, dim)


def own_place():
    return lax.axis_index("band"), 2 * lax.axis_index("z") + lax.axis_index("core")


def to_col(row):
    size = row.shape[1]
    same = iota((size, size), 0) == iota((size, size), 1)
    return jnp.sum(jnp.where(same, row, jnp.zeros_like(row)), axis=1, keepdims=True)


def to_row(col):
    size = col.shape[0]
    same = iota((size, size), 0) == iota((size, size), 1)
    return jnp.sum(jnp.where(same, col, jnp.zeros_like(col)), axis=0, keepdims=True)


def lon_diff(field):
    width = field.shape[1]
    return 0.5 * (pltpu.roll(field, width - 1, 1) - pltpu.roll(field, 1, 1))


def lat_diff(field):
    rows = field.shape[0]
    return 0.5 * (pltpu.roll(field, rows - 1, 0) - pltpu.roll(field, 1, 0))


def rank_in_row(mask_row):
    size = mask_row.shape[1]
    before = iota((size, size), 0) < iota((size, size), 1)
    return jnp.sum(jnp.where(before, to_col(mask_row), 0), axis=0, keepdims=True)


def slot_rows(mask_row, core, devices):
    rows = mask_row.shape[1]
    half = devices // 2
    line = iota((devices, rows), 0)
    slot = jnp.where(line < half, 2 * line + core, 2 * (line - half) + 1 - core)
    hit = (slot == rank_in_row(mask_row)) & (mask_row == 1)
    return hit.astype(F32)


WEIGHT_LANE = 300 - 256


def pack_tile(
    h_hbm,
    e_hbm,
    n_hbm,
    d_hbm,
    mask_hbm,
    keep_hbm,
    owner_hbm,
    row_hbm,
    count_hbm,
    fields_ref,
    west_ref,
    east_ref,
    north_ref,
    south_ref,
    filter_ref,
    marks_ref,
    h_ref,
    e_ref,
    n_ref,
    d_ref,
    mask_ref,
    keep_ref,
    owner_ref,
    row_ref,
    count_ref,
    sems,
):
    pairs = (
        (h_hbm, h_ref),
        (e_hbm, e_ref),
        (n_hbm, n_ref),
        (d_hbm, d_ref),
        (mask_hbm, mask_ref),
        (keep_hbm, keep_ref),
        (owner_hbm, owner_ref),
        (row_hbm, row_ref),
        (count_hbm, count_ref),
    )
    copies = [pltpu.make_async_copy(a, b, sems.at[i]) for i, (a, b) in enumerate(pairs)]
    for copy in copies:
        copy.start()
    fields_ref[...] = jnp.zeros(fields_ref.shape, F32)
    for copy in copies:
        copy.wait()
    rows, cols = h_ref.shape
    filter_ref[0:1, :] = mask_ref[...].astype(F32)
    filter_ref[1:2, :] = keep_ref[...]
    filter_ref[2:8, :] = jnp.zeros((6, rows), F32)
    for i, in_ref in enumerate((owner_ref, row_ref, count_ref)):
        marks_ref[i : i + 1, :] = in_ref[...].astype(F32)
    marks_ref[3:8, :] = jnp.zeros((5, marks_ref.shape[1]), F32)
    weight = to_col(mask_ref[...].astype(F32) * (1.0 - keep_ref[...]))
    level = d_ref[...].astype(F32)
    wet = (level > 0).astype(F32)
    values = (h_ref[...], wet * e_ref[...], wet * n_ref[...], level)
    lane = iota((rows, 128), 1)
    west = jnp.zeros(lane.shape, F32)
    east = jnp.zeros(lane.shape, F32)
    last = cols - HALO - 256
    for f, value in enumerate(values):
        fields_ref[f, :, 0:cols] = value
        inside = (lane >= HALO * f) & (lane < HALO * f + HALO)
        head = fields_ref[f, :, 0:128]
        tail = fields_ref[f, :, 256:384]
        if f:
            head = pltpu.roll(head, HALO * f, 1)
        west = jnp.where(inside, head, west)
        east = jnp.where(inside, pltpu.roll(tail, (HALO * f - last) % 128, 1), east)
        for out_ref, at in ((north_ref, 0), (south_ref, rows - HALO)):
            span = slice(at, at + HALO)
            lines = slice(HALO * f, HALO * f + HALO)
            edge = fields_ref[f, span, 256:384]
            if f == 3:
                edge = jnp.where(iota(edge.shape, 1) == WEIGHT_LANE, weight[span, :], edge)
            out_ref[lines, 0:256] = fields_ref[f, span, 0:256]
            out_ref[lines, 256:384] = edge
    west_ref[...] = west
    east_ref[...] = east


def third_tile(tail, left, right, f, cols):
    lane = iota(tail.shape, 1)
    first = cols - 256
    shifted = pltpu.roll(right, (first - HALO * f) % 128, 1)
    tail = jnp.where((lane >= first) & (lane < first + HALO), shifted, tail)
    shifted = pltpu.roll(left, (128 - HALO - HALO * f) % 128, 1)
    return jnp.where(lane >= 128 - HALO, shifted, tail)


def row_terms(terms, band):
    lane = iota(terms.shape, 1)
    return [
        jnp.sum(jnp.where(lane == band + 16 * i, terms, 0.0), axis=1, keepdims=True)
        for i in range(3)
    ]


def partial_sums(
    cols,
    fields_ref,
    left_ref,
    right_ref,
    above_ref,
    below_ref,
    filter_ref,
    terms_ref,
    cos_ref,
    sin_ref,
    table_ref,
    kernel_ref,
    placed_ref,
    near_ref,
    far_ref,
    ext_ref,
    weight_ref,
    west_ref,
    east_ref,
    mine_ref,
    other_ref,
    high_ref,
    low_ref,
    cells_ref,
):
    rows = fields_ref.shape[1]
    ext = rows + 2 * HALO
    devices = cos_ref.shape[0]
    half = devices // 2
    band, lon = own_place()
    for f in range(4):
        ext_ref[f, 0:rows, :] = fields_ref[f]
        ext_ref[f, rows : rows + HALO, :] = below_ref[HALO * f : HALO * f + HALO, :]
        ext_ref[f, rows + HALO : ext, :] = above_ref[HALO * f : HALO * f + HALO, :]
    edge = ext_ref[3, rows:ext, 256:384]
    marked = iota(edge.shape, 1) == WEIGHT_LANE
    mask, keep = filter_ref[0:1, :], filter_ref[1:2, :]
    weight_ref[0:rows, :] = jnp.broadcast_to(to_col(mask * (1.0 - keep)), (rows, 128))
    weight_ref[rows:ext, :] = jnp.broadcast_to(
        jnp.sum(jnp.where(marked, edge, 0.0), axis=1, keepdims=True), (2 * HALO, 128)
    )
    ext_ref[3, rows:ext, 256:384] = jnp.where(marked, 0.0, edge)
    corner = iota((2 * HALO, 128), 1)
    last = cols - HALO - 256
    for f in range(4):
        lines = slice(2 * HALO * f, 2 * HALO * f + 2 * HALO)
        inside = (corner >= HALO * f) & (corner < HALO * f + HALO)
        head = ext_ref[f, rows:ext, 0:128]
        tail = ext_ref[f, rows:ext, 256:384]
        if f:
            head = pltpu.roll(head, HALO * f, 1)
        west_ref[lines, :] = jnp.where(inside, head, 0.0)
        east_ref[lines, :] = jnp.where(inside, pltpu.roll(tail, (HALO * f - last) % 128, 1), 0.0)
    weight = weight_ref[:, 0:1]
    rest = 1.0 - weight
    metric, rotation, valid = row_terms(terms_ref[...], band)
    metric = metric * valid
    height, east, north = ext_ref[0], ext_ref[1], ext_ref[2]
    ext_ref[3, 0:rows, 256:384] = third_tile(
        ext_ref[3, 0:rows, 256:384], left_ref[...], right_ref[...], 3, cols
    )
    share = ext_ref[3] / LEVELS
    low_height = weight * height + COURANT * (
        metric * lon_diff(weight * east) + lat_diff(weight * north)
    )
    low_height = valid * low_height
    east_rest, north_rest = rest * east, rest * north
    middle = valid * (
        rest * height + COURANT * (metric * lon_diff(east_rest) + lat_diff(north_rest))
    )
    new_east = east_rest - rotation * north_rest + COURANT * share * metric * lon_diff(middle)
    new_north = north_rest + rotation * east_rest + COURANT * share * lat_diff(middle)
    chosen = slot_rows(mask, own_place()[1] % 2, devices).astype(jnp.bfloat16)
    sources = (height, east, north, low_height, lat_diff(low_height), middle, new_east, new_north)
    for v, field in enumerate(sources):
        lines = slice(devices * v, devices * v + devices)
        high, low = halves_of(field[0:rows, :])
        high_ref[lines, :] = bdot(chosen, high).astype(jnp.bfloat16)
        low_ref[lines, :] = bdot(chosen, low).astype(jnp.bfloat16)
    mine_ref[:, 24:56, :] = near_ref[...]
    other_ref[:, 24:56, :] = far_ref[...]
    level = ext_ref[3, 0:rows, :]
    for c, cells in enumerate(((level > 0).astype(F32), level)):
        cells_ref[devices * c : devices * c + devices, :] = bdot(
            chosen, cells.astype(jnp.bfloat16)
        ).astype(jnp.bfloat16)
    sums = bdot(high_ref[...], table_ref[0]) + bdot(low_ref[...], table_ref[0])
    sums = sums + bdot(high_ref[...], table_ref[1])
    turn_cos, turn_sin = cos_ref[pl.ds(lon, 1), :], sin_ref[pl.ds(lon, 1), :]
    for v in range(len(sources)):
        lines = slice(devices * v, devices * v + devices)
        on_cos, on_sin = sums[lines, 0:128], sums[lines, 128:256]
        all_cos = on_cos * turn_cos - on_sin * turn_sin
        all_sin = on_sin * turn_cos + on_cos * turn_sin
        if v == 5:
            all_cos = all_cos + placed_ref[:, 0:128]
            all_sin = all_sin + placed_ref[:, 128:256]
        for i, value in enumerate((all_cos, all_sin)):
            mine_ref[:, 2 * v + i, :] = value[0:half]
            other_ref[:, 2 * v + i, :] = value[half:devices]
    spread = bdot(cells_ref[...], kernel_ref[0]) + bdot(cells_ref[...], kernel_ref[1])
    spread = pltpu.roll(spread, lon * (GRID // devices), 1)
    for c in range(2):
        for i in range(4):
            part = spread[devices * c : devices * c + devices, 128 * i : 128 * i + 128]
            at = 16 + 4 * c + i
            mine_ref[:, at, :] = part[0:half]
            other_ref[:, at, :] = part[half:devices]


def pack_observations(
    values_ref,
    marks_ref,
    filter_ref,
    cos_ref,
    sin_ref,
    table_ref,
    near_ref,
    far_ref,
    placed_ref,
):
    number, width = values_ref.shape
    half = near_ref.shape[0]
    devices = 2 * half
    core = own_place()[1] % 2
    lengths = to_col(marks_ref[2:3, :])
    values = jnp.where(iota((number, width), 1).astype(F32) < lengths, values_ref[...], 0.0)
    high, low = halves_of(values)
    rest = (values - high.astype(F32) - low.astype(F32)).astype(jnp.bfloat16)
    owner_row = marks_ref[0:1, :].astype(jnp.int32)
    owner_col = to_col(owner_row)
    same = owner_col == owner_row
    before = same & (iota((number, number), 0) < iota((number, number), 1))
    arrival_row = jnp.sum(before.astype(jnp.int32), axis=0, keepdims=True)
    after = same & (iota((number, number), 0) > iota((number, number), 1))
    arrival_col = jnp.sum(after.astype(jnp.int32), axis=1, keepdims=True)
    chip_row, core_row = owner_row // 2, owner_row % 2
    target = chip_row * 16 + arrival_row
    label = marks_ref[1:2, :]
    arrived = (iota((number, 128), 1) == arrival_col).astype(F32).astype(jnp.bfloat16)
    for out_ref, side in ((near_ref, core), (far_ref, 1 - core)):
        goes = core_row == side
        sent = ((iota((16 * half, number), 0) == target) & goes).astype(F32)
        sent = sent.astype(jnp.bfloat16)
        block = bdot(sent, high) + bdot(sent, low) + bdot(sent, rest)
        block = block.reshape(half, 16, width)
        out_ref[:, 0:CAP, :] = block[:, 0:CAP, 0:128]
        out_ref[:, CAP : 2 * CAP, :] = block[:, 0:CAP, 128:256]
        named = ((iota((half, number), 0) == chip_row) & goes).astype(F32) * label
        out_ref[:, 2 * CAP : 32, :] = jnp.zeros((half, 32 - 2 * CAP, 128), F32)
        out_ref[:, 2 * CAP, :] = bdot(named.astype(jnp.bfloat16), arrived)
    head = table_ref[0, 0:width, :]
    sums = bdot(high, head) + bdot(low, head) + bdot(high, table_ref[1, 0:width, :])
    whose = (iota((number, devices), 1) == owner_col).astype(F32)
    turn_cos, turn_sin = pick_dot(whose, cos_ref[...]), pick_dot(whose, sin_ref[...])
    on_cos, on_sin = sums[:, 0:128], sums[:, 128:256]
    all_cos = on_cos * turn_cos - on_sin * turn_sin
    all_sin = on_sin * turn_cos + on_cos * turn_sin
    mask = filter_ref[0:1, :]
    rows = mask.shape[1]
    in_row = (iota((rows, number), 0).astype(F32) == label).astype(F32)
    slots = slot_rows(mask, core, devices).astype(jnp.bfloat16)
    chosen = bdot(slots, in_row.astype(jnp.bfloat16))
    placed_ref[:, 0:128] = pick_dot(chosen, all_cos)
    placed_ref[:, 128:256] = pick_dot(chosen, all_sin)


def join(mine_ref, both_ref, out_ref):
    other = 1 - own_place()[1] % 2
    for i in range(12):
        pair = slice(2 * i, 2 * i + 2)
        out_ref[:, i, :, :] = mine_ref[:, pair, :] + both_ref[other, :, pair, :]
    for i in range(12, 24):
        out_ref[:, i, :, :] = mine_ref[:, 2 * i : 2 * i + 2, :]
        out_ref[:, i + 12, :, :] = both_ref[other, :, 2 * i : 2 * i + 2, :]
    out_ref[:, 36, 0, :] = mine_ref[:, 48, :]
    out_ref[:, 36, 1, :] = both_ref[other, :, 48, :]


def unpack_observations(in_ref, corner_ref, dep_ref, west_ref, data_ref):
    half = in_ref.shape[0]
    rows = dep_ref.shape[0]
    lines = 4 * CAP
    total = half * lines
    spot = iota((128, total), 1) % lines
    label_row = jnp.zeros((1, total), F32)
    own = iota((half, total), 1) // lines == iota((half, total), 0)
    for s in range(2):
        here = (spot // (2 * CAP) == s) & (spot % CAP == iota((128, total), 0))
        across = bdot(
            in_ref[:, 36, s, :].astype(jnp.bfloat16), here.astype(F32).astype(jnp.bfloat16)
        )
        label_row = label_row + jnp.sum(jnp.where(own, across, 0.0), axis=0, keepdims=True)
    line = iota((rows, total), 1) % lines
    hit = iota((rows, total), 0).astype(F32) == label_row
    for i in range(2 * CAP):
        data_ref[:, 2 * i : 2 * i + 2, :] = in_ref[:, 12 + i, :, :]
    data = data_ref[...].reshape(total, 128)
    for i in range(2):
        side = (hit & ((line // CAP) % 2 == i)).astype(F32)
        dep_ref[:, 128 * i : 128 * i + 128] = pick_dot(side, data)
    dep_ref[:, 256:384] = jnp.zeros((rows, 128), F32)
    west_ref[0:rows, :] = pltpu.roll(dep_ref[:, 0:128], 14, 1)
    west_ref[rows : rows + corner_ref.shape[0], :] = corner_ref[...]


def own_row(
    in_ref,
    filter_ref,
    lines_ref,
    slope_ref,
    to_grid_ref,
    from_grid_ref,
    out_ref,
    left_ref,
    grid_ref,
    res_ref,
    sum_ref,
):
    band, lon = own_place()
    pairs = in_ref[0, 0:12, :, :]
    for i in range(1, in_ref.shape[0]):
        pairs = pairs + in_ref[i, 0:12, :, :]
    for i in range(12):
        sum_ref[2 * i : 2 * i + 2, :] = pairs[i]
    sums = sum_ref[...]
    mask, keep = filter_ref[0:1, :], filter_ref[1:2, :]
    chosen = ((rank_in_row(mask) == lon) & (mask == 1)).astype(F32)

    def pick(row):
        return jnp.sum(chosen * row, axis=1, keepdims=True)

    rows = mask.shape[1]
    weight = pick(1.0 - keep)
    both = lines_ref[pl.ds(band, 1), :]
    metric = pick(both[:, 0:rows])
    rotation = pick(both[:, 128 : 128 + rows])

    def line(i):
        return sums[i : i + 1, :]

    slope = slope_ref[0:1, :]
    left_ref[...] = jnp.zeros(left_ref.shape, F32)
    pairs = (
        (weight * (line(2) - rotation * line(4)), weight * (line(3) - rotation * line(5))),
        (metric * slope * line(7), -metric * slope * line(6)),
        (weight * (line(4) + rotation * line(2)), weight * (line(5) + rotation * line(3))),
        (line(8), line(9)),
    )
    for i, (on_cos, on_sin) in enumerate(pairs):
        left_ref[i : i + 1, 0:128] = on_cos
        left_ref[i : i + 1, 128:256] = on_sin
    at = tdot_few(left_ref[...], to_grid_ref)
    wet = jnp.concatenate([line(16), line(17), line(18), line(19)], axis=1)
    share = (COURANT / LEVELS) * jnp.concatenate([line(20), line(21), line(22), line(23)], axis=1)
    grid_ref[...] = jnp.zeros(grid_ref.shape, F32)
    grid_ref[0:1, :] = wet * at[0:1] + share * at[1:2]
    grid_ref[1:2, :] = wet * at[2:3] + share * at[3:4]
    back = tdot_few(grid_ref[...], from_grid_ref)
    res_ref[0:6, :] = sums[0:6]
    res_ref[6:8, :] = sums[10:12] + sums[6:8]
    for i in range(2):
        res_ref[8 + 2 * i : 9 + 2 * i, :] = line(12 + 2 * i) + back[i : i + 1, 0:128]
        res_ref[9 + 2 * i : 10 + 2 * i, :] = line(13 + 2 * i) + back[i : i + 1, 128:256]
    for i in range(3):
        out_ref[:, i, :, :] = jnp.broadcast_to(
            res_ref[4 * i : 4 * i + 4, :][None], (out_ref.shape[0], 4, 128)
        )


def slots_to_rows(all_ref, mask, at):
    half = all_ref.shape[1]
    lines = at.shape[0]
    here = iota((lines, mask.shape[1]), 1) == at
    rank = jnp.sum(
        jnp.where(here & (mask == 1), rank_in_row(mask) + 1.0, 0.0), axis=1, keepdims=True
    )
    total = jnp.zeros((lines, 12 * 128), F32)
    for c in range(2):
        chosen = (2 * iota((lines, half), 1) + c + 1).astype(F32) == rank
        every = [all_ref[c, :, v // 4, v % 4, :] for v in range(12)]
        total = total + pick_dot(chosen.astype(F32), jnp.concatenate(every, axis=1))
    return total


def band_edges(cols, all_ref, dep_ref, edge_ref, filter_ref, depx_ref, north_ref, south_ref):
    rows = dep_ref.shape[0]
    mask = filter_ref[0:1, :]
    first = cols - 256
    lane = iota((rows, 128), 1)
    depx_ref[:, 0:256] = dep_ref[:, 0:256]
    depx_ref[:, 256:384] = jnp.where(
        (lane == first) | (lane == first + 1), edge_ref[0:rows, :], 0.0
    )
    line = iota((8, 1), 0)
    ends = slots_to_rows(all_ref, mask, jnp.where(line < 4, line, line + (rows - 8)))
    for v in range(12):
        own = ends[:, 128 * v : 128 * v + 128]
        north_ref[4 * v : 4 * v + 4, :] = own[0:4]
        south_ref[4 * v : 4 * v + 4, :] = own[4:8]
    for out_ref, at in ((north_ref, 0), (south_ref, rows - 2)):
        for r in range(2):
            for t in range(3):
                out_ref[48 + 3 * r + t : 49 + 3 * r + t, :] = depx_ref[
                    at + r : at + r + 1, 128 * t : 128 * t + 128
                ]
        out_ref[54:56, :] = jnp.zeros((2, 128), F32)


EDGE = 16
SURE = 8


def two_steps(fields, low, weight, terms, dep):
    metric, rotation, valid = terms
    level = fields[3]
    wet = (level > 0).astype(F32)
    share = COURANT * (level / LEVELS)

    def half_step(height, east, north, f):
        height = height + weight * (low[f] - height)
        east = east + weight * (low[f + 1] - east)
        north = north + weight * (low[f + 2] - north)
        middle = valid * (height + COURANT * (metric * lon_diff(east) + lat_diff(north)))
        new_east = east - rotation * north + share * (metric * lon_diff(middle))
        new_north = north + rotation * east + share * lat_diff(middle)
        return middle, new_east, new_north

    middle, east, north = half_step(fields[0], fields[1], fields[2], 0)
    return half_step(middle + dep, wet * east, wet * north, 3)


def own_rows(
    cols,
    all_ref,
    filter_ref,
    cos_ref,
    sin_ref,
    table_ref,
    wide_ref,
    left_ref,
    right_ref,
    weight_ref,
    depx_ref,
    terms_ref,
    low_ref,
    inner_ref,
    stack_ref,
    ext_ref,
):
    mask = filter_ref[0:1, :]
    rows = mask.shape[1]
    band, lon = own_place()
    turn_cos, turn_sin = cos_ref[pl.ds(lon, 1), :], sin_ref[pl.ds(lon, 1), :]
    coef = slots_to_rows(all_ref, mask, iota((rows, 1), 0))
    for f in range(6):
        lines = slice(rows * f, rows * f + rows)
        on_cos = coef[:, 256 * f : 256 * f + 128]
        on_sin = coef[:, 256 * f + 128 : 256 * f + 256]
        stack_ref[lines, 0:128] = on_cos * turn_cos + on_sin * turn_sin
        stack_ref[lines, 128:256] = on_sin * turn_cos - on_cos * turn_sin
    low_ref[...] = tdot(stack_ref[...], table_ref)
    for f in range(4):
        ext_ref[f, :, 0:256] = wide_ref[f, 0:rows, 0:256]
        ext_ref[f, :, 256:384] = third_tile(
            wide_ref[f, 0:rows, 256:384], left_ref[...], right_ref[...], f, cols
        )
    state = two_steps(
        [ext_ref[f] for f in range(4)],
        [low_ref[rows * f : rows * f + rows, :] for f in range(6)],
        weight_ref[0:rows, 0:1],
        row_terms(terms_ref[0:rows, :], band),
        depx_ref[...],
    )
    for i in range(3):
        inner_ref[i] = state[i][SURE : rows - SURE]


def last_stage(
    wide_ref,
    left_ref,
    right_ref,
    corner_left_ref,
    corner_right_ref,
    weight_ref,
    own_ref,
    inner_ref,
    depx_ref,
    above_ref,
    below_ref,
    terms_ref,
    cos_ref,
    sin_ref,
    table_ref,
    h_hbm,
    e_hbm,
    n_hbm,
    stack_ref,
    dep_ref,
    ext_ref,
    h_ref,
    e_ref,
    n_ref,
    sems,
):
    rows, cols = h_ref.shape
    ext = rows + 2 * HALO
    band, lon = own_place()
    pairs = ((h_ref, h_hbm), (e_ref, e_hbm), (n_ref, n_hbm))
    spans = (pl.ds(SURE, rows - 2 * SURE), pl.ds(0, SURE), pl.ds(rows - SURE, SURE))
    copies = [
        [
            pltpu.make_async_copy(a.at[span, :], b.at[span, :], sems.at[i, j])
            for j, span in enumerate(spans)
        ]
        for i, (a, b) in enumerate(pairs)
    ]
    for i, (out_ref, _) in enumerate(pairs):
        out_ref[SURE : rows - SURE, :] = inner_ref[i, :, 0:cols]
        copies[i][0].start()
    for f in range(4):
        parts = (
            (slice(0, EDGE), slice(rows - EDGE, rows)),
            (slice(EDGE + 2 * HALO, 2 * EDGE + 2 * HALO), slice(0, EDGE)),
        )
        for to, at in parts:
            ext_ref[f, to, 0:256] = wide_ref[f, at, 0:256]
            ext_ref[f, to, 256:384] = third_tile(
                wide_ref[f, at, 256:384], left_ref[at, :], right_ref[at, :], f, cols
            )
        to = slice(EDGE, EDGE + 2 * HALO)
        lines = slice(2 * HALO * f, 2 * HALO * f + 2 * HALO)
        ext_ref[f, to, 0:256] = wide_ref[f, rows:ext, 0:256]
        ext_ref[f, to, 256:384] = third_tile(
            wide_ref[f, rows:ext, 256:384],
            corner_left_ref[lines, :],
            corner_right_ref[rows + 2 * HALO * f : rows + 2 * HALO * f + 2 * HALO, :],
            f,
            cols,
        )
    turn_cos, turn_sin = cos_ref[pl.ds(lon, 1), :], sin_ref[pl.ds(lon, 1), :]
    for f in range(6):
        for at, in_ref in ((8 * f, below_ref), (8 * f + 4, above_ref)):
            on_cos = in_ref[8 * f : 8 * f + 4, :]
            on_sin = in_ref[8 * f + 4 : 8 * f + 8, :]
            stack_ref[at : at + 4, 0:128] = on_cos * turn_cos + on_sin * turn_sin
            stack_ref[at : at + 4, 128:256] = on_sin * turn_cos - on_cos * turn_sin
    edges = tdot(stack_ref[...], table_ref)
    low = [
        jnp.concatenate(
            [
                own_ref[rows * f + rows - EDGE : rows * f + rows, :],
                edges[8 * f : 8 * f + 8, :],
                own_ref[rows * f : rows * f + EDGE, :],
            ],
            axis=0,
        )
        for f in range(6)
    ]
    dep_ref[0:EDGE, :] = depx_ref[rows - EDGE : rows, :]
    dep_ref[EDGE : EDGE + 2 * HALO, :] = jnp.zeros((2 * HALO, LANES), F32)
    dep_ref[EDGE + 2 * HALO : 2 * EDGE + 2 * HALO, :] = depx_ref[0:EDGE, :]
    for in_ref, at in ((below_ref, EDGE), (above_ref, EDGE + 2 * HALO - 2)):
        for r in range(2):
            for t in range(3):
                dep_ref[at + r : at + r + 1, 128 * t : 128 * t + 128] = in_ref[
                    48 + 3 * r + t : 49 + 3 * r + t, :
                ]

    def around(ref):
        return jnp.concatenate([ref[rows - EDGE : ext, :], ref[0:EDGE, :]], axis=0)

    state = two_steps(
        [ext_ref[f] for f in range(4)],
        low,
        around(weight_ref)[:, 0:1],
        row_terms(around(terms_ref), band),
        dep_ref[...],
    )
    south, north = slice(EDGE - SURE, EDGE), slice(EDGE + 2 * HALO, EDGE + 2 * HALO + SURE)
    for i, (out_ref, _) in enumerate(pairs):
        out_ref[0:SURE, :] = state[i][north, 0:cols]
        out_ref[rows - SURE : rows, :] = state[i][south, 0:cols]
        copies[i][1].start()
        copies[i][2].start()
    for group in copies:
        for copy in group:
            copy.wait()


def tables(length, cols, devices, rows, bands):
    mode = np.arange(MODES)
    norm = np.where(mode == 0, 1.0 / length, 2.0 / length)
    lane = np.arange(LANES)

    def angle(at, number):
        phase = (at[:, None].astype(np.int64) * number[None, :]) % length
        return phase * (2.0 * math.pi / length)

    inside = (lane < cols)[:, None]
    place = np.where(lane < LANES - HALO, lane, lane - LANES)
    shown = ((lane < cols + HALO) | (lane >= LANES - HALO))[:, None]
    around = angle(place, mode)
    analyse = np.concatenate([np.cos(around) * norm, np.sin(around) * norm], axis=1) * shown
    evaluate = (np.concatenate([np.cos(around), np.sin(around)], axis=1) * shown).T
    wide = np.arange(1, 2 * MODES - 1)
    spot = np.arange(GRID) * (length / GRID)
    gap = spot[None, :] - lane[:, None]
    kernel = np.full((LANES, GRID), 1.0 / length)
    for k in wide:
        kernel += (2.0 / length) * np.cos(2.0 * math.pi / length * k * gap)
    kernel *= inside
    coarse = (np.arange(GRID)[:, None] * mode[None, :]) % GRID * (2.0 * math.pi / GRID)
    to_grid = np.concatenate([np.cos(coarse), np.sin(coarse)], axis=1).T
    part = np.where(mode == 0, 1.0 / GRID, 2.0 / GRID)
    from_grid = np.concatenate([np.cos(coarse) * part, np.sin(coarse) * part], axis=1)
    turn = (np.arange(devices)[:, None] * mode[None, :]) % devices * (2.0 * math.pi / devices)
    slope = np.tile(np.sin(2.0 * math.pi / length * mode)[None, :], (8, 1))
    total = rows * bands
    index = np.arange(rows + 2 * HALO)
    local = np.where(index < rows + HALO, index, index - (rows + 2 * HALO))
    terms = np.zeros((rows + 2 * HALO, 128))
    lines = np.zeros((bands, 256))
    for b in range(bands):
        g = b * rows + local
        phi = (2.0 * ((g + 0.5) / total) - 1.0) * LIMIT
        terms[:, b] = 1.0 / np.cos(phi)
        terms[:, 16 + b] = ROTATION * np.sin(phi)
        terms[:, 32 + b] = (g >= 0) & (g < total)
        lines[b, 0:rows] = terms[0:rows, b]
        lines[b, 128 : 128 + rows] = terms[0:rows, 16 + b]
    made = dict(
        analyse=analyse,
        evaluate=evaluate,
        kernel=kernel,
        to_grid=to_grid,
        from_grid=from_grid,
        cos=np.cos(turn),
        sin=np.sin(turn),
        slope=slope,
        terms=terms,
        lines=lines,
    )
    for name, value in made.items():
        made[name] = value.astype(np.float32)
        if name in ("analyse", "evaluate", "kernel", "to_grid", "from_grid"):
            high = value.astype(ml_dtypes.bfloat16)
            low = (value - high.astype(np.float64)).astype(ml_dtypes.bfloat16)
            made[name] = np.stack([high, low])
    return made


VMEM = pl.BlockSpec(memory_space=pltpu.VMEM)
HBM = pl.BlockSpec(memory_space=pltpu.HBM)


def call(kernel, name, outs, args, scratch=(), direct=(), cost=1.0, outside=False):
    shapes = [jax.ShapeDtypeStruct(shape, F32) for shape in outs]
    specs = [
        HBM if i in direct else VMEM for i in range(len(args))
    ]
    args = [
        pltpu.with_memory_space_constraint(arg, pltpu.HBM) if i in direct else arg
        for i, arg in enumerate(args)
    ]
    held = [pltpu.VMEM(args[i].shape, args[i].dtype) for i in direct]
    held += [pltpu.SemaphoreType.DMA((len(direct),))] if direct else []
    return pl.pallas_call(
        kernel,
        name=name,
        out_shape=shapes,
        in_specs=specs,
        out_specs=[HBM if outside else VMEM] * len(shapes),
        scratch_shapes=held + [
            pltpu.VMEM(shape, F32) if isinstance(shape, tuple) else shape for shape in scratch
        ],
        cost_estimate=pl.CostEstimate(
            flops=int(cost * 1e9), bytes_accessed=int(cost * 2e6), transcendentals=0
        ),
        compiler_params=pltpu.CompilerParams(
            vmem_limit_bytes=40 * 2**20
        ),
    )(*args)


LON = ("z", "core")


def on_device(
    back_height,
    back_east,
    back_north,
    obs_values,
    obs_owner,
    obs_row,
    obs_count,
    polar_mask,
    keep_share,
    depth_level,
):
    rows, cols = back_height.shape
    bands, devices = lax.axis_size("band"), lax.axis_size(LON)
    half = devices // 2
    number, width = obs_values.shape
    ext = rows + 2 * HALO
    made = tables(cols * devices, cols, devices, rows, bands)

    def send(value, axis, shift, closed):
        count = lax.axis_size(axis)
        pairs = [(i, (i + shift) % count) for i in range(count) if closed or 0 <= i + shift < count]
        return lax.ppermute(value, axis, pairs)

    fields, west, east, north, south, kept, marks = call(
        pack_tile,
        "pack_tile",
        [(4, rows, LANES), (rows, 128), (rows, 128)] + [(4 * HALO, LANES)] * 2 + [(8, rows), (8, number)],
        (
            back_height,
            back_east,
            back_north,
            depth_level,
            polar_mask.reshape(1, rows),
            keep_share.reshape(1, rows),
            obs_owner.reshape(1, number),
            obs_row.reshape(1, number),
            obs_count.reshape(1, number),
        ),
        direct=range(9),
    )
    below, above = send(north, "band", -1, False), send(south, "band", 1, False)
    right, left = send(west, LON, -1, True), send(east, LON, 1, True)
    near, far, placed = call(
        pack_observations,
        "pack_observations",
        [(half, 32, 128), (half, 32, 128), (devices, 256)],
        (obs_values, marks, kept, made["cos"], made["sin"], made["analyse"]),
        cost=3.0,
    )
    wide, weight, corner_west, corner_east, mine, other = call(
        lambda *refs: partial_sums(cols, *refs),
        "partial_sums",
        [(4, ext, LANES), (ext, 128)] + [(8 * HALO, 128)] * 2 + [(half, 56, 128)] * 2,
        (
            fields,
            left,
            right,
            above,
            below,
            kept,
            made["terms"],
            made["cos"],
            made["sin"],
            made["analyse"],
            made["kernel"],
            placed,
            near,
            far,
        ),
        scratch=[pltpu.VMEM((n * devices, LANES), jnp.bfloat16) for n in (8, 8, 2)],
    )
    swapped = lax.all_gather(other, "core", axis=0, tiled=False)
    (joined,) = call(
        join, "join", [(half, 37, 2, 128)], (mine, swapped)
    )
    owned = lax.all_to_all(joined, "z", split_axis=0, concat_axis=0, tiled=True)
    (spread,) = call(
        own_row,
        "own_row",
        [(half, 3, 4, 128)],
        (
            owned,
            kept,
            made["lines"],
            made["slope"],
            made["to_grid"],
            made["from_grid"],
        ),
        scratch=[(8, 256), (8, GRID), (12, 128), (24, 128)],
    )
    shared = lax.all_to_all(spread, "z", split_axis=0, concat_axis=0, tiled=True)
    everyone = lax.all_gather(shared, "core", axis=0, tiled=False)
    dep, west = call(
        unpack_observations,
        "unpack_observations",
        [(rows, LANES), (rows + 8 * HALO, 128)],
        (owned, corner_west),
        scratch=[(half, 48, 128)],
    )
    corner_east = lax.optimization_barrier((corner_east, spread))[0]
    corner_right, corner_left = send(west, LON, -1, True), send(corner_east, LON, 1, True)
    dep, corner_left = lax.optimization_barrier((dep, corner_left))
    depx, north, south = call(
        lambda *refs: band_edges(cols, *refs),
        "band_edges",
        [(rows, LANES), (56, 128), (56, 128)],
        (everyone, dep, corner_right, kept),
    )
    below, above = send(north, "band", -1, False), send(south, "band", 1, False)
    own, inner = call(
        lambda *refs: own_rows(cols, *refs),
        "own_rows",
        [(6 * rows, LANES), (3, rows - 2 * SURE, LANES)],
        (
            everyone,
            kept,
            made["cos"],
            made["sin"],
            made["evaluate"],
            wide,
            left,
            right,
            weight,
            depx,
            made["terms"],
        ),
        scratch=[(6 * rows, 256), (4, rows, LANES)],
    )
    edge = 2 * EDGE + 2 * HALO
    return tuple(
        call(
            last_stage,
            "last_stage",
            [(rows, cols)] * 3,
            (
                wide,
                left,
                right,
                corner_left,
                corner_right,
                weight,
                own,
                inner,
                depx,
                above,
                below,
                made["terms"],
                made["cos"],
                made["sin"],
                made["evaluate"],
            ),
            scratch=[(48, 256), (edge, LANES), (4, edge, LANES)]
            + [(rows, cols)] * 3
            + [pltpu.SemaphoreType.DMA((3, 3))],
            outside=True,
        )
    )


def solution(mesh):
    placed = (
        P("band", LON),
        P("band", LON),
        P("band", LON),
        P(("band", *LON), None),
        P(("band", *LON), None),
        P(("band", *LON)),
        P(("band", *LON)),
        P("band"),
        P("band"),
        P("band", LON),
    )
    fine = jax.sharding.Mesh(
        mesh.devices.reshape(mesh.devices.shape[0], -1, 2), ("band", *LON)
    )
    return jax.shard_map(
        on_device,
        mesh=fine,
        in_specs=placed,
        out_specs=(P("band", LON), P("band", LON), P("band", LON)),
        check_vma=False,
    )
```

```python
import math

import jax
import jax.numpy as jnp
import ml_dtypes
import numpy as np
from jax import lax
from jax.experimental import pallas as pl
from jax.experimental.pallas import tpu as pltpu
from jax.sharding import PartitionSpec as P

MODES = 128
LEVELS = 50
COURANT = 0.25
ROTATION = 0.4
LIMIT = 1.3089969389957472
CAP = 12
LANES = 384
GRID = 512
HALO = 4
F32 = jnp.float32


def hdot(left, right):
    return jnp.dot(left, right, precision=lax.Precision.HIGHEST, preferred_element_type=F32)


def halves_of(value):
    high = value.astype(jnp.bfloat16)
    return high, (value - high.astype(F32)).astype(jnp.bfloat16)


def bdot(left, right):
    return jnp.dot(left, right, preferred_element_type=F32)


def pick_dot(chosen, value):
    high, low = halves_of(value)
    rest = (value - high.astype(F32) - low.astype(F32)).astype(jnp.bfloat16)
    chosen = chosen.astype(jnp.bfloat16)
    return bdot(chosen, high) + bdot(chosen, low) + bdot(chosen, rest)


def tdot(left, table_ref):
    high, low = halves_of(left)
    return bdot(high, table_ref[0]) + bdot(low, table_ref[0]) + bdot(high, table_ref[1])


def tdot_few(left, table_ref):
    lines = left.shape[0]
    high = left.astype(jnp.bfloat16).astype(F32)
    both = jnp.concatenate([high, left - high], axis=0).astype(jnp.bfloat16)
    first = bdot(both, table_ref[0])
    return first[0:lines] + first[lines:] + bdot(left.astype(jnp.bfloat16), table_ref[1])


def mdot(left, right):
    return jnp.dot(left, right, precision=lax.Precision.HIGH, preferred_element_type=F32)


def iota(shape, dim):
    return lax.broadcasted_iota(jnp.int32, shape, dim)


def own_place():
    return lax.axis_index("band"), 2 * lax.axis_index("z") + lax.axis_index("core")


def swap_odd(first, second):
    even = lax.axis_index("band") % 2 == 0
    return jnp.where(even, first, second), jnp.where(even, second, first)


def to_col(row):
    size = row.shape[1]
    same = iota((size, size), 0) == iota((size, size), 1)
    return jnp.sum(jnp.where(same, row, jnp.zeros_like(row)), axis=1, keepdims=True)


def to_row(col):
    size = col.shape[0]
    same = iota((size, size), 0) == iota((size, size), 1)
    return jnp.sum(jnp.where(same, col, jnp.zeros_like(col)), axis=0, keepdims=True)


def lon_diff(field):
    width = field.shape[1]
    return 0.5 * (pltpu.roll(field, width - 1, 1) - pltpu.roll(field, 1, 1))


def lat_diff(field):
    rows = field.shape[0]
    return 0.5 * (pltpu.roll(field, rows - 1, 0) - pltpu.roll(field, 1, 0))


def rank_in_row(mask_row):
    size = mask_row.shape[1]
    before = iota((size, size), 0) < iota((size, size), 1)
    return jnp.sum(jnp.where(before, to_col(mask_row), 0), axis=0, keepdims=True)


def slot_rows(mask_row, core, devices):
    rows = mask_row.shape[1]
    half = devices // 2
    line = iota((devices, rows), 0)
    slot = jnp.where(line < half, 2 * line + core, 2 * (line - half) + 1 - core)
    hit = (slot == rank_in_row(mask_row)) & (mask_row == 1)
    return hit.astype(F32)


WEIGHT_LANE = 300 - 256


def pack_tile(
    h_hbm,
    e_hbm,
    n_hbm,
    d_hbm,
    mask_hbm,
    keep_hbm,
    owner_hbm,
    row_hbm,
    count_hbm,
    fields_ref,
    west_ref,
    east_ref,
    north_ref,
    south_ref,
    filter_ref,
    marks_ref,
    h_ref,
    e_ref,
    n_ref,
    d_ref,
    mask_ref,
    keep_ref,
    owner_ref,
    row_ref,
    count_ref,
    sems,
):
    pairs = (
        (h_hbm, h_ref),
        (e_hbm, e_ref),
        (n_hbm, n_ref),
        (d_hbm, d_ref),
        (mask_hbm, mask_ref),
        (keep_hbm, keep_ref),
        (owner_hbm, owner_ref),
        (row_hbm, row_ref),
        (count_hbm, count_ref),
    )
    copies = [pltpu.make_async_copy(a, b, sems.at[i]) for i, (a, b) in enumerate(pairs)]
    for copy in copies:
        copy.start()
    fields_ref[...] = jnp.zeros(fields_ref.shape, F32)
    for copy in copies:
        copy.wait()
    rows, cols = h_ref.shape
    filter_ref[0:1, :] = mask_ref[...].astype(F32)
    filter_ref[1:2, :] = keep_ref[...]
    filter_ref[2:8, :] = jnp.zeros((6, rows), F32)
    for i, in_ref in enumerate((owner_ref, row_ref, count_ref)):
        marks_ref[i : i + 1, :] = in_ref[...].astype(F32)
    marks_ref[3:8, :] = jnp.zeros((5, marks_ref.shape[1]), F32)
    weight = to_col(mask_ref[...].astype(F32) * (1.0 - keep_ref[...]))
    level = d_ref[...].astype(F32)
    wet = (level > 0).astype(F32)
    values = (h_ref[...], wet * e_ref[...], wet * n_ref[...], level)
    lane = iota((rows, 128), 1)
    west = jnp.zeros(lane.shape, F32)
    east = jnp.zeros(lane.shape, F32)
    last = cols - HALO - 256
    for f, value in enumerate(values):
        fields_ref[f, :, 0:cols] = value
        inside = (lane >= HALO * f) & (lane < HALO * f + HALO)
        head = fields_ref[f, :, 0:128]
        tail = fields_ref[f, :, 256:384]
        if f:
            head = pltpu.roll(head, HALO * f, 1)
        west = jnp.where(inside, head, west)
        east = jnp.where(inside, pltpu.roll(tail, (HALO * f - last) % 128, 1), east)
        for out_ref, at in ((north_ref, 0), (south_ref, rows - HALO)):
            span = slice(at, at + HALO)
            lines = slice(HALO * f, HALO * f + HALO)
            edge = fields_ref[f, span, 256:384]
            if f == 3:
                edge = jnp.where(iota(edge.shape, 1) == WEIGHT_LANE, weight[span, :], edge)
            out_ref[lines, 0:256] = fields_ref[f, span, 0:256]
            out_ref[lines, 256:384] = edge
    west_ref[...] = west
    east_ref[...] = east
    north, south = north_ref[...], south_ref[...]
    north_ref[...], south_ref[...] = swap_odd(south, north)


def third_tile(tail, left, right, f, cols):
    lane = iota(tail.shape, 1)
    first = cols - 256
    shifted = pltpu.roll(right, (first - HALO * f) % 128, 1)
    tail = jnp.where((lane >= first) & (lane < first + HALO), shifted, tail)
    shifted = pltpu.roll(left, (128 - HALO - HALO * f) % 128, 1)
    return jnp.where(lane >= 128 - HALO, shifted, tail)


def row_terms(terms, band):
    lane = iota(terms.shape, 1)
    return [
        jnp.sum(jnp.where(lane == band + 16 * i, terms, 0.0), axis=1, keepdims=True)
        for i in range(3)
    ]


def partial_sums(
    cols,
    fields_ref,
    left_ref,
    right_ref,
    above_ref,
    below_ref,
    filter_ref,
    terms_ref,
    cos_ref,
    sin_ref,
    table_ref,
    kernel_ref,
    placed_ref,
    near_ref,
    far_ref,
    ext_ref,
    weight_ref,
    west_ref,
    east_ref,
    mine_ref,
    other_ref,
    high_ref,
    low_ref,
    cells_ref,
):
    rows = fields_ref.shape[1]
    ext = rows + 2 * HALO
    devices = cos_ref.shape[0]
    half = devices // 2
    band, lon = own_place()
    below, above = swap_odd(below_ref[...], above_ref[...])
    for f in range(4):
        ext_ref[f, 0:rows, :] = fields_ref[f]
        ext_ref[f, rows : rows + HALO, :] = below[HALO * f : HALO * f + HALO]
        ext_ref[f, rows + HALO : ext, :] = above[HALO * f : HALO * f + HALO]
    edge = ext_ref[3, rows:ext, 256:384]
    marked = iota(edge.shape, 1) == WEIGHT_LANE
    mask, keep = filter_ref[0:1, :], filter_ref[1:2, :]
    weight_ref[0:rows, :] = jnp.broadcast_to(to_col(mask * (1.0 - keep)), (rows, 128))
    weight_ref[rows:ext, :] = jnp.broadcast_to(
        jnp.sum(jnp.where(marked, edge, 0.0), axis=1, keepdims=True), (2 * HALO, 128)
    )
    ext_ref[3, rows:ext, 256:384] = jnp.where(marked, 0.0, edge)
    corner = iota((2 * HALO, 128), 1)
    last = cols - HALO - 256
    for f in range(4):
        lines = slice(2 * HALO * f, 2 * HALO * f + 2 * HALO)
        inside = (corner >= HALO * f) & (corner < HALO * f + HALO)
        head = ext_ref[f, rows:ext, 0:128]
        tail = ext_ref[f, rows:ext, 256:384]
        if f:
            head = pltpu.roll(head, HALO * f, 1)
        west_ref[lines, :] = jnp.where(inside, head, 0.0)
        east_ref[lines, :] = jnp.where(inside, pltpu.roll(tail, (HALO * f - last) % 128, 1), 0.0)
    weight = weight_ref[:, 0:1]
    rest = 1.0 - weight
    metric, rotation, valid = row_terms(terms_ref[...], band)
    metric = metric * valid
    height, east, north = ext_ref[0], ext_ref[1], ext_ref[2]
    ext_ref[3, 0:rows, 256:384] = third_tile(
        ext_ref[3, 0:rows, 256:384], left_ref[...], right_ref[...], 3, cols
    )
    share = ext_ref[3] / LEVELS
    low_height = weight * height + COURANT * (
        metric * lon_diff(weight * east) + lat_diff(weight * north)
    )
    low_height = valid * low_height
    east_rest, north_rest = rest * east, rest * north
    middle = valid * (
        rest * height + COURANT * (metric * lon_diff(east_rest) + lat_diff(north_rest))
    )
    new_east = east_rest - rotation * north_rest + COURANT * share * metric * lon_diff(middle)
    new_north = north_rest + rotation * east_rest + COURANT * share * lat_diff(middle)
    chosen = slot_rows(mask, own_place()[1] % 2, devices).astype(jnp.bfloat16)
    sources = (height, east, north, low_height, lat_diff(low_height), middle, new_east, new_north)
    for v, field in enumerate(sources):
        lines = slice(devices * v, devices * v + devices)
        high, low = halves_of(field[0:rows, :])
        high_ref[lines, :] = bdot(chosen, high).astype(jnp.bfloat16)
        low_ref[lines, :] = bdot(chosen, low).astype(jnp.bfloat16)
    mine_ref[:, 24:56, :] = near_ref[...]
    other_ref[:, 24:56, :] = far_ref[...]
    level = ext_ref[3, 0:rows, :]
    for c, cells in enumerate(((level > 0).astype(F32), level)):
        cells_ref[devices * c : devices * c + devices, :] = bdot(
            chosen, cells.astype(jnp.bfloat16)
        ).astype(jnp.bfloat16)
    sums = bdot(high_ref[...], table_ref[0]) + bdot(low_ref[...], table_ref[0])
    sums = sums + bdot(high_ref[...], table_ref[1])
    turn_cos, turn_sin = cos_ref[pl.ds(lon, 1), :], sin_ref[pl.ds(lon, 1), :]
    for v in range(len(sources)):
        lines = slice(devices * v, devices * v + devices)
        on_cos, on_sin = sums[lines, 0:128], sums[lines, 128:256]
        all_cos = on_cos * turn_cos - on_sin * turn_sin
        all_sin = on_sin * turn_cos + on_cos * turn_sin
        if v == 5:
            all_cos = all_cos + placed_ref[:, 0:128]
            all_sin = all_sin + placed_ref[:, 128:256]
        for i, value in enumerate((all_cos, all_sin)):
            mine_ref[:, 2 * v + i, :] = value[0:half]
            other_ref[:, 2 * v + i, :] = value[half:devices]
    spread = bdot(cells_ref[...], kernel_ref[0]) + bdot(cells_ref[...], kernel_ref[1])
    spread = pltpu.roll(spread, lon * (GRID // devices), 1)
    for c in range(2):
        for i in range(4):
            part = spread[devices * c : devices * c + devices, 128 * i : 128 * i + 128]
            at = 16 + 4 * c + i
            mine_ref[:, at, :] = part[0:half]
            other_ref[:, at, :] = part[half:devices]


def pack_observations(
    values_ref,
    marks_ref,
    filter_ref,
    cos_ref,
    sin_ref,
    table_ref,
    near_ref,
    far_ref,
    placed_ref,
):
    number, width = values_ref.shape
    half = near_ref.shape[0]
    devices = 2 * half
    core = own_place()[1] % 2
    lengths = to_col(marks_ref[2:3, :])
    values = jnp.where(iota((number, width), 1).astype(F32) < lengths, values_ref[...], 0.0)
    high, low = halves_of(values)
    rest = (values - high.astype(F32) - low.astype(F32)).astype(jnp.bfloat16)
    owner_row = marks_ref[0:1, :].astype(jnp.int32)
    owner_col = to_col(owner_row)
    same = owner_col == owner_row
    before = same & (iota((number, number), 0) < iota((number, number), 1))
    arrival_row = jnp.sum(before.astype(jnp.int32), axis=0, keepdims=True)
    after = same & (iota((number, number), 0) > iota((number, number), 1))
    arrival_col = jnp.sum(after.astype(jnp.int32), axis=1, keepdims=True)
    chip_row, core_row = owner_row // 2, owner_row % 2
    target = chip_row * 16 + arrival_row
    label = marks_ref[1:2, :]
    arrived = (iota((number, 128), 1) == arrival_col).astype(F32).astype(jnp.bfloat16)
    for out_ref, side in ((near_ref, core), (far_ref, 1 - core)):
        goes = core_row == side
        sent = ((iota((16 * half, number), 0) == target) & goes).astype(F32)
        sent = sent.astype(jnp.bfloat16)
        block = bdot(sent, high) + bdot(sent, low) + bdot(sent, rest)
        block = block.reshape(half, 16, width)
        out_ref[:, 0:CAP, :] = block[:, 0:CAP, 0:128]
        out_ref[:, CAP : 2 * CAP, :] = block[:, 0:CAP, 128:256]
        named = ((iota((half, number), 0) == chip_row) & goes).astype(F32) * label
        out_ref[:, 2 * CAP : 32, :] = jnp.zeros((half, 32 - 2 * CAP, 128), F32)
        out_ref[:, 2 * CAP, :] = bdot(named.astype(jnp.bfloat16), arrived)
    head = table_ref[0, 0:width, :]
    sums = bdot(high, head) + bdot(low, head) + bdot(high, table_ref[1, 0:width, :])
    whose = (iota((number, devices), 1) == owner_col).astype(F32)
    turn_cos, turn_sin = pick_dot(whose, cos_ref[...]), pick_dot(whose, sin_ref[...])
    on_cos, on_sin = sums[:, 0:128], sums[:, 128:256]
    all_cos = on_cos * turn_cos - on_sin * turn_sin
    all_sin = on_sin * turn_cos + on_cos * turn_sin
    mask = filter_ref[0:1, :]
    rows = mask.shape[1]
    in_row = (iota((rows, number), 0).astype(F32) == label).astype(F32)
    slots = slot_rows(mask, core, devices).astype(jnp.bfloat16)
    chosen = bdot(slots, in_row.astype(jnp.bfloat16))
    placed_ref[:, 0:128] = pick_dot(chosen, all_cos)
    placed_ref[:, 128:256] = pick_dot(chosen, all_sin)


def join(mine_ref, both_ref, out_ref):
    other = 1 - own_place()[1] % 2
    for i in range(12):
        pair = slice(2 * i, 2 * i + 2)
        out_ref[:, i, :, :] = mine_ref[:, pair, :] + both_ref[other, :, pair, :]
    for i in range(12, 24):
        out_ref[:, i, :, :] = mine_ref[:, 2 * i : 2 * i + 2, :]
        out_ref[:, i + 12, :, :] = both_ref[other, :, 2 * i : 2 * i + 2, :]
    out_ref[:, 36, 0, :] = mine_ref[:, 48, :]
    out_ref[:, 36, 1, :] = both_ref[other, :, 48, :]


def unpack_observations(in_ref, corner_ref, dep_ref, west_ref, data_ref):
    half = in_ref.shape[0]
    rows = dep_ref.shape[0]
    lines = 4 * CAP
    total = half * lines
    spot = iota((128, total), 1) % lines
    label_row = jnp.zeros((1, total), F32)
    own = iota((half, total), 1) // lines == iota((half, total), 0)
    for s in range(2):
        here = (spot // (2 * CAP) == s) & (spot % CAP == iota((128, total), 0))
        across = bdot(
            in_ref[:, 36, s, :].astype(jnp.bfloat16), here.astype(F32).astype(jnp.bfloat16)
        )
        label_row = label_row + jnp.sum(jnp.where(own, across, 0.0), axis=0, keepdims=True)
    line = iota((rows, total), 1) % lines
    hit = iota((rows, total), 0).astype(F32) == label_row
    for i in range(2 * CAP):
        data_ref[:, 2 * i : 2 * i + 2, :] = in_ref[:, 12 + i, :, :]
    data = data_ref[...].reshape(total, 128)
    for i in range(2):
        side = (hit & ((line // CAP) % 2 == i)).astype(F32)
        dep_ref[:, 128 * i : 128 * i + 128] = pick_dot(side, data)
    dep_ref[:, 256:384] = jnp.zeros((rows, 128), F32)
    west_ref[0:rows, :] = pltpu.roll(dep_ref[:, 0:128], 14, 1)
    west_ref[rows : rows + corner_ref.shape[0], :] = corner_ref[...]


def own_row(
    in_ref,
    filter_ref,
    lines_ref,
    slope_ref,
    to_grid_ref,
    from_grid_ref,
    out_ref,
    left_ref,
    grid_ref,
    res_ref,
    sum_ref,
):
    band, lon = own_place()
    pairs = in_ref[0, 0:12, :, :]
    for i in range(1, in_ref.shape[0]):
        pairs = pairs + in_ref[i, 0:12, :, :]
    for i in range(12):
        sum_ref[2 * i : 2 * i + 2, :] = pairs[i]
    sums = sum_ref[...]
    mask, keep = filter_ref[0:1, :], filter_ref[1:2, :]
    chosen = ((rank_in_row(mask) == lon) & (mask == 1)).astype(F32)

    def pick(row):
        return jnp.sum(chosen * row, axis=1, keepdims=True)

    rows = mask.shape[1]
    weight = pick(1.0 - keep)
    both = lines_ref[pl.ds(band, 1), :]
    metric = pick(both[:, 0:rows])
    rotation = pick(both[:, 128 : 128 + rows])

    def line(i):
        return sums[i : i + 1, :]

    slope = slope_ref[0:1, :]
    left_ref[...] = jnp.zeros(left_ref.shape, F32)
    pairs = (
        (weight * (line(2) - rotation * line(4)), weight * (line(3) - rotation * line(5))),
        (metric * slope * line(7), -metric * slope * line(6)),
        (weight * (line(4) + rotation * line(2)), weight * (line(5) + rotation * line(3))),
        (line(8), line(9)),
    )
    for i, (on_cos, on_sin) in enumerate(pairs):
        left_ref[i : i + 1, 0:128] = on_cos
        left_ref[i : i + 1, 128:256] = on_sin
    at = tdot_few(left_ref[...], to_grid_ref)
    wet = jnp.concatenate([line(16), line(17), line(18), line(19)], axis=1)
    share = (COURANT / LEVELS) * jnp.concatenate([line(20), line(21), line(22), line(23)], axis=1)
    grid_ref[...] = jnp.zeros(grid_ref.shape, F32)
    grid_ref[0:1, :] = wet * at[0:1] + share * at[1:2]
    grid_ref[1:2, :] = wet * at[2:3] + share * at[3:4]
    back = tdot_few(grid_ref[...], from_grid_ref)
    res_ref[0:6, :] = sums[0:6]
    res_ref[6:8, :] = sums[10:12] + sums[6:8]
    for i in range(2):
        res_ref[8 + 2 * i : 9 + 2 * i, :] = line(12 + 2 * i) + back[i : i + 1, 0:128]
        res_ref[9 + 2 * i : 10 + 2 * i, :] = line(13 + 2 * i) + back[i : i + 1, 128:256]
    for i in range(3):
        out_ref[:, i, :, :] = jnp.broadcast_to(
            res_ref[4 * i : 4 * i + 4, :][None], (out_ref.shape[0], 4, 128)
        )


def slots_to_rows(all_ref, mask, at):
    half = all_ref.shape[1]
    lines = at.shape[0]
    here = iota((lines, mask.shape[1]), 1) == at
    rank = jnp.sum(
        jnp.where(here & (mask == 1), rank_in_row(mask) + 1.0, 0.0), axis=1, keepdims=True
    )
    total = jnp.zeros((lines, 12 * 128), F32)
    for c in range(2):
        chosen = (2 * iota((lines, half), 1) + c + 1).astype(F32) == rank
        every = [all_ref[c, :, v // 4, v % 4, :] for v in range(12)]
        total = total + pick_dot(chosen.astype(F32), jnp.concatenate(every, axis=1))
    return total


def band_edges(cols, all_ref, dep_ref, edge_ref, filter_ref, depx_ref, north_ref, south_ref):
    rows = dep_ref.shape[0]
    mask = filter_ref[0:1, :]
    first = cols - 256
    lane = iota((rows, 128), 1)
    depx_ref[:, 0:256] = dep_ref[:, 0:256]
    depx_ref[:, 256:384] = jnp.where(
        (lane == first) | (lane == first + 1), edge_ref[0:rows, :], 0.0
    )
    line = iota((8, 1), 0)
    ends = slots_to_rows(all_ref, mask, jnp.where(line < 4, line, line + (rows - 8)))
    for v in range(12):
        own = ends[:, 128 * v : 128 * v + 128]
        north_ref[4 * v : 4 * v + 4, :] = own[0:4]
        south_ref[4 * v : 4 * v + 4, :] = own[4:8]
    for out_ref, at in ((north_ref, 0), (south_ref, rows - 2)):
        for r in range(2):
            for t in range(3):
                out_ref[48 + 3 * r + t : 49 + 3 * r + t, :] = depx_ref[
                    at + r : at + r + 1, 128 * t : 128 * t + 128
                ]
        out_ref[54:56, :] = jnp.zeros((2, 128), F32)
    north, south = north_ref[...], south_ref[...]
    north_ref[...], south_ref[...] = swap_odd(south, north)


EDGE = 16
SURE = 8


def two_steps(fields, low, weight, terms, dep):
    metric, rotation, valid = terms
    level = fields[3]
    wet = (level > 0).astype(F32)
    share = COURANT * (level / LEVELS)

    def half_step(height, east, north, f):
        height = height + weight * (low[f] - height)
        east = east + weight * (low[f + 1] - east)
        north = north + weight * (low[f + 2] - north)
        middle = valid * (height + COURANT * (metric * lon_diff(east) + lat_diff(north)))
        new_east = east - rotation * north + share * (metric * lon_diff(middle))
        new_north = north + rotation * east + share * lat_diff(middle)
        return middle, new_east, new_north

    middle, east, north = half_step(fields[0], fields[1], fields[2], 0)
    return half_step(middle + dep, wet * east, wet * north, 3)


def own_rows(
    cols,
    all_ref,
    filter_ref,
    cos_ref,
    sin_ref,
    table_ref,
    wide_ref,
    left_ref,
    right_ref,
    weight_ref,
    depx_ref,
    terms_ref,
    low_ref,
    inner_ref,
    stack_ref,
    ext_ref,
):
    mask = filter_ref[0:1, :]
    rows = mask.shape[1]
    band, lon = own_place()
    turn_cos, turn_sin = cos_ref[pl.ds(lon, 1), :], sin_ref[pl.ds(lon, 1), :]
    coef = slots_to_rows(all_ref, mask, iota((rows, 1), 0))
    for f in range(6):
        lines = slice(rows * f, rows * f + rows)
        on_cos = coef[:, 256 * f : 256 * f + 128]
        on_sin = coef[:, 256 * f + 128 : 256 * f + 256]
        stack_ref[lines, 0:128] = on_cos * turn_cos + on_sin * turn_sin
        stack_ref[lines, 128:256] = on_sin * turn_cos - on_cos * turn_sin
    low_ref[...] = tdot(stack_ref[...], table_ref)
    for f in range(4):
        ext_ref[f, :, 0:256] = wide_ref[f, 0:rows, 0:256]
        ext_ref[f, :, 256:384] = third_tile(
            wide_ref[f, 0:rows, 256:384], left_ref[...], right_ref[...], f, cols
        )
    state = two_steps(
        [ext_ref[f] for f in range(4)],
        [low_ref[rows * f : rows * f + rows, :] for f in range(6)],
        weight_ref[0:rows, 0:1],
        row_terms(terms_ref[0:rows, :], band),
        depx_ref[...],
    )
    for i in range(3):
        inner_ref[i] = state[i][SURE : rows - SURE]


def last_stage(
    wide_ref,
    left_ref,
    right_ref,
    corner_left_ref,
    corner_right_ref,
    weight_ref,
    own_ref,
    inner_ref,
    depx_ref,
    second_ref,
    first_ref,
    terms_ref,
    cos_ref,
    sin_ref,
    table_ref,
    h_hbm,
    e_hbm,
    n_hbm,
    stack_ref,
    dep_ref,
    ext_ref,
    h_ref,
    e_ref,
    n_ref,
    below_ref,
    above_ref,
    sems,
):
    rows, cols = h_ref.shape
    ext = rows + 2 * HALO
    band, lon = own_place()
    pairs = ((h_ref, h_hbm), (e_ref, e_hbm), (n_ref, n_hbm))
    spans = (pl.ds(SURE, rows - 2 * SURE), pl.ds(0, SURE), pl.ds(rows - SURE, SURE))
    copies = [
        [
            pltpu.make_async_copy(a.at[span, :], b.at[span, :], sems.at[i, j])
            for j, span in enumerate(spans)
        ]
        for i, (a, b) in enumerate(pairs)
    ]
    for i, (out_ref, _) in enumerate(pairs):
        out_ref[SURE : rows - SURE, :] = inner_ref[i, :, 0:cols]
        copies[i][0].start()
    for f in range(4):
        parts = (
            (slice(0, EDGE), slice(rows - EDGE, rows)),
            (slice(EDGE + 2 * HALO, 2 * EDGE + 2 * HALO), slice(0, EDGE)),
        )
        for to, at in parts:
            ext_ref[f, to, 0:256] = wide_ref[f, at, 0:256]
            ext_ref[f, to, 256:384] = third_tile(
                wide_ref[f, at, 256:384], left_ref[at, :], right_ref[at, :], f, cols
            )
        to = slice(EDGE, EDGE + 2 * HALO)
        lines = slice(2 * HALO * f, 2 * HALO * f + 2 * HALO)
        ext_ref[f, to, 0:256] = wide_ref[f, rows:ext, 0:256]
        ext_ref[f, to, 256:384] = third_tile(
            wide_ref[f, rows:ext, 256:384],
            corner_left_ref[lines, :],
            corner_right_ref[rows + 2 * HALO * f : rows + 2 * HALO * f + 2 * HALO, :],
            f,
            cols,
        )
    below_ref[...], above_ref[...] = swap_odd(first_ref[...], second_ref[...])
    turn_cos, turn_sin = cos_ref[pl.ds(lon, 1), :], sin_ref[pl.ds(lon, 1), :]
    for f in range(6):
        for at, in_ref in ((8 * f, below_ref), (8 * f + 4, above_ref)):
            on_cos = in_ref[8 * f : 8 * f + 4, :]
            on_sin = in_ref[8 * f + 4 : 8 * f + 8, :]
            stack_ref[at : at + 4, 0:128] = on_cos * turn_cos + on_sin * turn_sin
            stack_ref[at : at + 4, 128:256] = on_sin * turn_cos - on_cos * turn_sin
    edges = tdot(stack_ref[...], table_ref)
    low = [
        jnp.concatenate(
            [
                own_ref[rows * f + rows - EDGE : rows * f + rows, :],
                edges[8 * f : 8 * f + 8, :],
                own_ref[rows * f : rows * f + EDGE, :],
            ],
            axis=0,
        )
        for f in range(6)
    ]
    dep_ref[0:EDGE, :] = depx_ref[rows - EDGE : rows, :]
    dep_ref[EDGE : EDGE + 2 * HALO, :] = jnp.zeros((2 * HALO, LANES), F32)
    dep_ref[EDGE + 2 * HALO : 2 * EDGE + 2 * HALO, :] = depx_ref[0:EDGE, :]
    for in_ref, at in ((below_ref, EDGE), (above_ref, EDGE + 2 * HALO - 2)):
        for r in range(2):
            for t in range(3):
                dep_ref[at + r : at + r + 1, 128 * t : 128 * t + 128] = in_ref[
                    48 + 3 * r + t : 49 + 3 * r + t, :
                ]

    def around(ref):
        return jnp.concatenate([ref[rows - EDGE : ext, :], ref[0:EDGE, :]], axis=0)

    state = two_steps(
        [ext_ref[f] for f in range(4)],
        low,
        around(weight_ref)[:, 0:1],
        row_terms(around(terms_ref), band),
        dep_ref[...],
    )
    south, north = slice(EDGE - SURE, EDGE), slice(EDGE + 2 * HALO, EDGE + 2 * HALO + SURE)
    for i, (out_ref, _) in enumerate(pairs):
        out_ref[0:SURE, :] = state[i][north, 0:cols]
        out_ref[rows - SURE : rows, :] = state[i][south, 0:cols]
        copies[i][1].start()
        copies[i][2].start()
    for group in copies:
        for copy in group:
            copy.wait()


def tables(length, cols, devices, rows, bands):
    mode = np.arange(MODES)
    norm = np.where(mode == 0, 1.0 / length, 2.0 / length)
    lane = np.arange(LANES)

    def angle(at, number):
        phase = (at[:, None].astype(np.int64) * number[None, :]) % length
        return phase * (2.0 * math.pi / length)

    inside = (lane < cols)[:, None]
    place = np.where(lane < LANES - HALO, lane, lane - LANES)
    shown = ((lane < cols + HALO) | (lane >= LANES - HALO))[:, None]
    around = angle(place, mode)
    analyse = np.concatenate([np.cos(around) * norm, np.sin(around) * norm], axis=1) * shown
    evaluate = (np.concatenate([np.cos(around), np.sin(around)], axis=1) * shown).T
    wide = np.arange(1, 2 * MODES - 1)
    spot = np.arange(GRID) * (length / GRID)
    gap = spot[None, :] - lane[:, None]
    kernel = np.full((LANES, GRID), 1.0 / length)
    for k in wide:
        kernel += (2.0 / length) * np.cos(2.0 * math.pi / length * k * gap)
    kernel *= inside
    coarse = (np.arange(GRID)[:, None] * mode[None, :]) % GRID * (2.0 * math.pi / GRID)
    to_grid = np.concatenate([np.cos(coarse), np.sin(coarse)], axis=1).T
    part = np.where(mode == 0, 1.0 / GRID, 2.0 / GRID)
    from_grid = np.concatenate([np.cos(coarse) * part, np.sin(coarse) * part], axis=1)
    turn = (np.arange(devices)[:, None] * mode[None, :]) % devices * (2.0 * math.pi / devices)
    slope = np.tile(np.sin(2.0 * math.pi / length * mode)[None, :], (8, 1))
    total = rows * bands
    index = np.arange(rows + 2 * HALO)
    local = np.where(index < rows + HALO, index, index - (rows + 2 * HALO))
    terms = np.zeros((rows + 2 * HALO, 128))
    lines = np.zeros((bands, 256))
    for b in range(bands):
        g = b * rows + local
        phi = (2.0 * ((g + 0.5) / total) - 1.0) * LIMIT
        terms[:, b] = 1.0 / np.cos(phi)
        terms[:, 16 + b] = ROTATION * np.sin(phi)
        terms[:, 32 + b] = (g >= 0) & (g < total)
        lines[b, 0:rows] = terms[0:rows, b]
        lines[b, 128 : 128 + rows] = terms[0:rows, 16 + b]
    made = dict(
        analyse=analyse,
        evaluate=evaluate,
        kernel=kernel,
        to_grid=to_grid,
        from_grid=from_grid,
        cos=np.cos(turn),
        sin=np.sin(turn),
        slope=slope,
        terms=terms,
        lines=lines,
    )
    for name, value in made.items():
        made[name] = value.astype(np.float32)
        if name in ("analyse", "evaluate", "kernel", "to_grid", "from_grid"):
            high = value.astype(ml_dtypes.bfloat16)
            low = (value - high.astype(np.float64)).astype(ml_dtypes.bfloat16)
            made[name] = np.stack([high, low])
    return made


VMEM = pl.BlockSpec(memory_space=pltpu.VMEM)
HBM = pl.BlockSpec(memory_space=pltpu.HBM)


def call(kernel, name, outs, args, scratch=(), direct=(), cost=1.0, outside=False):
    shapes = [jax.ShapeDtypeStruct(shape, F32) for shape in outs]
    specs = [
        HBM if i in direct else VMEM for i in range(len(args))
    ]
    args = [
        pltpu.with_memory_space_constraint(arg, pltpu.HBM) if i in direct else arg
        for i, arg in enumerate(args)
    ]
    held = [pltpu.VMEM(args[i].shape, args[i].dtype) for i in direct]
    held += [pltpu.SemaphoreType.DMA((len(direct),))] if direct else []
    return pl.pallas_call(
        kernel,
        name=name,
        out_shape=shapes,
        in_specs=specs,
        out_specs=[HBM if outside else VMEM] * len(shapes),
        scratch_shapes=held + [
            pltpu.VMEM(shape, F32) if isinstance(shape, tuple) else shape for shape in scratch
        ],
        cost_estimate=pl.CostEstimate(
            flops=int(cost * 1e9), bytes_accessed=int(cost * 2e6), transcendentals=0
        ),
        compiler_params=pltpu.CompilerParams(
            vmem_limit_bytes=40 * 2**20
        ),
    )(*args)


LON = ("z", "core")


def on_device(
    back_height,
    back_east,
    back_north,
    obs_values,
    obs_owner,
    obs_row,
    obs_count,
    polar_mask,
    keep_share,
    depth_level,
):
    rows, cols = back_height.shape
    bands, devices = lax.axis_size("band"), lax.axis_size(LON)
    half = devices // 2
    number, width = obs_values.shape
    ext = rows + 2 * HALO
    made = tables(cols * devices, cols, devices, rows, bands)

    def send(value, axis, shift, closed):
        count = lax.axis_size(axis)
        pairs = [(i, (i + shift) % count) for i in range(count) if closed or 0 <= i + shift < count]
        return lax.ppermute(value, axis, pairs)

    even = [(i, i ^ 1) for i in range(bands)]
    odd = [(i, ((i + 1) ^ 1) - 1) for i in range(1, bands - 1)]
    fields, west, east, north, south, kept, marks = call(
        pack_tile,
        "pack_tile",
        [(4, rows, LANES), (rows, 128), (rows, 128)] + [(4 * HALO, LANES)] * 2 + [(8, rows), (8, number)],
        (
            back_height,
            back_east,
            back_north,
            depth_level,
            polar_mask.reshape(1, rows),
            keep_share.reshape(1, rows),
            obs_owner.reshape(1, number),
            obs_row.reshape(1, number),
            obs_count.reshape(1, number),
        ),
        direct=range(9),
    )
    below, above = lax.ppermute(north, "band", even), lax.ppermute(south, "band", odd)
    right, left = send(west, LON, -1, True), send(east, LON, 1, True)
    near, far, placed = call(
        pack_observations,
        "pack_observations",
        [(half, 32, 128), (half, 32, 128), (devices, 256)],
        (obs_values, marks, kept, made["cos"], made["sin"], made["analyse"]),
        cost=3.0,
    )
    wide, weight, corner_west, corner_east, mine, other = call(
        lambda *refs: partial_sums(cols, *refs),
        "partial_sums",
        [(4, ext, LANES), (ext, 128)] + [(8 * HALO, 128)] * 2 + [(half, 56, 128)] * 2,
        (
            fields,
            left,
            right,
            above,
            below,
            kept,
            made["terms"],
            made["cos"],
            made["sin"],
            made["analyse"],
            made["kernel"],
            placed,
            near,
            far,
        ),
        scratch=[pltpu.VMEM((n * devices, LANES), jnp.bfloat16) for n in (8, 8, 2)],
    )
    swapped = lax.all_gather(other, "core", axis=0, tiled=False)
    (joined,) = call(
        join, "join", [(half, 37, 2, 128)], (mine, swapped)
    )
    owned = lax.all_to_all(joined, "z", split_axis=0, concat_axis=0, tiled=True)
    (spread,) = call(
        own_row,
        "own_row",
        [(half, 3, 4, 128)],
        (
            owned,
            kept,
            made["lines"],
            made["slope"],
            made["to_grid"],
            made["from_grid"],
        ),
        scratch=[(8, 256), (8, GRID), (12, 128), (24, 128)],
    )
    shared = lax.all_to_all(spread, "z", split_axis=0, concat_axis=0, tiled=True)
    everyone = lax.all_gather(shared, "core", axis=0, tiled=False)
    dep, west = call(
        unpack_observations,
        "unpack_observations",
        [(rows, LANES), (rows + 8 * HALO, 128)],
        (owned, corner_west),
        scratch=[(half, 48, 128)],
    )
    corner_east = lax.optimization_barrier((corner_east, spread))[0]
    corner_right, corner_left = send(west, LON, -1, True), send(corner_east, LON, 1, True)
    dep, corner_left = lax.optimization_barrier((dep, corner_left))
    depx, north, south = call(
        lambda *refs: band_edges(cols, *refs),
        "band_edges",
        [(rows, LANES), (56, 128), (56, 128)],
        (everyone, dep, corner_right, kept),
    )
    below, above = lax.ppermute(north, "band", even), lax.ppermute(south, "band", odd)
    own, inner = call(
        lambda *refs: own_rows(cols, *refs),
        "own_rows",
        [(6 * rows, LANES), (3, rows - 2 * SURE, LANES)],
        (
            everyone,
            kept,
            made["cos"],
            made["sin"],
            made["evaluate"],
            wide,
            left,
            right,
            weight,
            depx,
            made["terms"],
        ),
        scratch=[(6 * rows, 256), (4, rows, LANES)],
    )
    edge = 2 * EDGE + 2 * HALO
    return tuple(
        call(
            last_stage,
            "last_stage",
            [(rows, cols)] * 3,
            (
                wide,
                left,
                right,
                corner_left,
                corner_right,
                weight,
                own,
                inner,
                depx,
                above,
                below,
                made["terms"],
                made["cos"],
                made["sin"],
                made["evaluate"],
            ),
            scratch=[(48, 256), (edge, LANES), (4, edge, LANES)]
            + [(rows, cols)] * 3
            + [(56, 128)] * 2
            + [pltpu.SemaphoreType.DMA((3, 3))],
            outside=True,
        )
    )


def solution(mesh):
    placed = (
        P("band", LON),
        P("band", LON),
        P("band", LON),
        P(("band", *LON), None),
        P(("band", *LON), None),
        P(("band", *LON)),
        P(("band", *LON)),
        P("band"),
        P("band"),
        P("band", LON),
    )
    fine = jax.sharding.Mesh(
        mesh.devices.reshape(mesh.devices.shape[0], -1, 2), ("band", *LON)
    )
    return jax.shard_map(
        on_device,
        mesh=fine,
        in_specs=placed,
        out_specs=(P("band", LON), P("band", LON), P("band", LON)),
        check_vma=False,
    )
```

```python
import math

import jax
import jax.numpy as jnp
import ml_dtypes
import numpy as np
from jax import lax
from jax.experimental import pallas as pl
from jax.experimental.pallas import tpu as pltpu
from jax.sharding import PartitionSpec as P

MODES = 128
LEVELS = 50
COURANT = 0.25
ROTATION = 0.4
LIMIT = 1.3089969389957472
CAP = 12
LANES = 384
GRID = 512
HALO = 4
F32 = jnp.float32


def hdot(left, right):
    return jnp.dot(left, right, precision=lax.Precision.HIGHEST, preferred_element_type=F32)


def halves_of(value):
    high = value.astype(jnp.bfloat16)
    return high, (value - high.astype(F32)).astype(jnp.bfloat16)


def bdot(left, right):
    return jnp.dot(left, right, preferred_element_type=F32)


def pick_dot(chosen, value):
    high, low = halves_of(value)
    rest = (value - high.astype(F32) - low.astype(F32)).astype(jnp.bfloat16)
    chosen = chosen.astype(jnp.bfloat16)
    return bdot(chosen, high) + bdot(chosen, low) + bdot(chosen, rest)


def tdot(left, table_ref):
    high, low = halves_of(left)
    return bdot(high, table_ref[0]) + bdot(low, table_ref[0]) + bdot(high, table_ref[1])


def tdot_few(left, table_ref):
    lines = left.shape[0]
    high = left.astype(jnp.bfloat16).astype(F32)
    both = jnp.concatenate([high, left - high], axis=0).astype(jnp.bfloat16)
    first = bdot(both, table_ref[0])
    return first[0:lines] + first[lines:] + bdot(left.astype(jnp.bfloat16), table_ref[1])


def mdot(left, right):
    return jnp.dot(left, right, precision=lax.Precision.HIGH, preferred_element_type=F32)


def iota(shape, dim):
    return lax.broadcasted_iota(jnp.int32, shape, dim)


def own_place():
    return lax.axis_index("band"), 2 * lax.axis_index("z") + lax.axis_index("core")


def swap_odd(first, second):
    even = lax.axis_index("band") % 2 == 0
    return jnp.where(even, first, second), jnp.where(even, second, first)


def to_col(row):
    size = row.shape[1]
    same = iota((size, size), 0) == iota((size, size), 1)
    return jnp.sum(jnp.where(same, row, jnp.zeros_like(row)), axis=1, keepdims=True)


def to_row(col):
    size = col.shape[0]
    same = iota((size, size), 0) == iota((size, size), 1)
    return jnp.sum(jnp.where(same, col, jnp.zeros_like(col)), axis=0, keepdims=True)


def lon_diff(field):
    width = field.shape[1]
    return 0.5 * (pltpu.roll(field, width - 1, 1) - pltpu.roll(field, 1, 1))


def lat_diff(field):
    rows = field.shape[0]
    return 0.5 * (pltpu.roll(field, rows - 1, 0) - pltpu.roll(field, 1, 0))


def rank_in_row(mask_row):
    size = mask_row.shape[1]
    before = iota((size, size), 0) < iota((size, size), 1)
    return jnp.sum(jnp.where(before, to_col(mask_row), 0), axis=0, keepdims=True)


def slot_rows(mask_row, core, devices):
    rows = mask_row.shape[1]
    half = devices // 2
    line = iota((devices, rows), 0)
    slot = jnp.where(line < half, 2 * line + core, 2 * (line - half) + 1 - core)
    hit = (slot == rank_in_row(mask_row)) & (mask_row == 1)
    return hit.astype(F32)


WEIGHT_LANE = 300 - 256


def pack_tile(
    h_hbm,
    e_hbm,
    n_hbm,
    d_hbm,
    mask_hbm,
    keep_hbm,
    owner_hbm,
    row_hbm,
    count_hbm,
    fields_ref,
    west_ref,
    east_ref,
    north_ref,
    south_ref,
    filter_ref,
    marks_ref,
    h_ref,
    e_ref,
    n_ref,
    d_ref,
    mask_ref,
    keep_ref,
    owner_ref,
    row_ref,
    count_ref,
    sems,
):
    pairs = (
        (h_hbm, h_ref),
        (e_hbm, e_ref),
        (n_hbm, n_ref),
        (d_hbm, d_ref),
        (mask_hbm, mask_ref),
        (keep_hbm, keep_ref),
        (owner_hbm, owner_ref),
        (row_hbm, row_ref),
        (count_hbm, count_ref),
    )
    copies = [pltpu.make_async_copy(a, b, sems.at[i]) for i, (a, b) in enumerate(pairs)]
    for copy in copies:
        copy.start()
    fields_ref[...] = jnp.zeros(fields_ref.shape, F32)
    for copy in copies:
        copy.wait()
    rows, cols = h_ref.shape
    filter_ref[0:1, :] = mask_ref[...].astype(F32)
    filter_ref[1:2, :] = keep_ref[...]
    filter_ref[2:8, :] = jnp.zeros((6, rows), F32)
    for i, in_ref in enumerate((owner_ref, row_ref, count_ref)):
        marks_ref[i : i + 1, :] = in_ref[...].astype(F32)
    marks_ref[3:8, :] = jnp.zeros((5, marks_ref.shape[1]), F32)
    weight = to_col(mask_ref[...].astype(F32) * (1.0 - keep_ref[...]))
    level = d_ref[...].astype(F32)
    wet = (level > 0).astype(F32)
    values = (h_ref[...], wet * e_ref[...], wet * n_ref[...], level)
    lane = iota((rows, 128), 1)
    west = jnp.zeros(lane.shape, F32)
    east = jnp.zeros(lane.shape, F32)
    last = cols - HALO - 256
    for f, value in enumerate(values):
        fields_ref[f, :, 0:cols] = value
        inside = (lane >= HALO * f) & (lane < HALO * f + HALO)
        head = fields_ref[f, :, 0:128]
        tail = fields_ref[f, :, 256:384]
        if f:
            head = pltpu.roll(head, HALO * f, 1)
        west = jnp.where(inside, head, west)
        east = jnp.where(inside, pltpu.roll(tail, (HALO * f - last) % 128, 1), east)
        for out_ref, at in ((north_ref, 0), (south_ref, rows - HALO)):
            span = slice(at, at + HALO)
            lines = slice(HALO * f, HALO * f + HALO)
            edge = fields_ref[f, span, 256:384]
            if f == 3:
                edge = jnp.where(iota(edge.shape, 1) == WEIGHT_LANE, weight[span, :], edge)
            out_ref[lines, 0:256] = fields_ref[f, span, 0:256]
            out_ref[lines, 256:384] = edge
    west_ref[...] = west
    east_ref[...] = east
    north, south = north_ref[...], south_ref[...]
    north_ref[...], south_ref[...] = swap_odd(north, south)


def third_tile(tail, left, right, f, cols):
    lane = iota(tail.shape, 1)
    first = cols - 256
    shifted = pltpu.roll(right, (first - HALO * f) % 128, 1)
    tail = jnp.where((lane >= first) & (lane < first + HALO), shifted, tail)
    shifted = pltpu.roll(left, (128 - HALO - HALO * f) % 128, 1)
    return jnp.where(lane >= 128 - HALO, shifted, tail)


def row_terms(terms, band):
    lane = iota(terms.shape, 1)
    return [
        jnp.sum(jnp.where(lane == band + 16 * i, terms, 0.0), axis=1, keepdims=True)
        for i in range(3)
    ]


def partial_sums(
    cols,
    fields_ref,
    left_ref,
    right_ref,
    above_ref,
    below_ref,
    filter_ref,
    terms_ref,
    cos_ref,
    sin_ref,
    table_ref,
    kernel_ref,
    placed_ref,
    near_ref,
    far_ref,
    ext_ref,
    weight_ref,
    west_ref,
    east_ref,
    mine_ref,
    other_ref,
    high_ref,
    low_ref,
    cells_ref,
):
    rows = fields_ref.shape[1]
    ext = rows + 2 * HALO
    devices = cos_ref.shape[0]
    half = devices // 2
    band, lon = own_place()
    below, above = swap_odd(below_ref[...], above_ref[...])
    for f in range(4):
        ext_ref[f, 0:rows, :] = fields_ref[f]
        ext_ref[f, rows : rows + HALO, :] = below[HALO * f : HALO * f + HALO]
        ext_ref[f, rows + HALO : ext, :] = above[HALO * f : HALO * f + HALO]
    edge = ext_ref[3, rows:ext, 256:384]
    marked = iota(edge.shape, 1) == WEIGHT_LANE
    mask, keep = filter_ref[0:1, :], filter_ref[1:2, :]
    weight_ref[0:rows, :] = jnp.broadcast_to(to_col(mask * (1.0 - keep)), (rows, 128))
    weight_ref[rows:ext, :] = jnp.broadcast_to(
        jnp.sum(jnp.where(marked, edge, 0.0), axis=1, keepdims=True), (2 * HALO, 128)
    )
    ext_ref[3, rows:ext, 256:384] = jnp.where(marked, 0.0, edge)
    corner = iota((2 * HALO, 128), 1)
    last = cols - HALO - 256
    for f in range(4):
        lines = slice(2 * HALO * f, 2 * HALO * f + 2 * HALO)
        inside = (corner >= HALO * f) & (corner < HALO * f + HALO)
        head = ext_ref[f, rows:ext, 0:128]
        tail = ext_ref[f, rows:ext, 256:384]
        if f:
            head = pltpu.roll(head, HALO * f, 1)
        west_ref[lines, :] = jnp.where(inside, head, 0.0)
        east_ref[lines, :] = jnp.where(inside, pltpu.roll(tail, (HALO * f - last) % 128, 1), 0.0)
    weight = weight_ref[:, 0:1]
    rest = 1.0 - weight
    metric, rotation, valid = row_terms(terms_ref[...], band)
    metric = metric * valid
    height, east, north = ext_ref[0], ext_ref[1], ext_ref[2]
    ext_ref[3, 0:rows, 256:384] = third_tile(
        ext_ref[3, 0:rows, 256:384], left_ref[...], right_ref[...], 3, cols
    )
    share = ext_ref[3] / LEVELS
    low_height = weight * height + COURANT * (
        metric * lon_diff(weight * east) + lat_diff(weight * north)
    )
    low_height = valid * low_height
    east_rest, north_rest = rest * east, rest * north
    middle = valid * (
        rest * height + COURANT * (metric * lon_diff(east_rest) + lat_diff(north_rest))
    )
    new_east = east_rest - rotation * north_rest + COURANT * share * metric * lon_diff(middle)
    new_north = north_rest + rotation * east_rest + COURANT * share * lat_diff(middle)
    chosen = slot_rows(mask, own_place()[1] % 2, devices).astype(jnp.bfloat16)
    sources = (height, east, north, low_height, lat_diff(low_height), middle, new_east, new_north)
    for v, field in enumerate(sources):
        lines = slice(devices * v, devices * v + devices)
        high, low = halves_of(field[0:rows, :])
        high_ref[lines, :] = bdot(chosen, high).astype(jnp.bfloat16)
        low_ref[lines, :] = bdot(chosen, low).astype(jnp.bfloat16)
    mine_ref[:, 24:56, :] = near_ref[...]
    other_ref[:, 24:56, :] = far_ref[...]
    level = ext_ref[3, 0:rows, :]
    for c, cells in enumerate(((level > 0).astype(F32), level)):
        cells_ref[devices * c : devices * c + devices, :] = bdot(
            chosen, cells.astype(jnp.bfloat16)
        ).astype(jnp.bfloat16)
    sums = bdot(high_ref[...], table_ref[0]) + bdot(low_ref[...], table_ref[0])
    sums = sums + bdot(high_ref[...], table_ref[1])
    turn_cos, turn_sin = cos_ref[pl.ds(lon, 1), :], sin_ref[pl.ds(lon, 1), :]
    for v in range(len(sources)):
        lines = slice(devices * v, devices * v + devices)
        on_cos, on_sin = sums[lines, 0:128], sums[lines, 128:256]
        all_cos = on_cos * turn_cos - on_sin * turn_sin
        all_sin = on_sin * turn_cos + on_cos * turn_sin
        if v == 5:
            all_cos = all_cos + placed_ref[:, 0:128]
            all_sin = all_sin + placed_ref[:, 128:256]
        for i, value in enumerate((all_cos, all_sin)):
            mine_ref[:, 2 * v + i, :] = value[0:half]
            other_ref[:, 2 * v + i, :] = value[half:devices]
    spread = bdot(cells_ref[...], kernel_ref[0]) + bdot(cells_ref[...], kernel_ref[1])
    spread = pltpu.roll(spread, lon * (GRID // devices), 1)
    for c in range(2):
        for i in range(4):
            part = spread[devices * c : devices * c + devices, 128 * i : 128 * i + 128]
            at = 16 + 4 * c + i
            mine_ref[:, at, :] = part[0:half]
            other_ref[:, at, :] = part[half:devices]


def pack_observations(
    values_ref,
    marks_ref,
    filter_ref,
    cos_ref,
    sin_ref,
    table_ref,
    near_ref,
    far_ref,
    placed_ref,
):
    number, width = values_ref.shape
    half = near_ref.shape[0]
    devices = 2 * half
    core = own_place()[1] % 2
    lengths = to_col(marks_ref[2:3, :])
    values = jnp.where(iota((number, width), 1).astype(F32) < lengths, values_ref[...], 0.0)
    high, low = halves_of(values)
    rest = (values - high.astype(F32) - low.astype(F32)).astype(jnp.bfloat16)
    owner_row = marks_ref[0:1, :].astype(jnp.int32)
    owner_col = to_col(owner_row)
    same = owner_col == owner_row
    before = same & (iota((number, number), 0) < iota((number, number), 1))
    arrival_row = jnp.sum(before.astype(jnp.int32), axis=0, keepdims=True)
    after = same & (iota((number, number), 0) > iota((number, number), 1))
    arrival_col = jnp.sum(after.astype(jnp.int32), axis=1, keepdims=True)
    chip_row, core_row = owner_row // 2, owner_row % 2
    target = chip_row * 16 + arrival_row
    label = marks_ref[1:2, :]
    arrived = (iota((number, 128), 1) == arrival_col).astype(F32).astype(jnp.bfloat16)
    for out_ref, side in ((near_ref, core), (far_ref, 1 - core)):
        goes = core_row == side
        sent = ((iota((16 * half, number), 0) == target) & goes).astype(F32)
        sent = sent.astype(jnp.bfloat16)
        block = bdot(sent, high) + bdot(sent, low) + bdot(sent, rest)
        block = block.reshape(half, 16, width)
        out_ref[:, 0:CAP, :] = block[:, 0:CAP, 0:128]
        out_ref[:, CAP : 2 * CAP, :] = block[:, 0:CAP, 128:256]
        named = ((iota((half, number), 0) == chip_row) & goes).astype(F32) * label
        out_ref[:, 2 * CAP : 32, :] = jnp.zeros((half, 32 - 2 * CAP, 128), F32)
        out_ref[:, 2 * CAP, :] = bdot(named.astype(jnp.bfloat16), arrived)
    head = table_ref[0, 0:width, :]
    sums = bdot(high, head) + bdot(low, head) + bdot(high, table_ref[1, 0:width, :])
    whose = (iota((number, devices), 1) == owner_col).astype(F32)
    turn_cos, turn_sin = pick_dot(whose, cos_ref[...]), pick_dot(whose, sin_ref[...])
    on_cos, on_sin = sums[:, 0:128], sums[:, 128:256]
    all_cos = on_cos * turn_cos - on_sin * turn_sin
    all_sin = on_sin * turn_cos + on_cos * turn_sin
    mask = filter_ref[0:1, :]
    rows = mask.shape[1]
    in_row = (iota((rows, number), 0).astype(F32) == label).astype(F32)
    slots = slot_rows(mask, core, devices).astype(jnp.bfloat16)
    chosen = bdot(slots, in_row.astype(jnp.bfloat16))
    placed_ref[:, 0:128] = pick_dot(chosen, all_cos)
    placed_ref[:, 128:256] = pick_dot(chosen, all_sin)


def join(mine_ref, both_ref, out_ref):
    other = 1 - own_place()[1] % 2
    for i in range(12):
        pair = slice(2 * i, 2 * i + 2)
        out_ref[:, i, :, :] = mine_ref[:, pair, :] + both_ref[other, :, pair, :]
    for i in range(12, 24):
        out_ref[:, i, :, :] = mine_ref[:, 2 * i : 2 * i + 2, :]
        out_ref[:, i + 12, :, :] = both_ref[other, :, 2 * i : 2 * i + 2, :]
    out_ref[:, 36, 0, :] = mine_ref[:, 48, :]
    out_ref[:, 36, 1, :] = both_ref[other, :, 48, :]


def unpack_observations(in_ref, corner_ref, dep_ref, west_ref, data_ref):
    half = in_ref.shape[0]
    rows = dep_ref.shape[0]
    lines = 4 * CAP
    total = half * lines
    spot = iota((128, total), 1) % lines
    label_row = jnp.zeros((1, total), F32)
    own = iota((half, total), 1) // lines == iota((half, total), 0)
    for s in range(2):
        here = (spot // (2 * CAP) == s) & (spot % CAP == iota((128, total), 0))
        across = bdot(
            in_ref[:, 36, s, :].astype(jnp.bfloat16), here.astype(F32).astype(jnp.bfloat16)
        )
        label_row = label_row + jnp.sum(jnp.where(own, across, 0.0), axis=0, keepdims=True)
    line = iota((rows, total), 1) % lines
    hit = iota((rows, total), 0).astype(F32) == label_row
    for i in range(2 * CAP):
        data_ref[:, 2 * i : 2 * i + 2, :] = in_ref[:, 12 + i, :, :]
    data = data_ref[...].reshape(total, 128)
    for i in range(2):
        side = (hit & ((line // CAP) % 2 == i)).astype(F32)
        dep_ref[:, 128 * i : 128 * i + 128] = pick_dot(side, data)
    dep_ref[:, 256:384] = jnp.zeros((rows, 128), F32)
    west_ref[0:rows, :] = pltpu.roll(dep_ref[:, 0:128], 14, 1)
    west_ref[rows : rows + corner_ref.shape[0], :] = corner_ref[...]


def own_row(
    in_ref,
    filter_ref,
    lines_ref,
    slope_ref,
    to_grid_ref,
    from_grid_ref,
    out_ref,
    left_ref,
    grid_ref,
    res_ref,
    sum_ref,
):
    band, lon = own_place()
    pairs = in_ref[0, 0:12, :, :]
    for i in range(1, in_ref.shape[0]):
        pairs = pairs + in_ref[i, 0:12, :, :]
    for i in range(12):
        sum_ref[2 * i : 2 * i + 2, :] = pairs[i]
    sums = sum_ref[...]
    mask, keep = filter_ref[0:1, :], filter_ref[1:2, :]
    chosen = ((rank_in_row(mask) == lon) & (mask == 1)).astype(F32)

    def pick(row):
        return jnp.sum(chosen * row, axis=1, keepdims=True)

    rows = mask.shape[1]
    weight = pick(1.0 - keep)
    both = lines_ref[pl.ds(band, 1), :]
    metric = pick(both[:, 0:rows])
    rotation = pick(both[:, 128 : 128 + rows])

    def line(i):
        return sums[i : i + 1, :]

    slope = slope_ref[0:1, :]
    left_ref[...] = jnp.zeros(left_ref.shape, F32)
    pairs = (
        (weight * (line(2) - rotation * line(4)), weight * (line(3) - rotation * line(5))),
        (metric * slope * line(7), -metric * slope * line(6)),
        (weight * (line(4) + rotation * line(2)), weight * (line(5) + rotation * line(3))),
        (line(8), line(9)),
    )
    for i, (on_cos, on_sin) in enumerate(pairs):
        left_ref[i : i + 1, 0:128] = on_cos
        left_ref[i : i + 1, 128:256] = on_sin
    at = tdot_few(left_ref[...], to_grid_ref)
    wet = jnp.concatenate([line(16), line(17), line(18), line(19)], axis=1)
    share = (COURANT / LEVELS) * jnp.concatenate([line(20), line(21), line(22), line(23)], axis=1)
    grid_ref[...] = jnp.zeros(grid_ref.shape, F32)
    grid_ref[0:1, :] = wet * at[0:1] + share * at[1:2]
    grid_ref[1:2, :] = wet * at[2:3] + share * at[3:4]
    back = tdot_few(grid_ref[...], from_grid_ref)
    res_ref[0:6, :] = sums[0:6]
    res_ref[6:8, :] = sums[10:12] + sums[6:8]
    for i in range(2):
        res_ref[8 + 2 * i : 9 + 2 * i, :] = line(12 + 2 * i) + back[i : i + 1, 0:128]
        res_ref[9 + 2 * i : 10 + 2 * i, :] = line(13 + 2 * i) + back[i : i + 1, 128:256]
    for i in range(3):
        out_ref[:, i, :, :] = jnp.broadcast_to(
            res_ref[4 * i : 4 * i + 4, :][None], (out_ref.shape[0], 4, 128)
        )


def slots_to_rows(all_ref, mask, at):
    half = all_ref.shape[1]
    lines = at.shape[0]
    here = iota((lines, mask.shape[1]), 1) == at
    rank = jnp.sum(
        jnp.where(here & (mask == 1), rank_in_row(mask) + 1.0, 0.0), axis=1, keepdims=True
    )
    total = jnp.zeros((lines, 12 * 128), F32)
    for c in range(2):
        chosen = (2 * iota((lines, half), 1) + c + 1).astype(F32) == rank
        every = [all_ref[c, :, v // 4, v % 4, :] for v in range(12)]
        total = total + pick_dot(chosen.astype(F32), jnp.concatenate(every, axis=1))
    return total


def band_edges(cols, all_ref, dep_ref, edge_ref, filter_ref, depx_ref, north_ref, south_ref):
    rows = dep_ref.shape[0]
    mask = filter_ref[0:1, :]
    first = cols - 256
    lane = iota((rows, 128), 1)
    depx_ref[:, 0:256] = dep_ref[:, 0:256]
    depx_ref[:, 256:384] = jnp.where(
        (lane == first) | (lane == first + 1), edge_ref[0:rows, :], 0.0
    )
    line = iota((8, 1), 0)
    ends = slots_to_rows(all_ref, mask, jnp.where(line < 4, line, line + (rows - 8)))
    for v in range(12):
        own = ends[:, 128 * v : 128 * v + 128]
        north_ref[4 * v : 4 * v + 4, :] = own[0:4]
        south_ref[4 * v : 4 * v + 4, :] = own[4:8]
    for out_ref, at in ((north_ref, 0), (south_ref, rows - 2)):
        for r in range(2):
            for t in range(3):
                out_ref[48 + 3 * r + t : 49 + 3 * r + t, :] = depx_ref[
                    at + r : at + r + 1, 128 * t : 128 * t + 128
                ]
        out_ref[54:56, :] = jnp.zeros((2, 128), F32)
    north, south = north_ref[...], south_ref[...]
    north_ref[...], south_ref[...] = swap_odd(north, south)


EDGE = 16
SURE = 8


def two_steps(fields, low, weight, terms, dep):
    metric, rotation, valid = terms
    level = fields[3]
    wet = (level > 0).astype(F32)
    share = COURANT * (level / LEVELS)

    def half_step(height, east, north, f):
        height = height + weight * (low[f] - height)
        east = east + weight * (low[f + 1] - east)
        north = north + weight * (low[f + 2] - north)
        middle = valid * (height + COURANT * (metric * lon_diff(east) + lat_diff(north)))
        new_east = east - rotation * north + share * (metric * lon_diff(middle))
        new_north = north + rotation * east + share * lat_diff(middle)
        return middle, new_east, new_north

    middle, east, north = half_step(fields[0], fields[1], fields[2], 0)
    return half_step(middle + dep, wet * east, wet * north, 3)


def own_rows(
    cols,
    all_ref,
    filter_ref,
    cos_ref,
    sin_ref,
    table_ref,
    wide_ref,
    left_ref,
    right_ref,
    weight_ref,
    depx_ref,
    terms_ref,
    low_ref,
    inner_ref,
    stack_ref,
    ext_ref,
):
    mask = filter_ref[0:1, :]
    rows = mask.shape[1]
    band, lon = own_place()
    turn_cos, turn_sin = cos_ref[pl.ds(lon, 1), :], sin_ref[pl.ds(lon, 1), :]
    coef = slots_to_rows(all_ref, mask, iota((rows, 1), 0))
    for f in range(6):
        lines = slice(rows * f, rows * f + rows)
        on_cos = coef[:, 256 * f : 256 * f + 128]
        on_sin = coef[:, 256 * f + 128 : 256 * f + 256]
        stack_ref[lines, 0:128] = on_cos * turn_cos + on_sin * turn_sin
        stack_ref[lines, 128:256] = on_sin * turn_cos - on_cos * turn_sin
    low_ref[...] = tdot(stack_ref[...], table_ref)
    for f in range(4):
        ext_ref[f, :, 0:256] = wide_ref[f, 0:rows, 0:256]
        ext_ref[f, :, 256:384] = third_tile(
            wide_ref[f, 0:rows, 256:384], left_ref[...], right_ref[...], f, cols
        )
    state = two_steps(
        [ext_ref[f] for f in range(4)],
        [low_ref[rows * f : rows * f + rows, :] for f in range(6)],
        weight_ref[0:rows, 0:1],
        row_terms(terms_ref[0:rows, :], band),
        depx_ref[...],
    )
    for i in range(3):
        inner_ref[i] = state[i][SURE : rows - SURE]


def last_stage(
    wide_ref,
    left_ref,
    right_ref,
    corner_left_ref,
    corner_right_ref,
    weight_ref,
    own_ref,
    inner_ref,
    depx_ref,
    second_ref,
    first_ref,
    terms_ref,
    cos_ref,
    sin_ref,
    table_ref,
    h_hbm,
    e_hbm,
    n_hbm,
    stack_ref,
    dep_ref,
    ext_ref,
    h_ref,
    e_ref,
    n_ref,
    below_ref,
    above_ref,
    sems,
):
    rows, cols = h_ref.shape
    ext = rows + 2 * HALO
    band, lon = own_place()
    pairs = ((h_ref, h_hbm), (e_ref, e_hbm), (n_ref, n_hbm))
    spans = (pl.ds(SURE, rows - 2 * SURE), pl.ds(0, SURE), pl.ds(rows - SURE, SURE))
    copies = [
        [
            pltpu.make_async_copy(a.at[span, :], b.at[span, :], sems.at[i, j])
            for j, span in enumerate(spans)
        ]
        for i, (a, b) in enumerate(pairs)
    ]
    for i, (out_ref, _) in enumerate(pairs):
        out_ref[SURE : rows - SURE, :] = inner_ref[i, :, 0:cols]
        copies[i][0].start()
    for f in range(4):
        parts = (
            (slice(0, EDGE), slice(rows - EDGE, rows)),
            (slice(EDGE + 2 * HALO, 2 * EDGE + 2 * HALO), slice(0, EDGE)),
        )
        for to, at in parts:
            ext_ref[f, to, 0:256] = wide_ref[f, at, 0:256]
            ext_ref[f, to, 256:384] = third_tile(
                wide_ref[f, at, 256:384], left_ref[at, :], right_ref[at, :], f, cols
            )
        to = slice(EDGE, EDGE + 2 * HALO)
        lines = slice(2 * HALO * f, 2 * HALO * f + 2 * HALO)
        ext_ref[f, to, 0:256] = wide_ref[f, rows:ext, 0:256]
        ext_ref[f, to, 256:384] = third_tile(
            wide_ref[f, rows:ext, 256:384],
            corner_left_ref[lines, :],
            corner_right_ref[rows + 2 * HALO * f : rows + 2 * HALO * f + 2 * HALO, :],
            f,
            cols,
        )
    below_ref[...], above_ref[...] = swap_odd(first_ref[...], second_ref[...])
    turn_cos, turn_sin = cos_ref[pl.ds(lon, 1), :], sin_ref[pl.ds(lon, 1), :]
    for f in range(6):
        for at, in_ref in ((8 * f, below_ref), (8 * f + 4, above_ref)):
            on_cos = in_ref[8 * f : 8 * f + 4, :]
            on_sin = in_ref[8 * f + 4 : 8 * f + 8, :]
            stack_ref[at : at + 4, 0:128] = on_cos * turn_cos + on_sin * turn_sin
            stack_ref[at : at + 4, 128:256] = on_sin * turn_cos - on_cos * turn_sin
    edges = tdot(stack_ref[...], table_ref)
    low = [
        jnp.concatenate(
            [
                own_ref[rows * f + rows - EDGE : rows * f + rows, :],
                edges[8 * f : 8 * f + 8, :],
                own_ref[rows * f : rows * f + EDGE, :],
            ],
            axis=0,
        )
        for f in range(6)
    ]
    dep_ref[0:EDGE, :] = depx_ref[rows - EDGE : rows, :]
    dep_ref[EDGE : EDGE + 2 * HALO, :] = jnp.zeros((2 * HALO, LANES), F32)
    dep_ref[EDGE + 2 * HALO : 2 * EDGE + 2 * HALO, :] = depx_ref[0:EDGE, :]
    for in_ref, at in ((below_ref, EDGE), (above_ref, EDGE + 2 * HALO - 2)):
        for r in range(2):
            for t in range(3):
                dep_ref[at + r : at + r + 1, 128 * t : 128 * t + 128] = in_ref[
                    48 + 3 * r + t : 49 + 3 * r + t, :
                ]

    def around(ref):
        return jnp.concatenate([ref[rows - EDGE : ext, :], ref[0:EDGE, :]], axis=0)

    state = two_steps(
        [ext_ref[f] for f in range(4)],
        low,
        around(weight_ref)[:, 0:1],
        row_terms(around(terms_ref), band),
        dep_ref[...],
    )
    south, north = slice(EDGE - SURE, EDGE), slice(EDGE + 2 * HALO, EDGE + 2 * HALO + SURE)
    for i, (out_ref, _) in enumerate(pairs):
        out_ref[0:SURE, :] = state[i][north, 0:cols]
        out_ref[rows - SURE : rows, :] = state[i][south, 0:cols]
        copies[i][1].start()
        copies[i][2].start()
    for group in copies:
        for copy in group:
            copy.wait()


def tables(length, cols, devices, rows, bands):
    mode = np.arange(MODES)
    norm = np.where(mode == 0, 1.0 / length, 2.0 / length)
    lane = np.arange(LANES)

    def angle(at, number):
        phase = (at[:, None].astype(np.int64) * number[None, :]) % length
        return phase * (2.0 * math.pi / length)

    inside = (lane < cols)[:, None]
    place = np.where(lane < LANES - HALO, lane, lane - LANES)
    shown = ((lane < cols + HALO) | (lane >= LANES - HALO))[:, None]
    around = angle(place, mode)
    analyse = np.concatenate([np.cos(around) * norm, np.sin(around) * norm], axis=1) * shown
    evaluate = (np.concatenate([np.cos(around), np.sin(around)], axis=1) * shown).T
    wide = np.arange(1, 2 * MODES - 1)
    spot = np.arange(GRID) * (length / GRID)
    gap = spot[None, :] - lane[:, None]
    kernel = np.full((LANES, GRID), 1.0 / length)
    for k in wide:
        kernel += (2.0 / length) * np.cos(2.0 * math.pi / length * k * gap)
    kernel *= inside
    coarse = (np.arange(GRID)[:, None] * mode[None, :]) % GRID * (2.0 * math.pi / GRID)
    to_grid = np.concatenate([np.cos(coarse), np.sin(coarse)], axis=1).T
    part = np.where(mode == 0, 1.0 / GRID, 2.0 / GRID)
    from_grid = np.concatenate([np.cos(coarse) * part, np.sin(coarse) * part], axis=1)
    turn = (np.arange(devices)[:, None] * mode[None, :]) % devices * (2.0 * math.pi / devices)
    slope = np.tile(np.sin(2.0 * math.pi / length * mode)[None, :], (8, 1))
    total = rows * bands
    index = np.arange(rows + 2 * HALO)
    local = np.where(index < rows + HALO, index, index - (rows + 2 * HALO))
    terms = np.zeros((rows + 2 * HALO, 128))
    lines = np.zeros((bands, 256))
    for b in range(bands):
        g = b * rows + local
        phi = (2.0 * ((g + 0.5) / total) - 1.0) * LIMIT
        terms[:, b] = 1.0 / np.cos(phi)
        terms[:, 16 + b] = ROTATION * np.sin(phi)
        terms[:, 32 + b] = (g >= 0) & (g < total)
        lines[b, 0:rows] = terms[0:rows, b]
        lines[b, 128 : 128 + rows] = terms[0:rows, 16 + b]
    made = dict(
        analyse=analyse,
        evaluate=evaluate,
        kernel=kernel,
        to_grid=to_grid,
        from_grid=from_grid,
        cos=np.cos(turn),
        sin=np.sin(turn),
        slope=slope,
        terms=terms,
        lines=lines,
    )
    for name, value in made.items():
        made[name] = value.astype(np.float32)
        if name in ("analyse", "evaluate", "kernel", "to_grid", "from_grid"):
            high = value.astype(ml_dtypes.bfloat16)
            low = (value - high.astype(np.float64)).astype(ml_dtypes.bfloat16)
            made[name] = np.stack([high, low])
    return made


VMEM = pl.BlockSpec(memory_space=pltpu.VMEM)
HBM = pl.BlockSpec(memory_space=pltpu.HBM)


def call(kernel, name, outs, args, scratch=(), direct=(), cost=1.0, outside=False):
    shapes = [jax.ShapeDtypeStruct(shape, F32) for shape in outs]
    specs = [
        HBM if i in direct else VMEM for i in range(len(args))
    ]
    args = [
        pltpu.with_memory_space_constraint(arg, pltpu.HBM) if i in direct else arg
        for i, arg in enumerate(args)
    ]
    held = [pltpu.VMEM(args[i].shape, args[i].dtype) for i in direct]
    held += [pltpu.SemaphoreType.DMA((len(direct),))] if direct else []
    return pl.pallas_call(
        kernel,
        name=name,
        out_shape=shapes,
        in_specs=specs,
        out_specs=[HBM if outside else VMEM] * len(shapes),
        scratch_shapes=held + [
            pltpu.VMEM(shape, F32) if isinstance(shape, tuple) else shape for shape in scratch
        ],
        cost_estimate=pl.CostEstimate(
            flops=int(cost * 1e9), bytes_accessed=int(cost * 2e6), transcendentals=0
        ),
        compiler_params=pltpu.CompilerParams(
            vmem_limit_bytes=40 * 2**20
        ),
    )(*args)


LON = ("z", "core")


def on_device(
    back_height,
    back_east,
    back_north,
    obs_values,
    obs_owner,
    obs_row,
    obs_count,
    polar_mask,
    keep_share,
    depth_level,
):
    rows, cols = back_height.shape
    bands, devices = lax.axis_size("band"), lax.axis_size(LON)
    half = devices // 2
    number, width = obs_values.shape
    ext = rows + 2 * HALO
    made = tables(cols * devices, cols, devices, rows, bands)

    def send(value, axis, shift, closed):
        count = lax.axis_size(axis)
        pairs = [(i, (i + shift) % count) for i in range(count) if closed or 0 <= i + shift < count]
        return lax.ppermute(value, axis, pairs)

    even = [(i, i ^ 1) for i in range(bands)]
    odd = [(i, ((i + 1) ^ 1) - 1) for i in range(1, bands - 1)]
    fields, west, east, north, south, kept, marks = call(
        pack_tile,
        "pack_tile",
        [(4, rows, LANES), (rows, 128), (rows, 128)] + [(4 * HALO, LANES)] * 2 + [(8, rows), (8, number)],
        (
            back_height,
            back_east,
            back_north,
            depth_level,
            polar_mask.reshape(1, rows),
            keep_share.reshape(1, rows),
            obs_owner.reshape(1, number),
            obs_row.reshape(1, number),
            obs_count.reshape(1, number),
        ),
        direct=range(9),
    )
    above, below = lax.ppermute(north, "band", odd), lax.ppermute(south, "band", even)
    right, left = send(west, LON, -1, True), send(east, LON, 1, True)
    near, far, placed = call(
        pack_observations,
        "pack_observations",
        [(half, 32, 128), (half, 32, 128), (devices, 256)],
        (obs_values, marks, kept, made["cos"], made["sin"], made["analyse"]),
        cost=3.0,
    )
    wide, weight, corner_west, corner_east, mine, other = call(
        lambda *refs: partial_sums(cols, *refs),
        "partial_sums",
        [(4, ext, LANES), (ext, 128)] + [(8 * HALO, 128)] * 2 + [(half, 56, 128)] * 2,
        (
            fields,
            left,
            right,
            above,
            below,
            kept,
            made["terms"],
            made["cos"],
            made["sin"],
            made["analyse"],
            made["kernel"],
            placed,
            near,
            far,
        ),
        scratch=[pltpu.VMEM((n * devices, LANES), jnp.bfloat16) for n in (8, 8, 2)],
    )
    swapped = lax.all_gather(other, "core", axis=0, tiled=False)
    (joined,) = call(
        join, "join", [(half, 37, 2, 128)], (mine, swapped)
    )
    owned = lax.all_to_all(joined, "z", split_axis=0, concat_axis=0, tiled=True)
    (spread,) = call(
        own_row,
        "own_row",
        [(half, 3, 4, 128)],
        (
            owned,
            kept,
            made["lines"],
            made["slope"],
            made["to_grid"],
            made["from_grid"],
        ),
        scratch=[(8, 256), (8, GRID), (12, 128), (24, 128)],
    )
    shared = lax.all_to_all(spread, "z", split_axis=0, concat_axis=0, tiled=True)
    everyone = lax.all_gather(shared, "core", axis=0, tiled=False)
    dep, west = call(
        unpack_observations,
        "unpack_observations",
        [(rows, LANES), (rows + 8 * HALO, 128)],
        (owned, corner_west),
        scratch=[(half, 48, 128)],
    )
    corner_east = lax.optimization_barrier((corner_east, spread))[0]
    corner_right, corner_left = send(west, LON, -1, True), send(corner_east, LON, 1, True)
    dep, corner_left = lax.optimization_barrier((dep, corner_left))
    depx, north, south = call(
        lambda *refs: band_edges(cols, *refs),
        "band_edges",
        [(rows, LANES), (56, 128), (56, 128)],
        (everyone, dep, corner_right, kept),
    )
    above, below = lax.ppermute(north, "band", odd), lax.ppermute(south, "band", even)
    own, inner = call(
        lambda *refs: own_rows(cols, *refs),
        "own_rows",
        [(6 * rows, LANES), (3, rows - 2 * SURE, LANES)],
        (
            everyone,
            kept,
            made["cos"],
            made["sin"],
            made["evaluate"],
            wide,
            left,
            right,
            weight,
            depx,
            made["terms"],
        ),
        scratch=[(6 * rows, 256), (4, rows, LANES)],
    )
    edge = 2 * EDGE + 2 * HALO
    return tuple(
        call(
            last_stage,
            "last_stage",
            [(rows, cols)] * 3,
            (
                wide,
                left,
                right,
                corner_left,
                corner_right,
                weight,
                own,
                inner,
                depx,
                above,
                below,
                made["terms"],
                made["cos"],
                made["sin"],
                made["evaluate"],
            ),
            scratch=[(48, 256), (edge, LANES), (4, edge, LANES)]
            + [(rows, cols)] * 3
            + [(56, 128)] * 2
            + [pltpu.SemaphoreType.DMA((3, 3))],
            outside=True,
        )
    )


def solution(mesh):
    placed = (
        P("band", LON),
        P("band", LON),
        P("band", LON),
        P(("band", *LON), None),
        P(("band", *LON), None),
        P(("band", *LON)),
        P(("band", *LON)),
        P("band"),
        P("band"),
        P("band", LON),
    )
    fine = jax.sharding.Mesh(
        mesh.devices.reshape(mesh.devices.shape[0], -1, 2), ("band", *LON)
    )
    return jax.shard_map(
        on_device,
        mesh=fine,
        in_specs=placed,
        out_specs=(P("band", LON), P("band", LON), P("band", LON)),
        check_vma=False,
    )
```

```python
import math

import jax
import jax.numpy as jnp
import ml_dtypes
import numpy as np
from jax import lax
from jax.experimental import pallas as pl
from jax.experimental.pallas import tpu as pltpu
from jax.sharding import PartitionSpec as P

MODES = 128
LEVELS = 50
COURANT = 0.25
ROTATION = 0.4
LIMIT = 1.3089969389957472
CAP = 12
LANES = 384
GRID = 512
HALO = 4
F32 = jnp.float32


def hdot(left, right):
    return jnp.dot(left, right, precision=lax.Precision.HIGHEST, preferred_element_type=F32)


def halves_of(value):
    high = value.astype(jnp.bfloat16)
    return high, (value - high.astype(F32)).astype(jnp.bfloat16)


def bdot(left, right):
    return jnp.dot(left, right, preferred_element_type=F32)


def pick_dot(chosen, value):
    high, low = halves_of(value)
    rest = (value - high.astype(F32) - low.astype(F32)).astype(jnp.bfloat16)
    chosen = chosen.astype(jnp.bfloat16)
    return bdot(chosen, high) + bdot(chosen, low) + bdot(chosen, rest)


def tdot(left, table_ref):
    high, low = halves_of(left)
    return bdot(high, table_ref[0]) + bdot(low, table_ref[0]) + bdot(high, table_ref[1])


def tdot_few(left, table_ref):
    lines = left.shape[0]
    high = left.astype(jnp.bfloat16).astype(F32)
    both = jnp.concatenate([high, left - high], axis=0).astype(jnp.bfloat16)
    first = bdot(both, table_ref[0])
    return first[0:lines] + first[lines:] + bdot(left.astype(jnp.bfloat16), table_ref[1])


def mdot(left, right):
    return jnp.dot(left, right, precision=lax.Precision.HIGH, preferred_element_type=F32)


def iota(shape, dim):
    return lax.broadcasted_iota(jnp.int32, shape, dim)


def own_place():
    return lax.axis_index("band"), 2 * lax.axis_index("z") + lax.axis_index("core")


def swap_odd(first, second):
    even = lax.axis_index("band") % 2 == 0
    return jnp.where(even, first, second), jnp.where(even, second, first)


def swap_cores(first, second):
    zero = lax.axis_index("core") == 0
    return jnp.where(zero, first, second), jnp.where(zero, second, first)


def to_col(row):
    size = row.shape[1]
    same = iota((size, size), 0) == iota((size, size), 1)
    return jnp.sum(jnp.where(same, row, jnp.zeros_like(row)), axis=1, keepdims=True)


def to_row(col):
    size = col.shape[0]
    same = iota((size, size), 0) == iota((size, size), 1)
    return jnp.sum(jnp.where(same, col, jnp.zeros_like(col)), axis=0, keepdims=True)


def lon_diff(field):
    width = field.shape[1]
    return 0.5 * (pltpu.roll(field, width - 1, 1) - pltpu.roll(field, 1, 1))


def lat_diff(field):
    rows = field.shape[0]
    return 0.5 * (pltpu.roll(field, rows - 1, 0) - pltpu.roll(field, 1, 0))


def rank_in_row(mask_row):
    size = mask_row.shape[1]
    before = iota((size, size), 0) < iota((size, size), 1)
    return jnp.sum(jnp.where(before, to_col(mask_row), 0), axis=0, keepdims=True)


def slot_rows(mask_row, core, devices):
    rows = mask_row.shape[1]
    half = devices // 2
    line = iota((devices, rows), 0)
    slot = jnp.where(line < half, 2 * line + core, 2 * (line - half) + 1 - core)
    hit = (slot == rank_in_row(mask_row)) & (mask_row == 1)
    return hit.astype(F32)


WEIGHT_LANE = 300 - 256


def pack_tile(
    h_hbm,
    e_hbm,
    n_hbm,
    d_hbm,
    mask_hbm,
    keep_hbm,
    owner_hbm,
    row_hbm,
    count_hbm,
    fields_ref,
    west_ref,
    east_ref,
    north_ref,
    south_ref,
    filter_ref,
    marks_ref,
    h_ref,
    e_ref,
    n_ref,
    d_ref,
    mask_ref,
    keep_ref,
    owner_ref,
    row_ref,
    count_ref,
    sems,
):
    pairs = (
        (h_hbm, h_ref),
        (e_hbm, e_ref),
        (n_hbm, n_ref),
        (d_hbm, d_ref),
        (mask_hbm, mask_ref),
        (keep_hbm, keep_ref),
        (owner_hbm, owner_ref),
        (row_hbm, row_ref),
        (count_hbm, count_ref),
    )
    copies = [pltpu.make_async_copy(a, b, sems.at[i]) for i, (a, b) in enumerate(pairs)]
    for copy in copies:
        copy.start()
    fields_ref[...] = jnp.zeros(fields_ref.shape, F32)
    for copy in copies:
        copy.wait()
    rows, cols = h_ref.shape
    filter_ref[0:1, :] = mask_ref[...].astype(F32)
    filter_ref[1:2, :] = keep_ref[...]
    filter_ref[2:8, :] = jnp.zeros((6, rows), F32)
    for i, in_ref in enumerate((owner_ref, row_ref, count_ref)):
        marks_ref[i : i + 1, :] = in_ref[...].astype(F32)
    marks_ref[3:8, :] = jnp.zeros((5, marks_ref.shape[1]), F32)
    weight = to_col(mask_ref[...].astype(F32) * (1.0 - keep_ref[...]))
    level = d_ref[...].astype(F32)
    wet = (level > 0).astype(F32)
    values = (h_ref[...], wet * e_ref[...], wet * n_ref[...], level)
    lane = iota((rows, 128), 1)
    west = jnp.zeros(lane.shape, F32)
    east = jnp.zeros(lane.shape, F32)
    last = cols - HALO - 256
    for f, value in enumerate(values):
        fields_ref[f, :, 0:cols] = value
        inside = (lane >= HALO * f) & (lane < HALO * f + HALO)
        head = fields_ref[f, :, 0:128]
        tail = fields_ref[f, :, 256:384]
        if f:
            head = pltpu.roll(head, HALO * f, 1)
        west = jnp.where(inside, head, west)
        east = jnp.where(inside, pltpu.roll(tail, (HALO * f - last) % 128, 1), east)
        for out_ref, at in ((north_ref, 0), (south_ref, rows - HALO)):
            span = slice(at, at + HALO)
            lines = slice(HALO * f, HALO * f + HALO)
            edge = fields_ref[f, span, 256:384]
            if f == 3:
                edge = jnp.where(iota(edge.shape, 1) == WEIGHT_LANE, weight[span, :], edge)
            out_ref[lines, 0:256] = fields_ref[f, span, 0:256]
            out_ref[lines, 256:384] = edge
    west_ref[...], east_ref[...] = swap_cores(west, east)
    north, south = north_ref[...], south_ref[...]
    north_ref[...], south_ref[...] = swap_odd(south, north)


def third_tile(tail, left, right, f, cols):
    lane = iota(tail.shape, 1)
    first = cols - 256
    shifted = pltpu.roll(right, (first - HALO * f) % 128, 1)
    tail = jnp.where((lane >= first) & (lane < first + HALO), shifted, tail)
    shifted = pltpu.roll(left, (128 - HALO - HALO * f) % 128, 1)
    return jnp.where(lane >= 128 - HALO, shifted, tail)


def row_terms(terms, band):
    lane = iota(terms.shape, 1)
    return [
        jnp.sum(jnp.where(lane == band + 16 * i, terms, 0.0), axis=1, keepdims=True)
        for i in range(3)
    ]


def partial_sums(
    cols,
    fields_ref,
    outer_ref,
    inner_ref,
    above_ref,
    below_ref,
    filter_ref,
    terms_ref,
    cos_ref,
    sin_ref,
    table_ref,
    kernel_ref,
    placed_ref,
    near_ref,
    far_ref,
    left_ref,
    right_ref,
    ext_ref,
    weight_ref,
    west_ref,
    east_ref,
    mine_ref,
    other_ref,
    high_ref,
    low_ref,
    cells_ref,
):
    rows = fields_ref.shape[1]
    ext = rows + 2 * HALO
    devices = cos_ref.shape[0]
    half = devices // 2
    band, lon = own_place()
    left_ref[...], right_ref[...] = swap_cores(outer_ref[...], inner_ref[...])
    below, above = swap_odd(below_ref[...], above_ref[...])
    for f in range(4):
        ext_ref[f, 0:rows, :] = fields_ref[f]
        ext_ref[f, rows : rows + HALO, :] = below[HALO * f : HALO * f + HALO]
        ext_ref[f, rows + HALO : ext, :] = above[HALO * f : HALO * f + HALO]
    edge = ext_ref[3, rows:ext, 256:384]
    marked = iota(edge.shape, 1) == WEIGHT_LANE
    mask, keep = filter_ref[0:1, :], filter_ref[1:2, :]
    weight_ref[0:rows, :] = jnp.broadcast_to(to_col(mask * (1.0 - keep)), (rows, 128))
    weight_ref[rows:ext, :] = jnp.broadcast_to(
        jnp.sum(jnp.where(marked, edge, 0.0), axis=1, keepdims=True), (2 * HALO, 128)
    )
    ext_ref[3, rows:ext, 256:384] = jnp.where(marked, 0.0, edge)
    corner = iota((2 * HALO, 128), 1)
    last = cols - HALO - 256
    for f in range(4):
        lines = slice(2 * HALO * f, 2 * HALO * f + 2 * HALO)
        inside = (corner >= HALO * f) & (corner < HALO * f + HALO)
        head = ext_ref[f, rows:ext, 0:128]
        tail = ext_ref[f, rows:ext, 256:384]
        if f:
            head = pltpu.roll(head, HALO * f, 1)
        west_ref[lines, :] = jnp.where(inside, head, 0.0)
        east_ref[lines, :] = jnp.where(inside, pltpu.roll(tail, (HALO * f - last) % 128, 1), 0.0)
    weight = weight_ref[:, 0:1]
    rest = 1.0 - weight
    metric, rotation, valid = row_terms(terms_ref[...], band)
    metric = metric * valid
    height, east, north = ext_ref[0], ext_ref[1], ext_ref[2]
    ext_ref[3, 0:rows, 256:384] = third_tile(
        ext_ref[3, 0:rows, 256:384], left_ref[...], right_ref[...], 3, cols
    )
    share = ext_ref[3] / LEVELS
    low_height = weight * height + COURANT * (
        metric * lon_diff(weight * east) + lat_diff(weight * north)
    )
    low_height = valid * low_height
    east_rest, north_rest = rest * east, rest * north
    middle = valid * (
        rest * height + COURANT * (metric * lon_diff(east_rest) + lat_diff(north_rest))
    )
    new_east = east_rest - rotation * north_rest + COURANT * share * metric * lon_diff(middle)
    new_north = north_rest + rotation * east_rest + COURANT * share * lat_diff(middle)
    chosen = slot_rows(mask, own_place()[1] % 2, devices).astype(jnp.bfloat16)
    sources = (height, east, north, low_height, lat_diff(low_height), middle, new_east, new_north)
    for v, field in enumerate(sources):
        lines = slice(devices * v, devices * v + devices)
        high, low = halves_of(field[0:rows, :])
        high_ref[lines, :] = bdot(chosen, high).astype(jnp.bfloat16)
        low_ref[lines, :] = bdot(chosen, low).astype(jnp.bfloat16)
    mine_ref[:, 24:56, :] = near_ref[...]
    other_ref[:, 24:56, :] = far_ref[...]
    level = ext_ref[3, 0:rows, :]
    for c, cells in enumerate(((level > 0).astype(F32), level)):
        cells_ref[devices * c : devices * c + devices, :] = bdot(
            chosen, cells.astype(jnp.bfloat16)
        ).astype(jnp.bfloat16)
    sums = bdot(high_ref[...], table_ref[0]) + bdot(low_ref[...], table_ref[0])
    sums = sums + bdot(high_ref[...], table_ref[1])
    turn_cos, turn_sin = cos_ref[pl.ds(lon, 1), :], sin_ref[pl.ds(lon, 1), :]
    for v in range(len(sources)):
        lines = slice(devices * v, devices * v + devices)
        on_cos, on_sin = sums[lines, 0:128], sums[lines, 128:256]
        all_cos = on_cos * turn_cos - on_sin * turn_sin
        all_sin = on_sin * turn_cos + on_cos * turn_sin
        if v == 5:
            all_cos = all_cos + placed_ref[:, 0:128]
            all_sin = all_sin + placed_ref[:, 128:256]
        for i, value in enumerate((all_cos, all_sin)):
            mine_ref[:, 2 * v + i, :] = value[0:half]
            other_ref[:, 2 * v + i, :] = value[half:devices]
    spread = bdot(cells_ref[...], kernel_ref[0]) + bdot(cells_ref[...], kernel_ref[1])
    spread = pltpu.roll(spread, lon * (GRID // devices), 1)
    for c in range(2):
        for i in range(4):
            part = spread[devices * c : devices * c + devices, 128 * i : 128 * i + 128]
            at = 16 + 4 * c + i
            mine_ref[:, at, :] = part[0:half]
            other_ref[:, at, :] = part[half:devices]


def pack_observations(
    values_ref,
    marks_ref,
    filter_ref,
    cos_ref,
    sin_ref,
    table_ref,
    near_ref,
    far_ref,
    placed_ref,
):
    number, width = values_ref.shape
    half = near_ref.shape[0]
    devices = 2 * half
    core = own_place()[1] % 2
    lengths = to_col(marks_ref[2:3, :])
    values = jnp.where(iota((number, width), 1).astype(F32) < lengths, values_ref[...], 0.0)
    high, low = halves_of(values)
    rest = (values - high.astype(F32) - low.astype(F32)).astype(jnp.bfloat16)
    owner_row = marks_ref[0:1, :].astype(jnp.int32)
    owner_col = to_col(owner_row)
    same = owner_col == owner_row
    before = same & (iota((number, number), 0) < iota((number, number), 1))
    arrival_row = jnp.sum(before.astype(jnp.int32), axis=0, keepdims=True)
    after = same & (iota((number, number), 0) > iota((number, number), 1))
    arrival_col = jnp.sum(after.astype(jnp.int32), axis=1, keepdims=True)
    chip_row, core_row = owner_row // 2, owner_row % 2
    target = chip_row * 16 + arrival_row
    label = marks_ref[1:2, :]
    arrived = (iota((number, 128), 1) == arrival_col).astype(F32).astype(jnp.bfloat16)
    for out_ref, side in ((near_ref, core), (far_ref, 1 - core)):
        goes = core_row == side
        sent = ((iota((16 * half, number), 0) == target) & goes).astype(F32)
        sent = sent.astype(jnp.bfloat16)
        block = bdot(sent, high) + bdot(sent, low) + bdot(sent, rest)
        block = block.reshape(half, 16, width)
        out_ref[:, 0:CAP, :] = block[:, 0:CAP, 0:128]
        out_ref[:, CAP : 2 * CAP, :] = block[:, 0:CAP, 128:256]
        named = ((iota((half, number), 0) == chip_row) & goes).astype(F32) * label
        out_ref[:, 2 * CAP : 32, :] = jnp.zeros((half, 32 - 2 * CAP, 128), F32)
        out_ref[:, 2 * CAP, :] = bdot(named.astype(jnp.bfloat16), arrived)
    head = table_ref[0, 0:width, :]
    sums = bdot(high, head) + bdot(low, head) + bdot(high, table_ref[1, 0:width, :])
    whose = (iota((number, devices), 1) == owner_col).astype(F32)
    turn_cos, turn_sin = pick_dot(whose, cos_ref[...]), pick_dot(whose, sin_ref[...])
    on_cos, on_sin = sums[:, 0:128], sums[:, 128:256]
    all_cos = on_cos * turn_cos - on_sin * turn_sin
    all_sin = on_sin * turn_cos + on_cos * turn_sin
    mask = filter_ref[0:1, :]
    rows = mask.shape[1]
    in_row = (iota((rows, number), 0).astype(F32) == label).astype(F32)
    slots = slot_rows(mask, core, devices).astype(jnp.bfloat16)
    chosen = bdot(slots, in_row.astype(jnp.bfloat16))
    placed_ref[:, 0:128] = pick_dot(chosen, all_cos)
    placed_ref[:, 128:256] = pick_dot(chosen, all_sin)


def join(mine_ref, both_ref, out_ref):
    other = 1 - own_place()[1] % 2
    for i in range(12):
        pair = slice(2 * i, 2 * i + 2)
        out_ref[:, i, :, :] = mine_ref[:, pair, :] + both_ref[other, :, pair, :]
    for i in range(12, 24):
        out_ref[:, i, :, :] = mine_ref[:, 2 * i : 2 * i + 2, :]
        out_ref[:, i + 12, :, :] = both_ref[other, :, 2 * i : 2 * i + 2, :]
    out_ref[:, 36, 0, :] = mine_ref[:, 48, :]
    out_ref[:, 36, 1, :] = both_ref[other, :, 48, :]


def unpack_observations(in_ref, corner_ref, dep_ref, west_ref, data_ref):
    half = in_ref.shape[0]
    rows = dep_ref.shape[0]
    lines = 4 * CAP
    total = half * lines
    spot = iota((128, total), 1) % lines
    label_row = jnp.zeros((1, total), F32)
    own = iota((half, total), 1) // lines == iota((half, total), 0)
    for s in range(2):
        here = (spot // (2 * CAP) == s) & (spot % CAP == iota((128, total), 0))
        across = bdot(
            in_ref[:, 36, s, :].astype(jnp.bfloat16), here.astype(F32).astype(jnp.bfloat16)
        )
        label_row = label_row + jnp.sum(jnp.where(own, across, 0.0), axis=0, keepdims=True)
    line = iota((rows, total), 1) % lines
    hit = iota((rows, total), 0).astype(F32) == label_row
    for i in range(2 * CAP):
        data_ref[:, 2 * i : 2 * i + 2, :] = in_ref[:, 12 + i, :, :]
    data = data_ref[...].reshape(total, 128)
    for i in range(2):
        side = (hit & ((line // CAP) % 2 == i)).astype(F32)
        dep_ref[:, 128 * i : 128 * i + 128] = pick_dot(side, data)
    dep_ref[:, 256:384] = jnp.zeros((rows, 128), F32)
    west_ref[0:rows, :] = pltpu.roll(dep_ref[:, 0:128], 14, 1)
    west_ref[rows : rows + corner_ref.shape[0], :] = corner_ref[...]


def own_row(
    in_ref,
    filter_ref,
    lines_ref,
    slope_ref,
    to_grid_ref,
    from_grid_ref,
    out_ref,
    left_ref,
    grid_ref,
    res_ref,
    sum_ref,
):
    band, lon = own_place()
    pairs = in_ref[0, 0:12, :, :]
    for i in range(1, in_ref.shape[0]):
        pairs = pairs + in_ref[i, 0:12, :, :]
    for i in range(12):
        sum_ref[2 * i : 2 * i + 2, :] = pairs[i]
    sums = sum_ref[...]
    mask, keep = filter_ref[0:1, :], filter_ref[1:2, :]
    chosen = ((rank_in_row(mask) == lon) & (mask == 1)).astype(F32)

    def pick(row):
        return jnp.sum(chosen * row, axis=1, keepdims=True)

    rows = mask.shape[1]
    weight = pick(1.0 - keep)
    both = lines_ref[pl.ds(band, 1), :]
    metric = pick(both[:, 0:rows])
    rotation = pick(both[:, 128 : 128 + rows])

    def line(i):
        return sums[i : i + 1, :]

    slope = slope_ref[0:1, :]
    left_ref[...] = jnp.zeros(left_ref.shape, F32)
    pairs = (
        (weight * (line(2) - rotation * line(4)), weight * (line(3) - rotation * line(5))),
        (metric * slope * line(7), -metric * slope * line(6)),
        (weight * (line(4) + rotation * line(2)), weight * (line(5) + rotation * line(3))),
        (line(8), line(9)),
    )
    for i, (on_cos, on_sin) in enumerate(pairs):
        left_ref[i : i + 1, 0:128] = on_cos
        left_ref[i : i + 1, 128:256] = on_sin
    at = tdot_few(left_ref[...], to_grid_ref)
    wet = jnp.concatenate([line(16), line(17), line(18), line(19)], axis=1)
    share = (COURANT / LEVELS) * jnp.concatenate([line(20), line(21), line(22), line(23)], axis=1)
    grid_ref[...] = jnp.zeros(grid_ref.shape, F32)
    grid_ref[0:1, :] = wet * at[0:1] + share * at[1:2]
    grid_ref[1:2, :] = wet * at[2:3] + share * at[3:4]
    back = tdot_few(grid_ref[...], from_grid_ref)
    res_ref[0:6, :] = sums[0:6]
    res_ref[6:8, :] = sums[10:12] + sums[6:8]
    for i in range(2):
        res_ref[8 + 2 * i : 9 + 2 * i, :] = line(12 + 2 * i) + back[i : i + 1, 0:128]
        res_ref[9 + 2 * i : 10 + 2 * i, :] = line(13 + 2 * i) + back[i : i + 1, 128:256]
    for i in range(3):
        out_ref[:, i, :, :] = jnp.broadcast_to(
            res_ref[4 * i : 4 * i + 4, :][None], (out_ref.shape[0], 4, 128)
        )


def slots_to_rows(all_ref, mask, at):
    half = all_ref.shape[1]
    lines = at.shape[0]
    here = iota((lines, mask.shape[1]), 1) == at
    rank = jnp.sum(
        jnp.where(here & (mask == 1), rank_in_row(mask) + 1.0, 0.0), axis=1, keepdims=True
    )
    total = jnp.zeros((lines, 12 * 128), F32)
    for c in range(2):
        chosen = (2 * iota((lines, half), 1) + c + 1).astype(F32) == rank
        every = [all_ref[c, :, v // 4, v % 4, :] for v in range(12)]
        total = total + pick_dot(chosen.astype(F32), jnp.concatenate(every, axis=1))
    return total


def band_edges(cols, all_ref, dep_ref, edge_ref, filter_ref, depx_ref, north_ref, south_ref):
    rows = dep_ref.shape[0]
    mask = filter_ref[0:1, :]
    first = cols - 256
    lane = iota((rows, 128), 1)
    depx_ref[:, 0:256] = dep_ref[:, 0:256]
    depx_ref[:, 256:384] = jnp.where(
        (lane == first) | (lane == first + 1), edge_ref[0:rows, :], 0.0
    )
    line = iota((8, 1), 0)
    ends = slots_to_rows(all_ref, mask, jnp.where(line < 4, line, line + (rows - 8)))
    for v in range(12):
        own = ends[:, 128 * v : 128 * v + 128]
        north_ref[4 * v : 4 * v + 4, :] = own[0:4]
        south_ref[4 * v : 4 * v + 4, :] = own[4:8]
    for out_ref, at in ((north_ref, 0), (south_ref, rows - 2)):
        for r in range(2):
            for t in range(3):
                out_ref[48 + 3 * r + t : 49 + 3 * r + t, :] = depx_ref[
                    at + r : at + r + 1, 128 * t : 128 * t + 128
                ]
        out_ref[54:56, :] = jnp.zeros((2, 128), F32)
    north, south = north_ref[...], south_ref[...]
    north_ref[...], south_ref[...] = swap_odd(south, north)


EDGE = 16
SURE = 8


def two_steps(fields, low, weight, terms, dep):
    metric, rotation, valid = terms
    level = fields[3]
    wet = (level > 0).astype(F32)
    share = COURANT * (level / LEVELS)

    def half_step(height, east, north, f):
        height = height + weight * (low[f] - height)
        east = east + weight * (low[f + 1] - east)
        north = north + weight * (low[f + 2] - north)
        middle = valid * (height + COURANT * (metric * lon_diff(east) + lat_diff(north)))
        new_east = east - rotation * north + share * (metric * lon_diff(middle))
        new_north = north + rotation * east + share * lat_diff(middle)
        return middle, new_east, new_north

    middle, east, north = half_step(fields[0], fields[1], fields[2], 0)
    return half_step(middle + dep, wet * east, wet * north, 3)


def own_rows(
    cols,
    all_ref,
    filter_ref,
    cos_ref,
    sin_ref,
    table_ref,
    wide_ref,
    left_ref,
    right_ref,
    weight_ref,
    depx_ref,
    terms_ref,
    low_ref,
    inner_ref,
    stack_ref,
    ext_ref,
):
    mask = filter_ref[0:1, :]
    rows = mask.shape[1]
    band, lon = own_place()
    turn_cos, turn_sin = cos_ref[pl.ds(lon, 1), :], sin_ref[pl.ds(lon, 1), :]
    coef = slots_to_rows(all_ref, mask, iota((rows, 1), 0))
    for f in range(6):
        lines = slice(rows * f, rows * f + rows)
        on_cos = coef[:, 256 * f : 256 * f + 128]
        on_sin = coef[:, 256 * f + 128 : 256 * f + 256]
        stack_ref[lines, 0:128] = on_cos * turn_cos + on_sin * turn_sin
        stack_ref[lines, 128:256] = on_sin * turn_cos - on_cos * turn_sin
    low_ref[...] = tdot(stack_ref[...], table_ref)
    for f in range(4):
        ext_ref[f, :, 0:256] = wide_ref[f, 0:rows, 0:256]
        ext_ref[f, :, 256:384] = third_tile(
            wide_ref[f, 0:rows, 256:384], left_ref[...], right_ref[...], f, cols
        )
    state = two_steps(
        [ext_ref[f] for f in range(4)],
        [low_ref[rows * f : rows * f + rows, :] for f in range(6)],
        weight_ref[0:rows, 0:1],
        row_terms(terms_ref[0:rows, :], band),
        depx_ref[...],
    )
    for i in range(3):
        inner_ref[i] = state[i][SURE : rows - SURE]


def last_stage(
    wide_ref,
    left_ref,
    right_ref,
    corner_left_ref,
    corner_right_ref,
    weight_ref,
    own_ref,
    inner_ref,
    depx_ref,
    second_ref,
    first_ref,
    terms_ref,
    cos_ref,
    sin_ref,
    table_ref,
    h_hbm,
    e_hbm,
    n_hbm,
    stack_ref,
    dep_ref,
    ext_ref,
    h_ref,
    e_ref,
    n_ref,
    below_ref,
    above_ref,
    sems,
):
    rows, cols = h_ref.shape
    ext = rows + 2 * HALO
    band, lon = own_place()
    pairs = ((h_ref, h_hbm), (e_ref, e_hbm), (n_ref, n_hbm))
    spans = (pl.ds(SURE, rows - 2 * SURE), pl.ds(0, SURE), pl.ds(rows - SURE, SURE))
    copies = [
        [
            pltpu.make_async_copy(a.at[span, :], b.at[span, :], sems.at[i, j])
            for j, span in enumerate(spans)
        ]
        for i, (a, b) in enumerate(pairs)
    ]
    for i, (out_ref, _) in enumerate(pairs):
        out_ref[SURE : rows - SURE, :] = inner_ref[i, :, 0:cols]
        copies[i][0].start()
    for f in range(4):
        parts = (
            (slice(0, EDGE), slice(rows - EDGE, rows)),
            (slice(EDGE + 2 * HALO, 2 * EDGE + 2 * HALO), slice(0, EDGE)),
        )
        for to, at in parts:
            ext_ref[f, to, 0:256] = wide_ref[f, at, 0:256]
            ext_ref[f, to, 256:384] = third_tile(
                wide_ref[f, at, 256:384], left_ref[at, :], right_ref[at, :], f, cols
            )
        to = slice(EDGE, EDGE + 2 * HALO)
        lines = slice(2 * HALO * f, 2 * HALO * f + 2 * HALO)
        ext_ref[f, to, 0:256] = wide_ref[f, rows:ext, 0:256]
        ext_ref[f, to, 256:384] = third_tile(
            wide_ref[f, rows:ext, 256:384],
            corner_left_ref[lines, :],
            corner_right_ref[rows + 2 * HALO * f : rows + 2 * HALO * f + 2 * HALO, :],
            f,
            cols,
        )
    below_ref[...], above_ref[...] = swap_odd(first_ref[...], second_ref[...])
    turn_cos, turn_sin = cos_ref[pl.ds(lon, 1), :], sin_ref[pl.ds(lon, 1), :]
    for f in range(6):
        for at, in_ref in ((8 * f, below_ref), (8 * f + 4, above_ref)):
            on_cos = in_ref[8 * f : 8 * f + 4, :]
            on_sin = in_ref[8 * f + 4 : 8 * f + 8, :]
            stack_ref[at : at + 4, 0:128] = on_cos * turn_cos + on_sin * turn_sin
            stack_ref[at : at + 4, 128:256] = on_sin * turn_cos - on_cos * turn_sin
    edges = tdot(stack_ref[...], table_ref)
    low = [
        jnp.concatenate(
            [
                own_ref[rows * f + rows - EDGE : rows * f + rows, :],
                edges[8 * f : 8 * f + 8, :],
                own_ref[rows * f : rows * f + EDGE, :],
            ],
            axis=0,
        )
        for f in range(6)
    ]
    dep_ref[0:EDGE, :] = depx_ref[rows - EDGE : rows, :]
    dep_ref[EDGE : EDGE + 2 * HALO, :] = jnp.zeros((2 * HALO, LANES), F32)
    dep_ref[EDGE + 2 * HALO : 2 * EDGE + 2 * HALO, :] = depx_ref[0:EDGE, :]
    for in_ref, at in ((below_ref, EDGE), (above_ref, EDGE + 2 * HALO - 2)):
        for r in range(2):
            for t in range(3):
                dep_ref[at + r : at + r + 1, 128 * t : 128 * t + 128] = in_ref[
                    48 + 3 * r + t : 49 + 3 * r + t, :
                ]

    def around(ref):
        return jnp.concatenate([ref[rows - EDGE : ext, :], ref[0:EDGE, :]], axis=0)

    state = two_steps(
        [ext_ref[f] for f in range(4)],
        low,
        around(weight_ref)[:, 0:1],
        row_terms(around(terms_ref), band),
        dep_ref[...],
    )
    south, north = slice(EDGE - SURE, EDGE), slice(EDGE + 2 * HALO, EDGE + 2 * HALO + SURE)
    for i, (out_ref, _) in enumerate(pairs):
        out_ref[0:SURE, :] = state[i][north, 0:cols]
        out_ref[rows - SURE : rows, :] = state[i][south, 0:cols]
        copies[i][1].start()
        copies[i][2].start()
    for group in copies:
        for copy in group:
            copy.wait()


def tables(length, cols, devices, rows, bands):
    mode = np.arange(MODES)
    norm = np.where(mode == 0, 1.0 / length, 2.0 / length)
    lane = np.arange(LANES)

    def angle(at, number):
        phase = (at[:, None].astype(np.int64) * number[None, :]) % length
        return phase * (2.0 * math.pi / length)

    inside = (lane < cols)[:, None]
    place = np.where(lane < LANES - HALO, lane, lane - LANES)
    shown = ((lane < cols + HALO) | (lane >= LANES - HALO))[:, None]
    around = angle(place, mode)
    analyse = np.concatenate([np.cos(around) * norm, np.sin(around) * norm], axis=1) * shown
    evaluate = (np.concatenate([np.cos(around), np.sin(around)], axis=1) * shown).T
    wide = np.arange(1, 2 * MODES - 1)
    spot = np.arange(GRID) * (length / GRID)
    gap = spot[None, :] - lane[:, None]
    kernel = np.full((LANES, GRID), 1.0 / length)
    for k in wide:
        kernel += (2.0 / length) * np.cos(2.0 * math.pi / length * k * gap)
    kernel *= inside
    coarse = (np.arange(GRID)[:, None] * mode[None, :]) % GRID * (2.0 * math.pi / GRID)
    to_grid = np.concatenate([np.cos(coarse), np.sin(coarse)], axis=1).T
    part = np.where(mode == 0, 1.0 / GRID, 2.0 / GRID)
    from_grid = np.concatenate([np.cos(coarse) * part, np.sin(coarse) * part], axis=1)
    turn = (np.arange(devices)[:, None] * mode[None, :]) % devices * (2.0 * math.pi / devices)
    slope = np.tile(np.sin(2.0 * math.pi / length * mode)[None, :], (8, 1))
    total = rows * bands
    index = np.arange(rows + 2 * HALO)
    local = np.where(index < rows + HALO, index, index - (rows + 2 * HALO))
    terms = np.zeros((rows + 2 * HALO, 128))
    lines = np.zeros((bands, 256))
    for b in range(bands):
        g = b * rows + local
        phi = (2.0 * ((g + 0.5) / total) - 1.0) * LIMIT
        terms[:, b] = 1.0 / np.cos(phi)
        terms[:, 16 + b] = ROTATION * np.sin(phi)
        terms[:, 32 + b] = (g >= 0) & (g < total)
        lines[b, 0:rows] = terms[0:rows, b]
        lines[b, 128 : 128 + rows] = terms[0:rows, 16 + b]
    made = dict(
        analyse=analyse,
        evaluate=evaluate,
        kernel=kernel,
        to_grid=to_grid,
        from_grid=from_grid,
        cos=np.cos(turn),
        sin=np.sin(turn),
        slope=slope,
        terms=terms,
        lines=lines,
    )
    for name, value in made.items():
        made[name] = value.astype(np.float32)
        if name in ("analyse", "evaluate", "kernel", "to_grid", "from_grid"):
            high = value.astype(ml_dtypes.bfloat16)
            low = (value - high.astype(np.float64)).astype(ml_dtypes.bfloat16)
            made[name] = np.stack([high, low])
    return made


VMEM = pl.BlockSpec(memory_space=pltpu.VMEM)
HBM = pl.BlockSpec(memory_space=pltpu.HBM)


def call(kernel, name, outs, args, scratch=(), direct=(), cost=1.0, outside=False):
    shapes = [jax.ShapeDtypeStruct(shape, F32) for shape in outs]
    specs = [
        HBM if i in direct else VMEM for i in range(len(args))
    ]
    args = [
        pltpu.with_memory_space_constraint(arg, pltpu.HBM) if i in direct else arg
        for i, arg in enumerate(args)
    ]
    held = [pltpu.VMEM(args[i].shape, args[i].dtype) for i in direct]
    held += [pltpu.SemaphoreType.DMA((len(direct),))] if direct else []
    return pl.pallas_call(
        kernel,
        name=name,
        out_shape=shapes,
        in_specs=specs,
        out_specs=[HBM if outside else VMEM] * len(shapes),
        scratch_shapes=held + [
            pltpu.VMEM(shape, F32) if isinstance(shape, tuple) else shape for shape in scratch
        ],
        cost_estimate=pl.CostEstimate(
            flops=int(cost * 1e9), bytes_accessed=int(cost * 2e6), transcendentals=0
        ),
        compiler_params=pltpu.CompilerParams(
            vmem_limit_bytes=40 * 2**20
        ),
    )(*args)


LON = ("z", "core")


def on_device(
    back_height,
    back_east,
    back_north,
    obs_values,
    obs_owner,
    obs_row,
    obs_count,
    polar_mask,
    keep_share,
    depth_level,
):
    rows, cols = back_height.shape
    bands, devices = lax.axis_size("band"), lax.axis_size(LON)
    half = devices // 2
    number, width = obs_values.shape
    ext = rows + 2 * HALO
    made = tables(cols * devices, cols, devices, rows, bands)

    def send(value, axis, shift, closed):
        count = lax.axis_size(axis)
        pairs = [(i, (i + shift) % count) for i in range(count) if closed or 0 <= i + shift < count]
        return lax.ppermute(value, axis, pairs)

    even = [(i, i ^ 1) for i in range(bands)]
    odd = [(i, ((i + 1) ^ 1) - 1) for i in range(1, bands - 1)]
    fields, west, east, north, south, kept, marks = call(
        pack_tile,
        "pack_tile",
        [(4, rows, LANES), (rows, 128), (rows, 128)] + [(4 * HALO, LANES)] * 2 + [(8, rows), (8, number)],
        (
            back_height,
            back_east,
            back_north,
            depth_level,
            polar_mask.reshape(1, rows),
            keep_share.reshape(1, rows),
            obs_owner.reshape(1, number),
            obs_row.reshape(1, number),
            obs_count.reshape(1, number),
        ),
        direct=range(9),
    )
    below, above = lax.ppermute(north, "band", even), lax.ppermute(south, "band", odd)
    across = [(i, (i + 1 if i % 2 else i - 1) % devices) for i in range(devices)]
    within = [(i, i ^ 1) for i in range(devices)]
    outer, inner = lax.ppermute(west, LON, across), lax.ppermute(east, LON, within)
    near, far, placed = call(
        pack_observations,
        "pack_observations",
        [(half, 32, 128), (half, 32, 128), (devices, 256)],
        (obs_values, marks, kept, made["cos"], made["sin"], made["analyse"]),
        cost=3.0,
    )
    left, right, wide, weight, corner_west, corner_east, mine, other = call(
        lambda *refs: partial_sums(cols, *refs),
        "partial_sums",
        [(rows, 128)] * 2 + [(4, ext, LANES), (ext, 128)] + [(8 * HALO, 128)] * 2 + [(half, 56, 128)] * 2,
        (
            fields,
            outer,
            inner,
            above,
            below,
            kept,
            made["terms"],
            made["cos"],
            made["sin"],
            made["analyse"],
            made["kernel"],
            placed,
            near,
            far,
        ),
        scratch=[pltpu.VMEM((n * devices, LANES), jnp.bfloat16) for n in (8, 8, 2)],
    )
    swapped = lax.all_gather(other, "core", axis=0, tiled=False)
    (joined,) = call(
        join, "join", [(half, 37, 2, 128)], (mine, swapped)
    )
    owned = lax.all_to_all(joined, "z", split_axis=0, concat_axis=0, tiled=True)
    (spread,) = call(
        own_row,
        "own_row",
        [(half, 3, 4, 128)],
        (
            owned,
            kept,
            made["lines"],
            made["slope"],
            made["to_grid"],
            made["from_grid"],
        ),
        scratch=[(8, 256), (8, GRID), (12, 128), (24, 128)],
    )
    shared = lax.all_to_all(spread, "z", split_axis=0, concat_axis=0, tiled=True)
    everyone = lax.all_gather(shared, "core", axis=0, tiled=False)
    dep, west = call(
        unpack_observations,
        "unpack_observations",
        [(rows, LANES), (rows + 8 * HALO, 128)],
        (owned, corner_west),
        scratch=[(half, 48, 128)],
    )
    corner_east = lax.optimization_barrier((corner_east, spread))[0]
    corner_right, corner_left = send(west, LON, -1, True), send(corner_east, LON, 1, True)
    dep, corner_left = lax.optimization_barrier((dep, corner_left))
    depx, north, south = call(
        lambda *refs: band_edges(cols, *refs),
        "band_edges",
        [(rows, LANES), (56, 128), (56, 128)],
        (everyone, dep, corner_right, kept),
    )
    below, above = lax.ppermute(north, "band", even), lax.ppermute(south, "band", odd)
    own, inner = call(
        lambda *refs: own_rows(cols, *refs),
        "own_rows",
        [(6 * rows, LANES), (3, rows - 2 * SURE, LANES)],
        (
            everyone,
            kept,
            made["cos"],
            made["sin"],
            made["evaluate"],
            wide,
            left,
            right,
            weight,
            depx,
            made["terms"],
        ),
        scratch=[(6 * rows, 256), (4, rows, LANES)],
    )
    edge = 2 * EDGE + 2 * HALO
    return tuple(
        call(
            last_stage,
            "last_stage",
            [(rows, cols)] * 3,
            (
                wide,
                left,
                right,
                corner_left,
                corner_right,
                weight,
                own,
                inner,
                depx,
                above,
                below,
                made["terms"],
                made["cos"],
                made["sin"],
                made["evaluate"],
            ),
            scratch=[(48, 256), (edge, LANES), (4, edge, LANES)]
            + [(rows, cols)] * 3
            + [(56, 128)] * 2
            + [pltpu.SemaphoreType.DMA((3, 3))],
            outside=True,
        )
    )


def solution(mesh):
    placed = (
        P("band", LON),
        P("band", LON),
        P("band", LON),
        P(("band", *LON), None),
        P(("band", *LON), None),
        P(("band", *LON)),
        P(("band", *LON)),
        P("band"),
        P("band"),
        P("band", LON),
    )
    fine = jax.sharding.Mesh(
        mesh.devices.reshape(mesh.devices.shape[0], -1, 2), ("band", *LON)
    )
    return jax.shard_map(
        on_device,
        mesh=fine,
        in_specs=placed,
        out_specs=(P("band", LON), P("band", LON), P("band", LON)),
        check_vma=False,
    )
```
